32 devices in a mesh: year: 4 (over z), row: 2 (over x), col: 4 (over y, core).
Axes of the slice: x: 2, y: 2, z: 4, core: 2. Of those that a mesh axis runs over, the one named last changes fastest.
Arguments:
- observed: float32 [4, 46, 128, 512], P('year', None, 'row', 'col'), may hold values from 0 to 0.8
- quality: int32 [4, 46, 128, 512], P('year', None, 'row', 'col'), may hold values from 0 to 3, as said below
- land_mask: int32 [128, 512], P('row', 'col'), may hold values 0 or 1
- params: float32 [4, 7, 128, 512], P('year', None, 'row', 'col'), may hold values from -0.3 to 3.4
- spatial_weight: float32 [7], replicated, may hold values from 0.2 to 2
- temporal_weight: float32 [7], replicated, may hold values from 0.2 to 2
Outputs:
- new_params: float32 [4, 7, 128, 512], P('year', None, 'row', 'col')
- residual: float32 [4, 7, 128, 512], P('year', None, 'row', 'col')
The draws below stay inside these ranges and needn't reach their ends.
Inputs may be any that keep to these rules, and one draw needn't show every extreme that they name: `quality`: 0 good, 1 marginal, 2 snow, 3 cloud.
All inputs are finite; a program needn't handle non-finite values. No bound on the sum of `land_mask` on one device may be relied on, other than what follows from the above.
Results may differ from the reference program's by a relative error of at most 0.0003.
Values sent between devices are 32-bit elements; how exact they have to be, the bound alone decides.
A program may use at most 64 MiB of HBM per device.

```python
import math
import jax
import jax.numpy as jnp
from jax import lax

DATES = 46
PARAMS = 7
ITERS = 4
YEARS = 4
NR = 128
NC = 512


def draw_quality(key, part):
    base_key = jax.random.fold_in(key, 11)
    level_key, other_key = jax.random.split(base_key)
    shape_all = (YEARS, DATES, NR, NC)
    chance = jax.random.randint(level_key, shape_all, 0, 1000)
    row_pos = lax.broadcasted_iota(jnp.int32, shape_all, 2)
    year_pos = lax.broadcasted_iota(jnp.int32, shape_all, 0)
    threshold = 250 + 600 * row_pos // max(NR - 1, 1) + 50 * year_pos // max(YEARS - 1, 1)
    others = jax.random.randint(other_key, shape_all, 1, 4)
    return jnp.where(chance < threshold, 0, others).astype(jnp.int32)


def draw_params(key, part):
    base_key = jax.random.fold_in(key, 23)
    lower = jnp.array([0.0, 0.3, -0.3, 0.25, 2.3, 0.6, 2.3], jnp.float32)
    upper = jnp.array([0.2, 0.7, 0.3, 0.45, 3.4, 0.8, 3.4], jnp.float32)
    unit = jax.random.uniform(base_key, (YEARS, PARAMS, NR, NC), jnp.float32)
    return lower[None, :, None, None] + (upper - lower)[None, :, None, None] * unit


def touch_ends(result, own_key, smallest, largest):
    longest = result.shape.index(max(result.shape))
    spots = []
    for shift in (0, 1):
        where = [jax.random.randint(jax.random.fold_in(own_key, axis), (), 0, length) for axis, length in enumerate(result.shape)]
        where[longest] = (where[longest] + shift) % result.shape[longest]
        spots.append(tuple(where))
    return result.at[spots[0]].set(smallest).at[spots[1]].set(largest)


def shard_levels(stream_key, dims, shards, low, top_value):
    loudness = 1.0
    for dim, parts in shards:
        draws = jax.random.uniform(jax.random.fold_in(jax.random.fold_in(stream_key, 6), dim), (parts,), jnp.float32, low / len(shards), top_value / len(shards))
        loudness = loudness * jnp.repeat(jnp.exp(draws), dims[dim] // parts).reshape((-1,) + (1,) * (len(dims) - 1 - dim))
    return loudness


def setup_inputs(seed: int = 0) -> dict:
    key_list = jax.random.split(jax.random.key(seed), 7)
    observed = jnp.clip(0.8 * jax.random.uniform(key_list[0], (YEARS, DATES, NR, NC), jnp.float32) ** shard_levels(key_list[0], (YEARS, DATES, NR, NC), ((0, 4), (2, 2), (3, 4)), -0.2, 0.2), 0.0, 0.8)
    quality = draw_quality(jax.random.fold_in(key_list[6], 71), 0)
    land_mask = touch_ends((jax.random.randint(key_list[2], (NR, NC), 0, 4) < 3).astype(jnp.int32), jax.random.fold_in(key_list[2], 1), 0, 1)
    params = draw_params(jax.random.fold_in(key_list[6], 71), 0)
    spatial_weight = jnp.clip(jnp.exp(jax.random.uniform(key_list[4], (PARAMS,), jnp.float32, math.log(0.2), math.log(2.0))), 0.2, 2.0)
    temporal_weight = jnp.clip(jnp.exp(jax.random.uniform(key_list[5], (PARAMS,), jnp.float32, math.log(0.2), math.log(2.0))), 0.2, 2.0)
    return {"observed": observed, "quality": quality, "land_mask": land_mask, "params": params, "spatial_weight": spatial_weight, "temporal_weight": temporal_weight}


damping = 0.1


def upper_pairs(count):
    return [(left_index, right_index) for left_index in range(count) for right_index in range(left_index, count)]


def curve_terms(observed, quality, land_mask, params):
    num_dates = observed.shape[1]
    count = params.shape[1]
    weight = jnp.where(quality == 0, 1.0, 0.0) + jnp.where(quality == 1, 0.5, 0.0)
    weight = weight * land_mask.astype(jnp.float32)[None, None] / num_dates
    date_times = (jnp.arange(num_dates, dtype=jnp.float32) / num_dates).reshape(1, num_dates, 1, 1)
    level_base, peak_value, green_slope, rise_mid, rise_log, fall_mid, fall_log = [params[:, index][:, None] for index in range(count)]
    rise_rate = jnp.exp(rise_log)
    fall_rate = jnp.exp(fall_log)
    rise_curve = jax.nn.sigmoid(rise_rate * (date_times - rise_mid))
    fall_curve = jax.nn.sigmoid(fall_rate * (date_times - fall_mid))
    season = rise_curve - fall_curve
    amplitude = peak_value - green_slope * date_times
    misfit = level_base + amplitude * season - observed
    rise_slope = rise_curve * (1.0 - rise_curve)
    fall_slope = fall_curve * (1.0 - fall_curve)
    jacobian = [jnp.ones_like(misfit), season, -date_times * season,
                -amplitude * rise_rate * rise_slope,
                amplitude * rise_slope * (date_times - rise_mid) * rise_rate,
                amplitude * fall_rate * fall_slope,
                -amplitude * fall_slope * (date_times - fall_mid) * fall_rate]
    weighted = [weight * column for column in jacobian]
    hessian = jnp.stack([jnp.sum(weighted[left_index] * jacobian[right_index], axis=1) for left_index, right_index in upper_pairs(count)])
    gradient = jnp.stack([jnp.sum(weighted[index] * misfit, axis=1) for index in range(count)], axis=1)
    return hessian, gradient


def blocks_from(hessian, count):
    blocks = [[None] * count for index in range(count)]
    for position, (left_index, right_index) in enumerate(upper_pairs(count)):
        blocks[left_index][right_index] = hessian[position]
        blocks[right_index][left_index] = hessian[position]
    return blocks


def block_apply(blocks, field):
    count = len(blocks)
    outputs = []
    for left_index in range(count):
        total = blocks[left_index][0] * field[:, 0]
        for right_index in range(1, count):
            total = total + blocks[left_index][right_index] * field[:, right_index]
        outputs.append(total)
    return jnp.stack(outputs, axis=1)


def invert(blocks):
    count = len(blocks)
    left_rows = [list(row) for row in blocks]
    right_rows = [[jnp.full_like(blocks[0][0], 1.0 if left_index == right_index else 0.0) for right_index in range(count)] for left_index in range(count)]
    for pivot in range(count):
        scale = 1.0 / left_rows[pivot][pivot]
        left_rows[pivot] = [entry * scale for entry in left_rows[pivot]]
        right_rows[pivot] = [entry * scale for entry in right_rows[pivot]]
        for other in range(count):
            if other != pivot:
                factor = left_rows[other][pivot]
                left_rows[other] = [entry - factor * base_entry for entry, base_entry in zip(left_rows[other], left_rows[pivot])]
                right_rows[other] = [entry - factor * base_entry for entry, base_entry in zip(right_rows[other], right_rows[pivot])]
    return right_rows


def prior_apply(field, spatial_weight, temporal_weight):
    padded = jnp.pad(field, ((1, 1), (0, 0), (1, 1), (1, 1)), mode="edge")
    plane = 4.0 * field - (padded[1:-1, :, :-2, 1:-1] + padded[1:-1, :, 2:, 1:-1] + padded[1:-1, :, 1:-1, :-2] + padded[1:-1, :, 1:-1, 2:])
    yearly = 2.0 * field - (padded[:-2, :, 1:-1, 1:-1] + padded[2:, :, 1:-1, 1:-1])
    return spatial_weight[None, :, None, None] * plane + temporal_weight[None, :, None, None] * yearly


def reference(observed, quality, land_mask, params, spatial_weight, temporal_weight):
    count = params.shape[1]

    def per_year(inputs):
        return curve_terms(inputs[0][None], inputs[1][None], land_mask, inputs[2][None])

    hess_all, grad_all = lax.map(per_year, (observed, quality, params))
    hessian = jnp.moveaxis(hess_all[:, :, 0], 0, 1)
    data_grad = grad_all[:, 0]
    blocks = blocks_from(hessian, count)
    shifted = [list(row) for row in blocks]
    for index in range(count):
        shifted[index][index] = blocks[index][index] + (damping + 4.0 * spatial_weight[index] + 2.0 * temporal_weight[index])
    precond = invert(shifted)

    def operate(field):
        return block_apply(blocks, field) + damping * field + prior_apply(field, spatial_weight, temporal_weight)

    residual = -(data_grad + prior_apply(params, spatial_weight, temporal_weight))
    step_field = jnp.zeros_like(params)
    search = block_apply(precond, residual)
    direction = search
    inner_now = jnp.sum(residual * search)
    for sweep in range(ITERS):
        image = operate(direction)
        step_len = inner_now / jnp.sum(direction * image)
        step_field = step_field + step_len * direction
        residual = residual - step_len * image
        if sweep + 1 < ITERS:
            search = block_apply(precond, residual)
            inner_next = jnp.sum(residual * search)
            direction = search + (inner_next / inner_now) * direction
            inner_now = inner_next
    return params + step_field, residual
```

```python
import functools

import jax
import jax.numpy as jnp
from jax import lax
from jax.experimental import pallas as pl
from jax.experimental.pallas import tpu as pltpu
from jax.sharding import PartitionSpec as P

ITERS = 4
ROUNDS = ITERS + 1
SUB = 8
BLOCKS = 1
LEAD = 2
DAMPING = 0.1
MESH = pl.DeviceIdType.MESH


def pairs_of(count):
    return [(i, j) for i in range(count) for j in range(i, count)]


def kernel(
    sizes,
    observed,
    quality,
    land_mask,
    params,
    spatial_weight,
    temporal_weight,
    new_params,
    residual,
    obs,
    qual,
    land,
    spatial,
    temporal,
    field,
    inverse,
    resid,
    slope,
    moments,
    notes,
    slots,
    load_sem,
    send_sem,
    recv_sem,
    row_send,
    row_recv,
    sum_send,
    sum_recv,
):
    n_year, n_row, n_col = sizes
    dates, rows, cols = obs.shape
    count = resid.shape[1]
    step_rows = SUB * BLOCKS
    chunks = rows // step_rows
    pairs = pairs_of(count)
    place = {pair: at for at, pair in enumerate(pairs)}

    year, row, col = lax.axis_index("year"), lax.axis_index("row"), lax.axis_index("col")
    even = lax.rem(row, 2) == 1

    has_prev, has_next = year > 0, year < n_year - 1
    has_left, has_right = col > 0, col < n_col - 1
    has_up, has_down = row > 0, row < n_row - 1
    has_first = jnp.logical_or(jnp.logical_and(even, has_up), jnp.logical_and(~even, has_down))
    has_last = jnp.logical_or(jnp.logical_and(even, has_down), jnp.logical_and(~even, has_up))
    toward_first = row + jnp.where(even, -1, 1)
    toward_last = row + jnp.where(even, 1, -1)

    def chunk_rows(position):
        chunk = jnp.where(even, position, chunks - 1 - position)
        return pl.multiple_of(chunk * step_rows, step_rows)

    total_devices = n_year * n_row * n_col
    near = (n_year - 1) + (n_row - 1) <= ITERS

    def peer(other):
        spot = lax.rem((year * n_row + row) * n_col + col + other, total_devices)
        return (spot // (n_row * n_col), lax.rem(spot // n_col, n_row), lax.rem(spot, n_col))

    barrier = pltpu.get_barrier_semaphore()
    if near:
        for present, target in (
            (has_prev, (year - 1, row, col)),
            (has_next, (year + 1, row, col)),
            (has_up, (year, row - 1, col)),
            (has_down, (year, row + 1, col)),
        ):
            @pl.when(present)
            def _(target=target):
                pl.semaphore_signal(barrier, inc=1, device_id=target, device_id_type=MESH)

        for other in range(1, n_col):
            pl.semaphore_signal(
                barrier,
                inc=1,
                device_id=(year, row, lax.rem(col + other, n_col)),
                device_id_type=MESH,
            )
        expected = n_col - 1
        for present in (has_prev, has_next, has_up, has_down):
            expected = expected + present.astype(jnp.int32)
    else:
        for other in range(1, total_devices):
            pl.semaphore_signal(barrier, inc=1, device_id=peer(other), device_id_type=MESH)
        expected = total_devices - 1

    param_load = pltpu.make_async_copy(
        params.at[0], field.at[0, 0, :, pl.ds(SUB, rows), :], load_sem.at[0]
    )
    small_loads = (
        pltpu.make_async_copy(land_mask, land, load_sem.at[1]),
        pltpu.make_async_copy(spatial_weight, spatial, load_sem.at[2]),
        pltpu.make_async_copy(temporal_weight, temporal, load_sem.at[3]),
    )

    def input_loads(position):
        start = chunk_rows(position)
        where = (slice(None), pl.ds(start, step_rows), slice(None))
        return (
            pltpu.make_async_copy(observed.at[0].at[where], obs.at[where], load_sem.at[4 + 2 * position]),
            pltpu.make_async_copy(quality.at[0].at[where], qual.at[where], load_sem.at[5 + 2 * position]),
        )

    param_load.start()
    for copy in small_loads:
        copy.start()
    for position in range(chunks):
        for copy in input_loads(position):
            copy.start()

    pl.semaphore_wait(barrier, expected)

    sides = (
        (has_next, (year + 1, row, col), 1, has_prev),
        (has_prev, (year - 1, row, col), 2, has_next),
        (has_right, (year, row, col + 1), 3, has_left),
        (has_left, (year, row, col - 1), 4, has_right),
    )

    def side_copy(step, position, side):
        _, target, slot, _ = sides[side]
        where = pl.ds(chunk_rows(position) + SUB, step_rows)
        return pltpu.make_async_remote_copy(
            src_ref=field.at[step, 0, :, where, :],
            dst_ref=field.at[step, slot, :, where, :],
            send_sem=send_sem.at[step, side],
            recv_sem=recv_sem.at[step, side, position],
            device_id=target,
            device_id_type=MESH,
        )

    def whole_copy(step, side):
        return pltpu.make_async_remote_copy(
            src_ref=field.at[step, 0, :, pl.ds(SUB, rows), :],
            dst_ref=field.at[step, sides[side][2], :, pl.ds(SUB, rows), :],
            send_sem=send_sem.at[step, side],
            recv_sem=recv_sem.at[step, side, 0],
            device_id=sides[side][1],
            device_id_type=MESH,
        )

    def row_copy(step, last):
        top = jnp.logical_xor(even, last)
        source = pl.multiple_of(jnp.where(top, SUB, rows), SUB)
        target = pl.multiple_of(jnp.where(top, rows + SUB, 0), SUB)
        return pltpu.make_async_remote_copy(
            src_ref=field.at[step, 0, :, pl.ds(source, SUB), :],
            dst_ref=field.at[step, 0, :, pl.ds(target, SUB), :],
            send_sem=row_send.at[step, int(last)],
            recv_sem=row_recv.at[step, int(last)],
            device_id=(year, toward_last if last else toward_first, col),
            device_id_type=MESH,
        )

    def turn(position, side):
        return lax.rem(position, 2) == side

    def start_sends(step, position, chosen=range(4), keep=None):
        for side in chosen:
            present = sides[side][0]
            if keep is not None and side < 2:
                present = jnp.logical_and(present, keep(position, side))

            @pl.when(present)
            def _(side=side):
                side_copy(step, position, side).start()

    def wait_sides(step, position, chosen=range(4), keep=None):
        for side in chosen:
            present = sides[side][3]
            if keep is not None and side < 2:
                present = jnp.logical_and(present, keep(position, side))

            @pl.when(present)
            def _(side=side):
                side_copy(step, position, side).wait_recv()

    def close_edges(step, first, last):
        for flag, at_last, present in ((first, False, has_first), (last, True, has_last)):
            top = jnp.logical_xor(even, at_last)

            @pl.when(jnp.logical_and(flag, present))
            def _(at_last=at_last):
                row_copy(step, at_last).start()

            def repeat(source, edge, target):
                for p in range(count):
                    block = field[step, 0, p, source : source + SUB, :]
                    field[step, 0, p, target : target + SUB, :] = jnp.broadcast_to(
                        block[edge : edge + 1, :], (SUB, cols)
                    )

            @pl.when(jnp.logical_and(jnp.logical_and(flag, ~present), top))
            def _():
                repeat(SUB, 0, 0)

            @pl.when(jnp.logical_and(jnp.logical_and(flag, ~present), ~top))
            def _():
                repeat(rows, SUB - 1, rows + SUB)

    def wait_edges(step, first, last):
        for flag, at_last, present in ((first, False, has_first), (last, True, has_last)):
            @pl.when(jnp.logical_and(flag, present))
            def _(at_last=at_last):
                row_copy(step, at_last).wait_recv()

    param_load.wait()

    def send_params(position, carry):
        start_sends(0, position)
        return carry

    lax.fori_loop(0, chunks, send_params, 0)
    close_edges(0, True, True)

    prev_slot = jnp.where(has_prev, 1, 0)
    next_slot = jnp.where(has_next, 2, 0)
    left_slot = jnp.where(has_left, 3, 0)
    right_slot = jnp.where(has_right, 4, 0)
    lane = lax.broadcasted_iota(jnp.int32, (SUB, cols), 1)
    level = lax.broadcasted_iota(jnp.int32, (SUB, cols), 0)
    lane_first, lane_last = lane == 0, lane == cols - 1
    level_first, level_last = level == 0, level == SUB - 1
    grid_left = lane == jnp.where(has_left, -1, 0)
    grid_right = lane == jnp.where(has_right, -1, cols - 1)

    def plane_sum(step, p, start):
        own = pl.ds(start + SUB, SUB)
        here = field[step, 0, p, own, :]
        above = field[step, 0, p, pl.ds(start, SUB), :]
        below = field[step, 0, p, pl.ds(start + 2 * SUB, SUB), :]
        up = pltpu.roll(jnp.where(level_last, above, here), 1, 0)
        down = pltpu.roll(jnp.where(level_first, below, here), SUB - 1, 0)
        left = pltpu.roll(jnp.where(lane_last, field[step, left_slot, p, own, :], here), 1, 1)
        right = pltpu.roll(
            jnp.where(lane_first, field[step, right_slot, p, own, :], here), cols - 1, 1
        )
        left = jnp.where(grid_left, here, left)
        right = jnp.where(grid_right, here, right)
        return here, (up + down) + (left + right)

    def around(step, p, start):
        own = pl.ds(start + SUB, SUB)
        here, plane = plane_sum(step, p, start)
        yearly = field[step, prev_slot, p, own, :] + field[step, next_slot, p, own, :]
        return here, spatial[p] * plane + temporal[p] * yearly

    def precondition(start, values):
        rows_here = pl.ds(start, SUB)
        entry = [inverse[at, rows_here, :] for at in range(len(pairs))]
        outs = []
        for p in range(count):
            total = entry[place[(0, p)]] * values[0]
            for q in range(1, count):
                total = total + entry[place[(min(p, q), max(p, q))]] * values[q]
            outs.append(total)
        return outs

    def dot(left, right):
        terms = [a * b for a, b in zip(left, right)]
        while len(terms) > 1:
            terms = [sum(terms[i : i + 2][1:], terms[i]) for i in range(0, len(terms), 2)]
        return terms[0]

    def normal(start):
        here = pl.ds(start, SUB)
        base, peak, slope, rise_mid, rise_log, fall_mid, fall_log = [
            field[0, 0, p, pl.ds(start + SUB, SUB), :] for p in range(count)
        ]
        rise_rate, fall_rate = jnp.exp(rise_log), jnp.exp(fall_log)
        rise_half, fall_half = 0.5 * rise_rate, 0.5 * fall_rate

        def date_step(date, sums):
            time = date.astype(jnp.float32) * (1.0 / dates)
            flag = qual[date, here, :].astype(jnp.float32)
            weight = jnp.maximum(1.0 - 0.5 * flag, 0.0)
            rise_gap = time - rise_mid
            fall_gap = time - fall_mid
            rise = jnp.tanh(rise_half * rise_gap)
            fall = jnp.tanh(fall_half * fall_gap)
            season = rise - fall
            height = peak - slope * time
            rise_bell = height - height * (rise * rise)
            fall_bell = height - height * (fall * fall)
            basis = [
                None,
                season,
                time * season,
                rise_bell,
                rise_gap * rise_bell,
                fall_bell,
                fall_gap * fall_bell,
            ]
            weighted = [weight] + [weight * item for item in basis[1:]]
            out = []
            for i, j in pairs:
                term = weighted[j] if i == 0 else basis[i] * weighted[j]
                out.append(sums[place[(i, j)]] + term)
            seen = obs[date, here, :]
            for i in range(count):
                out.append(sums[len(pairs) + i] + seen * weighted[i])
            return tuple(out)

        zero = jnp.zeros((SUB, cols), jnp.float32)
        sums = lax.fori_loop(
            0, dates, date_step, (zero,) * (len(pairs) + count), unroll=dates
        )
        share = land[here, :].astype(jnp.float32) * (1.0 / dates)
        rise_scale, fall_scale = 0.25 * rise_rate, 0.25 * fall_rate
        scale = [None, 0.5, -0.5, -rise_scale, rise_scale, fall_scale, -fall_scale]
        shared = [share] + [share * item for item in scale[1:]]
        block = {}
        for i, j in pairs:
            factor = shared[j] if i == 0 else shared[j] * scale[i]
            block[(i, j)] = sums[place[(i, j)]] * factor
        for p in range(count):
            total = shared[p] * sums[len(pairs) + p]
            for q, value in ((0, base), (1, peak), (2, slope)):
                total = total - block[(min(p, q), max(p, q))] * value
            resid[0, p, here, :] = total
        for p in range(count):
            block[(p, p)] = block[(p, p)] + (DAMPING + 4.0 * spatial[p] + 2.0 * temporal[p])
        for k in range(count):
            turn = 1.0 / block[(k, k)]
            edge = {i: block[(min(i, k), max(i, k))] for i in range(count) if i != k}
            lean = {i: edge[i] * turn for i in edge}
            for i, j in pairs:
                if i != k and j != k:
                    block[(i, j)] = block[(i, j)] - edge[i] * lean[j]
            for i in edge:
                block[(min(i, k), max(i, k))] = lean[i]
            block[(k, k)] = -turn
        for pair in pairs:
            inverse[place[pair], here, :] = -block[pair]

    zero = jnp.zeros((SUB, cols), jnp.float32)

    def walk(step, position):
        return chunk_rows(position), position == 0, position == chunks - 1

    def make_stage(stage):
        def body(position, carry):
            odd_sum, even_sum = carry
            start, first, last = walk(stage, position)
            wait_sides(stage, position)
            wait_edges(stage, first, last)
            for b in range(BLOCKS):
                at = pl.multiple_of(start + b * SUB, SUB)
                rows_here = pl.ds(at, SUB)
                held, pushed = [], []
                for p in range(count):
                    here, push = around(stage, p, at)
                    if stage == 0:
                        push = (resid[0, p, rows_here, :] + push) - (
                            4.0 * spatial[p] + 2.0 * temporal[p]
                        ) * here
                    resid[stage, p, rows_here, :] = push
                    held.append(here)
                    pushed.append(push)
                if stage > 0:
                    odd_sum = odd_sum + dot(held, pushed)
                turned = precondition(at, pushed)
                for p in range(count):
                    field[stage + 1, 0, p, pl.ds(at + SUB, SUB), :] = turned[p]
                even_sum = even_sum + dot(turned, pushed)
            start_sends(stage + 1, position, keep=turn if stage + 1 == ITERS else None)
            close_edges(stage + 1, first, last)
            return odd_sum, even_sum

        return body

    for copy in small_loads:
        copy.wait()

    first_stage = make_stage(0)

    def opening(position, carry):
        @pl.when(position < chunks)
        def _():
            for copy in input_loads(position):
                copy.wait()
            for b in range(BLOCKS):
                normal(pl.multiple_of(chunk_rows(position) + b * SUB, SUB))

        return lax.cond(
            position >= LEAD, lambda c: first_stage(position - LEAD, c), lambda c: c, carry
        )

    sums = []
    for stage in range(ITERS):
        if stage == 0:
            odd_sum, even_sum = lax.fori_loop(0, chunks + LEAD, opening, (zero, zero))
        else:
            odd_sum, even_sum = lax.fori_loop(0, chunks, make_stage(stage), (zero, zero))
            sums.append(odd_sum)
        sums.append(even_sum)

    others = total_devices - 1

    def sum_copy(note, other):
        return pltpu.make_async_remote_copy(
            src_ref=notes.at[note, pl.ds(0, 1)],
            dst_ref=slots.at[note, pl.ds(other - 1, 1)],
            send_sem=sum_send.at[note, other - 1],
            recv_sem=sum_recv.at[note, other - 1],
            device_id=peer(other),
            device_id_type=MESH,
        )

    def gather(note):
        for other in range(1, total_devices):
            sum_copy(note, other).wait_recv()
        return jnp.sum(slots[note], axis=0, keepdims=True) + notes[note, 0:1, :]

    for at, value in enumerate(sums):
        moments[at : at + 1, :] = jnp.sum(value, axis=0, keepdims=True)
    moments[len(sums) : SUB, :] = jnp.zeros((SUB - len(sums), cols), jnp.float32)
    folded = jnp.broadcast_to(jnp.sum(moments[...], axis=1, keepdims=True), (SUB, cols))
    notes[0, 0:1, :] = jnp.sum(jnp.where(lane == level, folded, 0.0), axis=0, keepdims=True)
    for other in range(1, total_devices):
        sum_copy(0, other).start()

    def send_rest(position, carry):
        start_sends(ITERS, position, (0, 1), lambda at, side: ~turn(at, side))
        return carry

    lax.fori_loop(0, chunks, send_rest, 0)

    def closing(position, last_sum):
        start, first, last = walk(ITERS, position)
        later = turn(position, 0)
        slot = jnp.where(later, prev_slot, next_slot)
        twice = jnp.where(jnp.where(later, has_prev, has_next), 2.0, 1.0)
        alone = jnp.where(jnp.where(later, has_next, has_prev), 0.0, 1.0)
        wait_sides(ITERS, position, keep=turn)
        wait_edges(ITERS, first, last)
        for b in range(BLOCKS):
            at = pl.multiple_of(start + b * SUB, SUB)
            held, pushed = [], []
            for p in range(count):
                here, plane = plane_sum(ITERS, p, at)
                beside = field[ITERS, slot, p, pl.ds(at + SUB, SUB), :]
                plane = spatial[p] * plane
                resid[ITERS, p, pl.ds(at, SUB), :] = plane + temporal[p] * beside
                held.append(here)
                pushed.append(plane + temporal[p] * (twice * beside + alone * here))
            last_sum = last_sum + dot(held, pushed)
        return last_sum

    last_sum = lax.fori_loop(0, chunks, closing, zero)
    notes[1, 0:1, :] = jnp.sum(last_sum, axis=0, keepdims=True)
    for other in range(1, total_devices):
        sum_copy(1, other).start()

    known = jnp.where(lane == level, jnp.broadcast_to(gather(0), (SUB, cols)), 0.0)
    known = jnp.broadcast_to(jnp.sum(known, axis=1, keepdims=True), (SUB, cols))
    mu = [known[at : at + 1, :] for at in range(2 * ITERS - 1)]
    drop = [mu[at] - mu[at + 1] for at in range(2 * ITERS - 2)]

    def form(coefs, table):
        total = None
        for i, left in enumerate(coefs):
            for j in range(i, len(coefs)):
                term = left * coefs[j] * table[i + j]
                term = term if i == j else 2.0 * term
                total = term if total is None else total + term
        return total

    one = jnp.ones_like(mu[0])
    search, direction = [one], [one]
    lengths = [jnp.zeros_like(one)] * ITERS
    inner = mu[0]
    for sweep in range(ITERS - 1):
        alpha = inner / form(direction, drop)
        for j in range(sweep + 1):
            lengths[j] = lengths[j] + alpha * direction[j]
        grown = []
        for j in range(sweep + 2):
            change = None
            if j <= sweep:
                change = direction[j]
            if j > 0:
                change = -direction[j - 1] if change is None else change - direction[j - 1]
            base = search[j] if j <= sweep else None
            grown.append(-alpha * change if base is None else base - alpha * change)
        search = grown
        fresh = form(search, mu)
        ratio = fresh / inner
        inner = fresh
        direction = [
            search[j] + ratio * direction[j] if j <= sweep else search[j]
            for j in range(sweep + 2)
        ]
    curve = form(direction, drop + [mu[-1]])
    bend = direction[-1] * direction[-1]

    def wide(values):
        return [jnp.broadcast_to(value, (SUB, cols)) for value in values]

    def mixes(values, head):
        return wide(
            [head - values[0]]
            + [values[j - 1] - values[j] for j in range(1, ITERS)]
            + [values[-1]]
        )

    paces, steers = wide(lengths[:-1]), wide(direction)
    base_mix, slope_mix = mixes(lengths, 1.0)[:-1], mixes(direction, 0.0)

    def prepare(position, carry):
        start, _, _ = walk(ITERS, position)
        slot = jnp.where(turn(position, 0), next_slot, prev_slot)
        wait_sides(ITERS, position, (0, 1), lambda at, side: ~turn(at, side))
        for b in range(BLOCKS):
            at = pl.multiple_of(start + b * SUB, SUB)
            rows_here, padded = pl.ds(at, SUB), pl.ds(at + SUB, SUB)
            for p in range(count):
                vectors = [field[j + 1, 0, p, padded, :] for j in range(ITERS)]
                total = field[0, 0, p, padded, :]
                for pace, vector in zip(paces, vectors):
                    total = total + pace * vector
                new_params[0, p, rows_here, :] = total
                total = steers[0] * vectors[0]
                for steer, vector in zip(steers[1:], vectors[1:]):
                    total = total + steer * vector
                slope[0, p, rows_here, :] = total
                vectors = [resid[j, p, rows_here, :] for j in range(ITERS + 1)]
                vectors[-1] = vectors[-1] + temporal[p] * field[ITERS, slot, p, padded, :]
                total = base_mix[0] * vectors[0]
                for mix, vector in zip(base_mix[1:], vectors[1:]):
                    total = total + mix * vector
                residual[0, p, rows_here, :] = total
                total = slope_mix[0] * vectors[0]
                for mix, vector in zip(slope_mix[1:], vectors[1:]):
                    total = total + mix * vector
                slope[1, p, rows_here, :] = total
        return carry

    lax.fori_loop(0, chunks, prepare, 0)

    for step in range(ROUNDS):
        for side in range(4):
            @pl.when(sides[side][0])
            def _(side=side, step=step):
                whole_copy(step, side).wait_send()
        for at_last, present in ((False, has_first), (True, has_last)):
            @pl.when(present)
            def _(at_last=at_last, step=step):
                row_copy(step, at_last).wait_send()
    for other in range(1, total_devices):
        sum_copy(0, other).wait_send()

    final = jnp.broadcast_to(jnp.sum(gather(1), axis=1, keepdims=True), (1, cols))
    alpha = jnp.broadcast_to(inner / (curve - bend * final), (SUB, cols))

    def finish(b, carry):
        rows_here = pl.ds(pl.multiple_of(b * SUB, SUB), SUB)
        for p in range(count):
            new_params[0, p, rows_here, :] = (
                new_params[0, p, rows_here, :] + alpha * slope[0, p, rows_here, :]
            )
            residual[0, p, rows_here, :] = (
                residual[0, p, rows_here, :] + alpha * slope[1, p, rows_here, :]
            )
        return carry

    lax.fori_loop(0, rows // SUB, finish, 0)

    for other in range(1, total_devices):
        sum_copy(1, other).wait_send()


def store_kernel(new_params, residual, new_params_out, residual_out, sem):
    copies = (
        pltpu.make_async_copy(new_params, new_params_out, sem.at[0]),
        pltpu.make_async_copy(residual, residual_out, sem.at[1]),
    )
    for copy in copies:
        copy.start()
    for copy in copies:
        copy.wait()


def per_device(sizes, observed, quality, land_mask, params, spatial_weight, temporal_weight):
    n_year, n_row, n_col = sizes
    _, dates, rows, cols = observed.shape
    count = params.shape[1]
    chunks = rows // (SUB * BLOCKS)
    others = n_year * n_row * n_col - 1
    f32 = jnp.float32
    vmem = pl.BlockSpec(memory_space=pltpu.VMEM)
    hbm = pl.BlockSpec(memory_space=pltpu.HBM)
    dma = pltpu.SemaphoreType.DMA
    outs = (jax.ShapeDtypeStruct(params.shape, f32), jax.ShapeDtypeStruct(params.shape, f32))
    results = pl.pallas_call(
        functools.partial(kernel, sizes),
        out_shape=outs,
        in_specs=[hbm] * 6,
        out_specs=(vmem, vmem),
        scratch_shapes=[
            pltpu.VMEM((dates, rows, cols), f32),
            pltpu.VMEM((dates, rows, cols), jnp.int32),
            pltpu.VMEM((rows, cols), jnp.int32),
            pltpu.SMEM((count,), f32),
            pltpu.SMEM((count,), f32),
            pltpu.VMEM((ROUNDS, 5, count, rows + 2 * SUB, cols), f32),
            pltpu.VMEM((count * (count + 1) // 2, rows, cols), f32),
            pltpu.VMEM((ROUNDS, count, rows, cols), f32),
            pltpu.VMEM((2, count, rows, cols), f32),
            pltpu.VMEM((SUB, cols), f32),
            pltpu.VMEM((2, SUB, cols), f32),
            pltpu.VMEM((2, max(others, 1), cols), f32),
            dma((4 + 2 * chunks,)),
            dma((ROUNDS, 4)),
            dma((ROUNDS, 4, chunks)),
            dma((ROUNDS, 2)),
            dma((ROUNDS, 2)),
            dma((2, max(others, 1))),
            dma((2, max(others, 1))),
        ],
        compiler_params=pltpu.CompilerParams(
            collective_id=0, has_side_effects=True, vmem_limit_bytes=24 * 2**20
        ),
        name="gauss_newton",
    )(
        *[
            pltpu.with_memory_space_constraint(operand, pltpu.HBM)
            for operand in (
                observed, quality, land_mask, params, spatial_weight, temporal_weight
            )
        ]
    )
    return pl.pallas_call(
        store_kernel,
        out_shape=outs,
        in_specs=[vmem, vmem],
        out_specs=(hbm, hbm),
        scratch_shapes=[dma((2,))],
        compiler_params=pltpu.CompilerParams(vmem_limit_bytes=2**20),
        name="store",
    )(*results)


def solution(mesh):
    sizes = tuple(mesh.shape[axis] for axis in ("year", "row", "col"))
    grid = P("year", None, "row", "col")
    return jax.shard_map(
        functools.partial(per_device, sizes),
        mesh=mesh,
        in_specs=(grid, grid, P("row", "col"), grid, P(), P()),
        out_specs=(grid, grid),
        check_vma=False,
    )
```

```python
import functools

import jax
import jax.numpy as jnp
from jax import lax
from jax.experimental import pallas as pl
from jax.experimental.pallas import tpu as pltpu
from jax.sharding import PartitionSpec as P

ITERS = 4
ROUNDS = ITERS + 1
SUB = 8
LEAD = 2
PAIR = 2
DAMPING = 0.1
MESH = pl.DeviceIdType.MESH


def pairs_of(count):
    return [(i, j) for i in range(count) for j in range(i, count)]


def kernel(
    sizes,
    observed,
    quality,
    land_mask,
    params,
    spatial_weight,
    temporal_weight,
    new_params,
    residual,
    obs,
    qual,
    land,
    spatial,
    temporal,
    field,
    inverse,
    resid,
    slope,
    moments,
    notes,
    slots,
    load_sem,
    send_sem,
    year_recv,
    col_recv,
    row_send,
    row_recv,
    sum_send,
    sum_recv,
):
    n_year, n_row, n_col = sizes
    dates, rows, cols = obs.shape
    count = resid.shape[1]
    chunks = rows // SUB
    wide_rows = SUB * PAIR
    pairs = pairs_of(count)
    place = {pair: at for at, pair in enumerate(pairs)}

    year, row, col = lax.axis_index("year"), lax.axis_index("row"), lax.axis_index("col")
    even = lax.rem(row, 2) == 1

    has_prev, has_next = year > 0, year < n_year - 1
    has_left, has_right = col > 0, col < n_col - 1
    has_up, has_down = row > 0, row < n_row - 1
    has_first = jnp.logical_or(jnp.logical_and(even, has_up), jnp.logical_and(~even, has_down))
    has_last = jnp.logical_or(jnp.logical_and(even, has_down), jnp.logical_and(~even, has_up))
    toward_first = row + jnp.where(even, -1, 1)
    toward_last = row + jnp.where(even, 1, -1)

    def chunk_rows(position):
        chunk = jnp.where(even, position, chunks - 1 - position)
        return pl.multiple_of(chunk * SUB, SUB)

    def wide_start(group):
        group = jnp.where(even, group, chunks // PAIR - 1 - group)
        return pl.multiple_of(group * wide_rows, wide_rows)

    total_devices = n_year * n_row * n_col
    near = (n_year - 1) + (n_row - 1) <= ITERS

    def peer(other):
        spot = lax.rem((year * n_row + row) * n_col + col + other, total_devices)
        return (spot // (n_row * n_col), lax.rem(spot // n_col, n_row), lax.rem(spot, n_col))

    barrier = pltpu.get_barrier_semaphore()
    if near:
        for present, target in (
            (has_prev, (year - 1, row, col)),
            (has_next, (year + 1, row, col)),
            (has_up, (year, row - 1, col)),
            (has_down, (year, row + 1, col)),
        ):
            @pl.when(present)
            def _(target=target):
                pl.semaphore_signal(barrier, inc=1, device_id=target, device_id_type=MESH)

        for other in range(1, n_col):
            pl.semaphore_signal(
                barrier,
                inc=1,
                device_id=(year, row, lax.rem(col + other, n_col)),
                device_id_type=MESH,
            )
        expected = n_col - 1
        for present in (has_prev, has_next, has_up, has_down):
            expected = expected + present.astype(jnp.int32)
    else:
        for other in range(1, total_devices):
            pl.semaphore_signal(barrier, inc=1, device_id=peer(other), device_id_type=MESH)
        expected = total_devices - 1

    param_load = pltpu.make_async_copy(
        params.at[0], field.at[0, 0, :, pl.ds(SUB, rows), :], load_sem.at[0]
    )
    small_loads = (
        pltpu.make_async_copy(land_mask, land, load_sem.at[1]),
        pltpu.make_async_copy(spatial_weight, spatial, load_sem.at[2]),
        pltpu.make_async_copy(temporal_weight, temporal, load_sem.at[3]),
    )

    def input_loads(group):
        where = (slice(None), pl.ds(wide_start(group), wide_rows), slice(None))
        return (
            pltpu.make_async_copy(observed.at[0].at[where], obs.at[where], load_sem.at[4 + 2 * group]),
            pltpu.make_async_copy(quality.at[0].at[where], qual.at[where], load_sem.at[5 + 2 * group]),
        )

    param_load.start()
    for copy in small_loads:
        copy.start()
    for group in range(chunks // PAIR):
        for copy in input_loads(group):
            copy.start()

    pl.semaphore_wait(barrier, expected)

    sides = (
        (has_next, (year + 1, row, col), 1, has_prev),
        (has_prev, (year - 1, row, col), 2, has_next),
        (has_right, (year, row, col + 1), 3, has_left),
        (has_left, (year, row, col - 1), 4, has_right),
    )

    def side_copy(step, position, side):
        _, target, slot, _ = sides[side]
        if side < 2:
            where = pl.ds(chunk_rows(position) + SUB, SUB)
            landing = year_recv.at[step % 2, side, position]
        else:
            group = position // PAIR
            where = pl.ds(pl.multiple_of(wide_start(group) + SUB, SUB), wide_rows)
            landing = col_recv.at[step % 2, side - 2, group]
        return pltpu.make_async_remote_copy(
            src_ref=field.at[step, 0, :, where, :],
            dst_ref=field.at[step, slot, :, where, :],
            send_sem=send_sem.at[side],
            recv_sem=landing,
            device_id=target,
            device_id_type=MESH,
        )

    def row_spot(last):
        top = jnp.logical_xor(even, last)
        source = pl.multiple_of(jnp.where(top, SUB, rows), SUB)
        target = pl.multiple_of(jnp.where(top, rows + SUB, 0), SUB)
        return source, target, (year, toward_last if last else toward_first, col)

    def row_copy(step, last):
        source, target, device = row_spot(last)
        return pltpu.make_async_remote_copy(
            src_ref=field.at[step, 0, :, pl.ds(source, SUB), :],
            dst_ref=field.at[step, 0, :, pl.ds(target, SUB), :],
            send_sem=row_send.at[int(last)],
            recv_sem=row_recv.at[step % 2, int(last)],
            device_id=device,
            device_id_type=MESH,
        )

    def side_sends(side):
        where = (slice(None), 0, slice(None), pl.ds(SUB, rows), slice(None))
        return pltpu.make_async_remote_copy(
            src_ref=field.at[where],
            dst_ref=field.at[where],
            send_sem=send_sem.at[side],
            recv_sem=send_sem.at[side],
            device_id=sides[side][1],
            device_id_type=MESH,
        )

    def row_sends(last):
        source, _, device = row_spot(last)
        where = (slice(None), 0, slice(None), pl.ds(source, SUB), slice(None))
        return pltpu.make_async_remote_copy(
            src_ref=field.at[where],
            dst_ref=field.at[where],
            send_sem=row_send.at[int(last)],
            recv_sem=row_send.at[int(last)],
            device_id=device,
            device_id_type=MESH,
        )

    def turn(position, side):
        return lax.rem(position, 2) == side

    def start_sends(step, position, chosen=range(4), keep=None):
        for side in chosen:
            present = sides[side][0]
            if side >= 2:
                ready = lax.rem(position, PAIR) == PAIR - 1
                present = jnp.logical_and(present, ready)
            elif keep is not None:
                present = jnp.logical_and(present, keep(position, side))

            @pl.when(present)
            def _(side=side):
                side_copy(step, position, side).start()

    def wait_sides(step, position, chosen=range(4), keep=None):
        for side in chosen:
            present = sides[side][3]
            if side >= 2:
                present = jnp.logical_and(present, lax.rem(position, PAIR) == 0)
            elif keep is not None:
                present = jnp.logical_and(present, keep(position, side))

            @pl.when(present)
            def _(side=side):
                side_copy(step, position, side).wait_recv()

    def close_edges(step, first, last):
        for flag, at_last, present in ((first, False, has_first), (last, True, has_last)):
            top = jnp.logical_xor(even, at_last)

            @pl.when(jnp.logical_and(flag, present))
            def _(at_last=at_last):
                row_copy(step, at_last).start()

            def repeat(source, edge, target):
                for p in range(count):
                    block = field[step, 0, p, source : source + SUB, :]
                    field[step, 0, p, target : target + SUB, :] = jnp.broadcast_to(
                        block[edge : edge + 1, :], (SUB, cols)
                    )

            @pl.when(jnp.logical_and(jnp.logical_and(flag, ~present), top))
            def _():
                repeat(SUB, 0, 0)

            @pl.when(jnp.logical_and(jnp.logical_and(flag, ~present), ~top))
            def _():
                repeat(rows, SUB - 1, rows + SUB)

    def wait_edges(step, first, last):
        for flag, at_last, present in ((first, False, has_first), (last, True, has_last)):
            @pl.when(jnp.logical_and(flag, present))
            def _(at_last=at_last):
                row_copy(step, at_last).wait_recv()

    param_load.wait()

    def send_params(position, carry):
        start_sends(0, position)
        return carry

    lax.fori_loop(0, chunks, send_params, 0)
    close_edges(0, True, True)

    prev_slot = jnp.where(has_prev, 1, 0)
    next_slot = jnp.where(has_next, 2, 0)
    left_slot = jnp.where(has_left, 3, 0)
    right_slot = jnp.where(has_right, 4, 0)
    lane = lax.broadcasted_iota(jnp.int32, (SUB, cols), 1)
    level = lax.broadcasted_iota(jnp.int32, (SUB, cols), 0)
    lane_first, lane_last = lane == 0, lane == cols - 1
    level_first, level_last = level == 0, level == SUB - 1
    grid_left = lane == jnp.where(has_left, -1, 0)
    grid_right = lane == jnp.where(has_right, -1, cols - 1)

    def plane_sum(step, p, start):
        own = pl.ds(start + SUB, SUB)
        here = field[step, 0, p, own, :]
        above = field[step, 0, p, pl.ds(start, SUB), :]
        below = field[step, 0, p, pl.ds(start + 2 * SUB, SUB), :]
        up = pltpu.roll(jnp.where(level_last, above, here), 1, 0)
        down = pltpu.roll(jnp.where(level_first, below, here), SUB - 1, 0)
        left = pltpu.roll(jnp.where(lane_last, field[step, left_slot, p, own, :], here), 1, 1)
        right = pltpu.roll(
            jnp.where(lane_first, field[step, right_slot, p, own, :], here), cols - 1, 1
        )
        left = jnp.where(grid_left, here, left)
        right = jnp.where(grid_right, here, right)
        return here, (up + down) + (left + right)

    def around(step, p, start):
        own = pl.ds(start + SUB, SUB)
        here, plane = plane_sum(step, p, start)
        yearly = field[step, prev_slot, p, own, :] + field[step, next_slot, p, own, :]
        return here, spatial[p] * plane + temporal[p] * yearly

    def precondition(start, values):
        rows_here = pl.ds(start, SUB)
        entry = [inverse[at, rows_here, :] for at in range(len(pairs))]
        outs = []
        for p in range(count):
            total = entry[place[(0, p)]] * values[0]
            for q in range(1, count):
                total = total + entry[place[(min(p, q), max(p, q))]] * values[q]
            outs.append(total)
        return outs

    def dot(left, right):
        terms = [a * b for a, b in zip(left, right)]
        while len(terms) > 1:
            terms = [sum(terms[i : i + 2][1:], terms[i]) for i in range(0, len(terms), 2)]
        return terms[0]

    def normal(start):
        here = pl.ds(start, SUB)
        base, peak, slope, rise_mid, rise_log, fall_mid, fall_log = [
            field[0, 0, p, pl.ds(start + SUB, SUB), :] for p in range(count)
        ]
        rise_rate, fall_rate = jnp.exp(rise_log), jnp.exp(fall_log)
        rise_half, fall_half = 0.5 * rise_rate, 0.5 * fall_rate

        def date_step(date, sums):
            time = date.astype(jnp.float32) * (1.0 / dates)
            flag = qual[date, here, :].astype(jnp.float32)
            weight = jnp.maximum(1.0 - 0.5 * flag, 0.0)
            rise_gap = time - rise_mid
            fall_gap = time - fall_mid
            rise = jnp.tanh(rise_half * rise_gap)
            fall = jnp.tanh(fall_half * fall_gap)
            season = rise - fall
            height = peak - slope * time
            rise_bell = height - height * (rise * rise)
            fall_bell = height - height * (fall * fall)
            basis = [
                None,
                season,
                time * season,
                rise_bell,
                rise_gap * rise_bell,
                fall_bell,
                fall_gap * fall_bell,
            ]
            weighted = [weight] + [weight * item for item in basis[1:]]
            out = []
            for i, j in pairs:
                term = weighted[j] if i == 0 else basis[i] * weighted[j]
                out.append(sums[place[(i, j)]] + term)
            seen = obs[date, here, :]
            for i in range(count):
                out.append(sums[len(pairs) + i] + seen * weighted[i])
            return tuple(out)

        zero = jnp.zeros((SUB, cols), jnp.float32)
        sums = lax.fori_loop(
            0, dates, date_step, (zero,) * (len(pairs) + count), unroll=dates
        )
        share = land[here, :].astype(jnp.float32) * (1.0 / dates)
        rise_scale, fall_scale = 0.25 * rise_rate, 0.25 * fall_rate
        scale = [None, 0.5, -0.5, -rise_scale, rise_scale, fall_scale, -fall_scale]
        shared = [share] + [share * item for item in scale[1:]]
        block = {}
        for i, j in pairs:
            factor = shared[j] if i == 0 else shared[j] * scale[i]
            block[(i, j)] = sums[place[(i, j)]] * factor
        for p in range(count):
            total = shared[p] * sums[len(pairs) + p]
            for q, value in ((0, base), (1, peak), (2, slope)):
                total = total - block[(min(p, q), max(p, q))] * value
            resid[0, p, here, :] = total
        for p in range(count):
            block[(p, p)] = block[(p, p)] + (DAMPING + 4.0 * spatial[p] + 2.0 * temporal[p])
        for k in range(count):
            turn = 1.0 / block[(k, k)]
            edge = {i: block[(min(i, k), max(i, k))] for i in range(count) if i != k}
            lean = {i: edge[i] * turn for i in edge}
            for i, j in pairs:
                if i != k and j != k:
                    block[(i, j)] = block[(i, j)] - edge[i] * lean[j]
            for i in edge:
                block[(min(i, k), max(i, k))] = lean[i]
            block[(k, k)] = -turn
        for pair in pairs:
            inverse[place[pair], here, :] = -block[pair]

    zero = jnp.zeros((SUB, cols), jnp.float32)

    def walk(position):
        return chunk_rows(position), position == 0, position == chunks - 1

    def make_stage(stage):
        def body(position, carry):
            odd_sum, even_sum = carry
            start, first, last = walk(position)
            wait_sides(stage, position)
            wait_edges(stage, first, last)
            rows_here = pl.ds(start, SUB)
            held, pushed = [], []
            for p in range(count):
                here, push = around(stage, p, start)
                if stage == 0:
                    push = (resid[0, p, rows_here, :] + push) - (
                        4.0 * spatial[p] + 2.0 * temporal[p]
                    ) * here
                resid[stage, p, rows_here, :] = push
                held.append(here)
                pushed.append(push)
            if stage > 0:
                odd_sum = odd_sum + dot(held, pushed)
            turned = precondition(start, pushed)
            for p in range(count):
                field[stage + 1, 0, p, pl.ds(start + SUB, SUB), :] = turned[p]
            even_sum = even_sum + dot(turned, pushed)
            start_sends(stage + 1, position, keep=turn if stage + 1 == ITERS else None)
            close_edges(stage + 1, first, last)
            return odd_sum, even_sum

        return body

    for copy in small_loads:
        copy.wait()

    first_stage = make_stage(0)

    def opening(position, carry):
        @pl.when(position < chunks)
        def _():
            @pl.when(lax.rem(position, PAIR) == 0)
            def _():
                for copy in input_loads(position // PAIR):
                    copy.wait()

            normal(chunk_rows(position))

        return lax.cond(
            position >= LEAD, lambda c: first_stage(position - LEAD, c), lambda c: c, carry
        )

    sums = []
    for stage in range(ITERS):
        if stage == 0:
            odd_sum, even_sum = lax.fori_loop(0, chunks + LEAD, opening, (zero, zero))
        else:
            odd_sum, even_sum = lax.fori_loop(0, chunks, make_stage(stage), (zero, zero))
            sums.append(odd_sum)
        sums.append(even_sum)

    others = total_devices - 1

    def sum_copy(note, other):
        return pltpu.make_async_remote_copy(
            src_ref=notes.at[note, pl.ds(0, 1)],
            dst_ref=slots.at[note, pl.ds(other - 1, 1)],
            send_sem=sum_send.at[note],
            recv_sem=sum_recv.at[note],
            device_id=peer(other),
            device_id_type=MESH,
        )

    def sum_copies(note):
        return pltpu.make_async_remote_copy(
            src_ref=slots.at[note],
            dst_ref=slots.at[note],
            send_sem=sum_send.at[note],
            recv_sem=sum_recv.at[note],
            device_id=peer(1),
            device_id_type=MESH,
        )

    def gather(note):
        sum_copies(note).wait_recv()
        return jnp.sum(slots[note], axis=0, keepdims=True) + notes[note, 0:1, :]

    for at, value in enumerate(sums):
        moments[at : at + 1, :] = jnp.sum(value, axis=0, keepdims=True)
    moments[len(sums) : SUB, :] = jnp.zeros((SUB - len(sums), cols), jnp.float32)
    folded = jnp.broadcast_to(jnp.sum(moments[...], axis=1, keepdims=True), (SUB, cols))
    notes[0, 0:1, :] = jnp.sum(jnp.where(lane == level, folded, 0.0), axis=0, keepdims=True)
    for other in range(1, total_devices):
        sum_copy(0, other).start()

    def send_rest(position, carry):
        start_sends(ITERS, position, (0, 1), lambda at, side: ~turn(at, side))
        return carry

    lax.fori_loop(0, chunks, send_rest, 0)

    def closing(position, last_sum):
        start, first, last = walk(position)
        later = turn(position, 0)
        slot = jnp.where(later, prev_slot, next_slot)
        twice = jnp.where(jnp.where(later, has_prev, has_next), 2.0, 1.0)
        alone = jnp.where(jnp.where(later, has_next, has_prev), 0.0, 1.0)
        wait_sides(ITERS, position, keep=turn)
        wait_edges(ITERS, first, last)
        held, pushed = [], []
        for p in range(count):
            here, plane = plane_sum(ITERS, p, start)
            beside = field[ITERS, slot, p, pl.ds(start + SUB, SUB), :]
            plane = spatial[p] * plane
            resid[ITERS, p, pl.ds(start, SUB), :] = plane + temporal[p] * beside
            held.append(here)
            pushed.append(plane + temporal[p] * (twice * beside + alone * here))
        last_sum = last_sum + dot(held, pushed)
        return last_sum

    last_sum = lax.fori_loop(0, chunks, closing, zero)
    notes[1, 0:1, :] = jnp.sum(last_sum, axis=0, keepdims=True)
    for other in range(1, total_devices):
        sum_copy(1, other).start()

    known = jnp.where(lane == level, jnp.broadcast_to(gather(0), (SUB, cols)), 0.0)
    known = jnp.broadcast_to(jnp.sum(known, axis=1, keepdims=True), (SUB, cols))
    mu = [known[at : at + 1, :] for at in range(2 * ITERS - 1)]
    drop = [mu[at] - mu[at + 1] for at in range(2 * ITERS - 2)]

    def form(coefs, table):
        total = None
        for i, left in enumerate(coefs):
            for j in range(i, len(coefs)):
                term = left * coefs[j] * table[i + j]
                term = term if i == j else 2.0 * term
                total = term if total is None else total + term
        return total

    one = jnp.ones_like(mu[0])
    search, direction = [one], [one]
    lengths = [jnp.zeros_like(one)] * ITERS
    inner = mu[0]
    for sweep in range(ITERS - 1):
        alpha = inner / form(direction, drop)
        for j in range(sweep + 1):
            lengths[j] = lengths[j] + alpha * direction[j]
        grown = []
        for j in range(sweep + 2):
            change = None
            if j <= sweep:
                change = direction[j]
            if j > 0:
                change = -direction[j - 1] if change is None else change - direction[j - 1]
            base = search[j] if j <= sweep else None
            grown.append(-alpha * change if base is None else base - alpha * change)
        search = grown
        fresh = form(search, mu)
        ratio = fresh / inner
        inner = fresh
        direction = [
            search[j] + ratio * direction[j] if j <= sweep else search[j]
            for j in range(sweep + 2)
        ]
    curve = form(direction, drop + [mu[-1]])
    bend = direction[-1] * direction[-1]

    def wide(values):
        return [jnp.broadcast_to(value, (SUB, cols)) for value in values]

    def mixes(values, head):
        return wide(
            [head - values[0]]
            + [values[j - 1] - values[j] for j in range(1, ITERS)]
            + [values[-1]]
        )

    paces, steers = wide(lengths[:-1]), wide(direction)
    base_mix, slope_mix = mixes(lengths, 1.0)[:-1], mixes(direction, 0.0)

    def prepare(position, carry):
        start, _, _ = walk(position)
        slot = jnp.where(turn(position, 0), next_slot, prev_slot)
        wait_sides(ITERS, position, (0, 1), lambda at, side: ~turn(at, side))
        rows_here, padded = pl.ds(start, SUB), pl.ds(start + SUB, SUB)
        for p in range(count):
            vectors = [field[j + 1, 0, p, padded, :] for j in range(ITERS)]
            total = field[0, 0, p, padded, :]
            for pace, vector in zip(paces, vectors):
                total = total + pace * vector
            new_params[0, p, rows_here, :] = total
            total = steers[0] * vectors[0]
            for steer, vector in zip(steers[1:], vectors[1:]):
                total = total + steer * vector
            slope[0, p, rows_here, :] = total
            vectors = [resid[j, p, rows_here, :] for j in range(ITERS + 1)]
            vectors[-1] = vectors[-1] + temporal[p] * field[ITERS, slot, p, padded, :]
            total = base_mix[0] * vectors[0]
            for mix, vector in zip(base_mix[1:], vectors[1:]):
                total = total + mix * vector
            residual[0, p, rows_here, :] = total
            total = slope_mix[0] * vectors[0]
            for mix, vector in zip(slope_mix[1:], vectors[1:]):
                total = total + mix * vector
            slope[1, p, rows_here, :] = total
        return carry

    lax.fori_loop(0, chunks, prepare, 0)

    for side in range(4):
        @pl.when(sides[side][0])
        def _(side=side):
            side_sends(side).wait_send()

    for at_last, present in ((False, has_first), (True, has_last)):
        @pl.when(present)
        def _(at_last=at_last):
            row_sends(at_last).wait_send()

    sum_copies(0).wait_send()

    final = jnp.broadcast_to(jnp.sum(gather(1), axis=1, keepdims=True), (1, cols))
    alpha = jnp.broadcast_to(inner / (curve - bend * final), (SUB, cols))

    def finish(b, carry):
        rows_here = pl.ds(pl.multiple_of(b * SUB, SUB), SUB)
        for p in range(count):
            new_params[0, p, rows_here, :] = (
                new_params[0, p, rows_here, :] + alpha * slope[0, p, rows_here, :]
            )
            residual[0, p, rows_here, :] = (
                residual[0, p, rows_here, :] + alpha * slope[1, p, rows_here, :]
            )
        return carry

    lax.fori_loop(0, rows // SUB, finish, 0)

    sum_copies(1).wait_send()


def store_kernel(new_params, residual, new_params_out, residual_out, sem):
    copies = (
        pltpu.make_async_copy(new_params, new_params_out, sem.at[0]),
        pltpu.make_async_copy(residual, residual_out, sem.at[1]),
    )
    for copy in copies:
        copy.start()
    for copy in copies:
        copy.wait()


def per_device(sizes, observed, quality, land_mask, params, spatial_weight, temporal_weight):
    n_year, n_row, n_col = sizes
    _, dates, rows, cols = observed.shape
    count = params.shape[1]
    chunks = rows // SUB
    groups = chunks // PAIR
    others = n_year * n_row * n_col - 1
    f32 = jnp.float32
    vmem = pl.BlockSpec(memory_space=pltpu.VMEM)
    hbm = pl.BlockSpec(memory_space=pltpu.HBM)
    dma = pltpu.SemaphoreType.DMA
    outs = (jax.ShapeDtypeStruct(params.shape, f32), jax.ShapeDtypeStruct(params.shape, f32))
    results = pl.pallas_call(
        functools.partial(kernel, sizes),
        out_shape=outs,
        in_specs=[hbm] * 6,
        out_specs=(vmem, vmem),
        scratch_shapes=[
            pltpu.VMEM((dates, rows, cols), f32),
            pltpu.VMEM((dates, rows, cols), jnp.int32),
            pltpu.VMEM((rows, cols), jnp.int32),
            pltpu.SMEM((count,), f32),
            pltpu.SMEM((count,), f32),
            pltpu.VMEM((ROUNDS, 5, count, rows + 2 * SUB, cols), f32),
            pltpu.VMEM((count * (count + 1) // 2, rows, cols), f32),
            pltpu.VMEM((ROUNDS, count, rows, cols), f32),
            pltpu.VMEM((2, count, rows, cols), f32),
            pltpu.VMEM((SUB, cols), f32),
            pltpu.VMEM((2, SUB, cols), f32),
            pltpu.VMEM((2, max(others, 1), cols), f32),
            dma((4 + 2 * groups,)),
            dma((4,)),
            dma((2, 2, chunks)),
            dma((2, 2, groups)),
            dma((2,)),
            dma((2, 2)),
            dma((2,)),
            dma((2,)),
        ],
        compiler_params=pltpu.CompilerParams(
            collective_id=0, has_side_effects=True, vmem_limit_bytes=24 * 2**20
        ),
        name="gauss_newton",
    )(
        *[
            pltpu.with_memory_space_constraint(operand, pltpu.HBM)
            for operand in (
                observed, quality, land_mask, params, spatial_weight, temporal_weight
            )
        ]
    )
    return pl.pallas_call(
        store_kernel,
        out_shape=outs,
        in_specs=[vmem, vmem],
        out_specs=(hbm, hbm),
        scratch_shapes=[dma((2,))],
        compiler_params=pltpu.CompilerParams(vmem_limit_bytes=2**20),
        name="store",
    )(*results)


def solution(mesh):
    sizes = tuple(mesh.shape[axis] for axis in ("year", "row", "col"))
    grid = P("year", None, "row", "col")
    return jax.shard_map(
        functools.partial(per_device, sizes),
        mesh=mesh,
        in_specs=(grid, grid, P("row", "col"), grid, P(), P()),
        out_specs=(grid, grid),
        check_vma=False,
    )
```

```python
import functools

import jax
import jax.numpy as jnp
from jax import lax
from jax.experimental import pallas as pl
from jax.experimental.pallas import tpu as pltpu
from jax.sharding import PartitionSpec as P

ITERS = 4
ROUNDS = ITERS + 1
SUB = 8
LEAD = 2
PAIR = 2
LEVEL = (1, 2, 3)
DAMPING = 0.1
MESH = pl.DeviceIdType.MESH


def pairs_of(count):
    return [(i, j) for i in range(count) for j in range(i, count)]


def kernel(
    sizes,
    observed,
    quality,
    land_mask,
    params,
    spatial_weight,
    temporal_weight,
    anchor,
    slope,
    pace,
    obs,
    qual,
    land,
    spatial,
    temporal,
    field,
    inverse,
    resid,
    moments,
    notes,
    slots,
    load_sem,
    send_sem,
    year_recv,
    col_recv,
    rest_recv,
    row_send,
    row_recv,
    sum_send,
    sum_recv,
    level_sem,
):
    n_year, n_row, n_col = sizes
    dates, rows, cols = obs.shape
    count = resid.shape[1]
    chunks = rows // SUB
    wide_rows = SUB * PAIR
    pairs = pairs_of(count)
    place = {pair: at for at, pair in enumerate(pairs)}

    year, row, col = lax.axis_index("year"), lax.axis_index("row"), lax.axis_index("col")
    even = lax.rem(row, 2) == 1

    has_prev, has_next = year > 0, year < n_year - 1
    has_left, has_right = col > 0, col < n_col - 1
    has_up, has_down = row > 0, row < n_row - 1
    has_first = jnp.logical_or(jnp.logical_and(even, has_up), jnp.logical_and(~even, has_down))
    has_last = jnp.logical_or(jnp.logical_and(even, has_down), jnp.logical_and(~even, has_up))
    toward_first = row + jnp.where(even, -1, 1)
    toward_last = row + jnp.where(even, 1, -1)

    def chunk_rows(position):
        chunk = jnp.where(even, position, chunks - 1 - position)
        return pl.multiple_of(chunk * SUB, SUB)

    def wide_start(group):
        group = jnp.where(even, group, chunks // PAIR - 1 - group)
        return pl.multiple_of(group * wide_rows, wide_rows)

    total_devices = n_year * n_row * n_col
    near = (n_year - 1) + (n_row - 1) <= ITERS

    def peer(other):
        spot = lax.rem((year * n_row + row) * n_col + col + other, total_devices)
        return (spot // (n_row * n_col), lax.rem(spot // n_col, n_row), lax.rem(spot, n_col))

    barrier = pltpu.get_barrier_semaphore()
    if near:
        for present, target in (
            (has_prev, (year - 1, row, col)),
            (has_next, (year + 1, row, col)),
            (has_up, (year, row - 1, col)),
            (has_down, (year, row + 1, col)),
        ):
            @pl.when(present)
            def _(target=target):
                pl.semaphore_signal(barrier, inc=1, device_id=target, device_id_type=MESH)

        for other in range(1, n_col):
            pl.semaphore_signal(
                barrier,
                inc=1,
                device_id=(year, row, lax.rem(col + other, n_col)),
                device_id_type=MESH,
            )
        expected = n_col - 1
        for present in (has_prev, has_next, has_up, has_down):
            expected = expected + present.astype(jnp.int32)
    else:
        for other in range(1, total_devices):
            pl.semaphore_signal(barrier, inc=1, device_id=peer(other), device_id_type=MESH)
        expected = total_devices - 1

    param_load = pltpu.make_async_copy(
        params.at[0], field.at[0, 0, :, pl.ds(SUB, rows), :], load_sem.at[0]
    )
    small_loads = (
        pltpu.make_async_copy(land_mask, land, load_sem.at[1]),
        pltpu.make_async_copy(spatial_weight, spatial, load_sem.at[2]),
        pltpu.make_async_copy(temporal_weight, temporal, load_sem.at[3]),
    )

    def input_loads(group):
        where = (slice(None), pl.ds(wide_start(group), wide_rows), slice(None))
        return (
            pltpu.make_async_copy(observed.at[0].at[where], obs.at[where], load_sem.at[4 + 2 * group]),
            pltpu.make_async_copy(quality.at[0].at[where], qual.at[where], load_sem.at[5 + 2 * group]),
        )

    param_load.start()
    for copy in small_loads:
        copy.start()
    for group in range(chunks // PAIR):
        for copy in input_loads(group):
            copy.start()

    pl.semaphore_wait(barrier, expected)

    sides = (
        (has_next, (year + 1, row, col), 1, has_prev),
        (has_prev, (year - 1, row, col), 2, has_next),
        (has_right, (year, row, col + 1), 3, has_left),
        (has_left, (year, row, col - 1), 4, has_right),
    )

    split = (count + 1) // 2
    early = (pl.ds(0, split), pl.ds(split, count - split))

    def side_copy(step, position, side):
        _, target, slot, _ = sides[side]
        which = early[side] if side < 2 and step == ITERS else slice(None)
        if side < 2:
            where = pl.ds(chunk_rows(position) + SUB, SUB)
            landing = year_recv.at[step % 2, position]
        else:
            group = position // PAIR
            where = pl.ds(pl.multiple_of(wide_start(group) + SUB, SUB), wide_rows)
            landing = col_recv.at[step % 2, group]
        return pltpu.make_async_remote_copy(
            src_ref=field.at[step, 0, which, where, :],
            dst_ref=field.at[step, slot, which, where, :],
            send_sem=send_sem.at[side],
            recv_sem=landing,
            device_id=target,
            device_id_type=MESH,
        )

    def rest_copy(side):
        _, target, slot, _ = sides[side]
        which, where = early[1 - side], pl.ds(SUB, rows)
        return pltpu.make_async_remote_copy(
            src_ref=field.at[ITERS, 0, which, where, :],
            dst_ref=field.at[ITERS, slot, which, where, :],
            send_sem=send_sem.at[side],
            recv_sem=rest_recv,
            device_id=target,
            device_id_type=MESH,
        )

    def row_spot(last):
        top = jnp.logical_xor(even, last)
        source = pl.multiple_of(jnp.where(top, SUB, rows), SUB)
        target = pl.multiple_of(jnp.where(top, rows + SUB, 0), SUB)
        return source, target, (year, toward_last if last else toward_first, col)

    def row_copy(step, last):
        source, target, device = row_spot(last)
        return pltpu.make_async_remote_copy(
            src_ref=field.at[step, 0, :, pl.ds(source, SUB), :],
            dst_ref=field.at[step, 0, :, pl.ds(target, SUB), :],
            send_sem=row_send.at[int(last)],
            recv_sem=row_recv.at[step % 2, int(last)],
            device_id=device,
            device_id_type=MESH,
        )

    def side_sends(side):
        where = (slice(None), 0, slice(None), pl.ds(SUB, rows), slice(None))
        return pltpu.make_async_remote_copy(
            src_ref=field.at[where],
            dst_ref=field.at[where],
            send_sem=send_sem.at[side],
            recv_sem=send_sem.at[side],
            device_id=sides[side][1],
            device_id_type=MESH,
        )

    def row_sends(last):
        source, _, device = row_spot(last)
        where = (slice(None), 0, slice(None), pl.ds(source, SUB), slice(None))
        return pltpu.make_async_remote_copy(
            src_ref=field.at[where],
            dst_ref=field.at[where],
            send_sem=row_send.at[int(last)],
            recv_sem=row_send.at[int(last)],
            device_id=device,
            device_id_type=MESH,
        )

    def start_sends(step, position):
        for side in range(4):
            present = sides[side][0]
            if side >= 2:
                ready = lax.rem(position, PAIR) == PAIR - 1
                present = jnp.logical_and(present, ready)

            @pl.when(present)
            def _(side=side):
                side_copy(step, position, side).start()

    def wait_pair(first, second, left, right, both):
        @pl.when(jnp.logical_and(first, second))
        def _():
            both.wait_recv()

        @pl.when(jnp.logical_and(first, ~second))
        def _():
            left.wait_recv()

        @pl.when(jnp.logical_and(second, ~first))
        def _():
            right.wait_recv()

    def landing_of(place, semaphore):
        return pltpu.make_async_remote_copy(
            src_ref=place,
            dst_ref=place,
            send_sem=send_sem.at[0],
            recv_sem=semaphore,
            device_id=sides[0][1],
            device_id_type=MESH,
        )

    def wait_years(step, position):
        where = pl.ds(chunk_rows(position) + SUB, SUB)
        slots_here = pl.ds(1, 1 if step == ITERS else 2)
        both = landing_of(
            field.at[step, slots_here, :, where, :], year_recv.at[step % 2, position]
        )
        ends = [side_copy(step, position, side) for side in (0, 1)]
        wait_pair(has_prev, has_next, *ends, both)

    def wait_cols(step, position):
        group = position // PAIR
        where = pl.ds(pl.multiple_of(wide_start(group) + SUB, SUB), wide_rows)
        both = landing_of(
            field.at[step, pl.ds(3, 2), :, where, :], col_recv.at[step % 2, group]
        )
        ends = [side_copy(step, position, side) for side in (2, 3)]

        @pl.when(lax.rem(position, PAIR) == 0)
        def _():
            wait_pair(has_left, has_right, *ends, both)

    def wait_rest():
        both = landing_of(field.at[ITERS, 1, :, pl.ds(SUB, rows), :], rest_recv)
        wait_pair(has_prev, has_next, rest_copy(0), rest_copy(1), both)

    def close_edges(step, first, last):
        for flag, at_last, present in ((first, False, has_first), (last, True, has_last)):
            top = jnp.logical_xor(even, at_last)

            @pl.when(jnp.logical_and(flag, present))
            def _(at_last=at_last):
                row_copy(step, at_last).start()

            def repeat(source, edge, target):
                for p in range(count):
                    block = field[step, 0, p, source : source + SUB, :]
                    field[step, 0, p, target : target + SUB, :] = jnp.broadcast_to(
                        block[edge : edge + 1, :], (SUB, cols)
                    )

            @pl.when(jnp.logical_and(jnp.logical_and(flag, ~present), top))
            def _():
                repeat(SUB, 0, 0)

            @pl.when(jnp.logical_and(jnp.logical_and(flag, ~present), ~top))
            def _():
                repeat(rows, SUB - 1, rows + SUB)

    def wait_edges(step, first, last):
        for flag, at_last, present in ((first, False, has_first), (last, True, has_last)):
            @pl.when(jnp.logical_and(flag, present))
            def _(at_last=at_last):
                row_copy(step, at_last).wait_recv()

    param_load.wait()

    def send_params(position, carry):
        start_sends(0, position)
        return carry

    lax.fori_loop(0, chunks, send_params, 0)
    close_edges(0, True, True)

    prev_slot = jnp.where(has_prev, 1, 0)
    next_slot = jnp.where(has_next, 2, 0)
    left_slot = jnp.where(has_left, 3, 0)
    right_slot = jnp.where(has_right, 4, 0)
    lane = lax.broadcasted_iota(jnp.int32, (SUB, cols), 1)
    level = lax.broadcasted_iota(jnp.int32, (SUB, cols), 0)
    lane_first, lane_last = lane == 0, lane == cols - 1
    level_first, level_last = level == 0, level == SUB - 1
    grid_left = lane == jnp.where(has_left, -1, 0)
    grid_right = lane == jnp.where(has_right, -1, cols - 1)

    def plane_sum(step, p, start):
        own = pl.ds(start + SUB, SUB)
        here = field[step, 0, p, own, :]
        above = field[step, 0, p, pl.ds(start, SUB), :]
        below = field[step, 0, p, pl.ds(start + 2 * SUB, SUB), :]
        up = pltpu.roll(jnp.where(level_last, above, here), 1, 0)
        down = pltpu.roll(jnp.where(level_first, below, here), SUB - 1, 0)
        left = pltpu.roll(jnp.where(lane_last, field[step, left_slot, p, own, :], here), 1, 1)
        right = pltpu.roll(
            jnp.where(lane_first, field[step, right_slot, p, own, :], here), cols - 1, 1
        )
        left = jnp.where(grid_left, here, left)
        right = jnp.where(grid_right, here, right)
        return here, (up + down) + (left + right)

    def around(step, p, start):
        own = pl.ds(start + SUB, SUB)
        here, plane = plane_sum(step, p, start)
        yearly = field[step, prev_slot, p, own, :] + field[step, next_slot, p, own, :]
        return here, spatial[p] * plane + temporal[p] * yearly

    def precondition(start, values):
        rows_here = pl.ds(start, SUB)
        entry = [inverse[at, rows_here, :] for at in range(len(pairs))]
        outs = []
        for p in range(count):
            total = entry[place[(0, p)]] * values[0]
            for q in range(1, count):
                total = total + entry[place[(min(p, q), max(p, q))]] * values[q]
            outs.append(total)
        return outs

    def dot(left, right):
        terms = [a * b for a, b in zip(left, right)]
        while len(terms) > 1:
            terms = [sum(terms[i : i + 2][1:], terms[i]) for i in range(0, len(terms), 2)]
        return terms[0]

    def normal(start):
        here = pl.ds(start, SUB)
        base, peak, slope, rise_mid, rise_log, fall_mid, fall_log = [
            field[0, 0, p, pl.ds(start + SUB, SUB), :] for p in range(count)
        ]
        rise_rate, fall_rate = jnp.exp(rise_log), jnp.exp(fall_log)
        rise_half, fall_half = 0.5 * rise_rate, 0.5 * fall_rate

        def date_step(date, sums):
            time = date.astype(jnp.float32) * (1.0 / dates)
            flag = qual[date, here, :].astype(jnp.float32)
            weight = jnp.maximum(1.0 - 0.5 * flag, 0.0)
            rise_gap = time - rise_mid
            fall_gap = time - fall_mid
            rise = jnp.tanh(rise_half * rise_gap)
            fall = jnp.tanh(fall_half * fall_gap)
            season = rise - fall
            height = peak - slope * time
            rise_bell = height - height * (rise * rise)
            fall_bell = height - height * (fall * fall)
            basis = [
                None,
                season,
                time * season,
                rise_bell,
                rise_gap * rise_bell,
                fall_bell,
                fall_gap * fall_bell,
            ]
            weighted = [weight] + [weight * item for item in basis[1:]]
            out = []
            for i, j in pairs:
                term = weighted[j] if i == 0 else basis[i] * weighted[j]
                out.append(sums[place[(i, j)]] + term)
            seen = obs[date, here, :]
            for i in range(count):
                out.append(sums[len(pairs) + i] + seen * weighted[i])
            return tuple(out)

        zero = jnp.zeros((SUB, cols), jnp.float32)
        sums = lax.fori_loop(
            0, dates, date_step, (zero,) * (len(pairs) + count), unroll=dates
        )
        share = land[here, :].astype(jnp.float32) * (1.0 / dates)
        rise_scale, fall_scale = 0.25 * rise_rate, 0.25 * fall_rate
        scale = [None, 0.5, -0.5, -rise_scale, rise_scale, fall_scale, -fall_scale]
        shared = [share] + [share * item for item in scale[1:]]
        block = {}
        for i, j in pairs:
            factor = shared[j] if i == 0 else shared[j] * scale[i]
            block[(i, j)] = sums[place[(i, j)]] * factor
        for p in range(count):
            total = shared[p] * sums[len(pairs) + p]
            for q, value in ((0, base), (1, peak), (2, slope)):
                total = total - block[(min(p, q), max(p, q))] * value
            resid[0, p, here, :] = total
        for p in range(count):
            block[(p, p)] = block[(p, p)] + (DAMPING + 4.0 * spatial[p] + 2.0 * temporal[p])
        for k in range(count):
            turn = 1.0 / block[(k, k)]
            edge = {i: block[(min(i, k), max(i, k))] for i in range(count) if i != k}
            lean = {i: edge[i] * turn for i in edge}
            for i, j in pairs:
                if i != k and j != k:
                    block[(i, j)] = block[(i, j)] - edge[i] * lean[j]
            for i in edge:
                block[(min(i, k), max(i, k))] = lean[i]
            block[(k, k)] = -turn
        for pair in pairs:
            inverse[place[pair], here, :] = -block[pair]

    zero = jnp.zeros((SUB, cols), jnp.float32)

    def walk(position):
        return chunk_rows(position), position == 0, position == chunks - 1

    def make_stage(stage):
        def body(position, carry):
            odd_sum, even_sum = carry
            start, first, last = walk(position)
            wait_cols(stage, position)
            wait_years(stage, position)
            wait_edges(stage, first, last)
            rows_here = pl.ds(start, SUB)
            held, pushed = [], []
            for p in range(count):
                here, push = around(stage, p, start)
                if stage == 0:
                    push = (resid[0, p, rows_here, :] + push) - (
                        4.0 * spatial[p] + 2.0 * temporal[p]
                    ) * here
                resid[stage, p, rows_here, :] = push
                held.append(here)
                pushed.append(push)
            if stage > 0:
                odd_sum = odd_sum + dot(held, pushed)
            turned = precondition(start, pushed)
            for p in range(count):
                field[stage + 1, 0, p, pl.ds(start + SUB, SUB), :] = turned[p]
            even_sum = even_sum + dot(turned, pushed)
            start_sends(stage + 1, position)
            close_edges(stage + 1, first, last)
            return odd_sum, even_sum

        return body

    def keep_level():
        if n_col % 2 == 0:
            partner = col + 1 - 2 * lax.rem(col, 2)
            pl.semaphore_signal(
                level_sem, inc=1, device_id=(year, row, partner), device_id_type=MESH
            )
            pl.semaphore_wait(level_sem, 1)

    for copy in small_loads:
        copy.wait()

    first_stage = make_stage(0)

    def opening(position, carry):
        @pl.when(position < chunks)
        def _():
            @pl.when(lax.rem(position, PAIR) == 0)
            def _():
                for copy in input_loads(position // PAIR):
                    copy.wait()

            normal(chunk_rows(position))

        return lax.cond(
            position >= LEAD, lambda c: first_stage(position - LEAD, c), lambda c: c, carry
        )

    sums = []
    for stage in range(ITERS):
        if stage == 0:
            odd_sum, even_sum = lax.fori_loop(0, chunks + LEAD, opening, (zero, zero))
        else:
            if stage in LEVEL:
                keep_level()
            odd_sum, even_sum = lax.fori_loop(0, chunks, make_stage(stage), (zero, zero))
            sums.append(odd_sum)
        sums.append(even_sum)

    others = total_devices - 1

    def sum_copy(note, other):
        return pltpu.make_async_remote_copy(
            src_ref=notes.at[note, pl.ds(0, 1)],
            dst_ref=slots.at[note, pl.ds(other - 1, 1)],
            send_sem=sum_send.at[note],
            recv_sem=sum_recv.at[note],
            device_id=peer(other),
            device_id_type=MESH,
        )

    def sum_copies(note):
        return pltpu.make_async_remote_copy(
            src_ref=slots.at[note],
            dst_ref=slots.at[note],
            send_sem=sum_send.at[note],
            recv_sem=sum_recv.at[note],
            device_id=peer(1),
            device_id_type=MESH,
        )

    def gather(note):
        sum_copies(note).wait_recv()
        return jnp.sum(slots[note], axis=0, keepdims=True) + notes[note, 0:1, :]

    for at, value in enumerate(sums):
        moments[at : at + 1, :] = jnp.sum(value, axis=0, keepdims=True)
    moments[len(sums) : SUB, :] = jnp.zeros((SUB - len(sums), cols), jnp.float32)
    folded = jnp.broadcast_to(jnp.sum(moments[...], axis=1, keepdims=True), (SUB, cols))
    notes[0, 0:1, :] = jnp.sum(jnp.where(lane == level, folded, 0.0), axis=0, keepdims=True)
    for other in range(1, total_devices):
        sum_copy(0, other).start()

    for side in range(2):
        @pl.when(sides[side][0])
        def _(side=side):
            rest_copy(side).start()

    def factors(near_side, far_side):
        return jnp.where(near_side, 2.0, 1.0), jnp.where(far_side, 0.0, 1.0)

    first_edge = [(prev_slot, *factors(has_prev, has_next))] * split
    first_edge += [(next_slot, *factors(has_next, has_prev))] * (count - split)
    other_slot = [next_slot] * split + [prev_slot] * (count - split)

    def closing(position, last_sum):
        start, first, last = walk(position)
        rows_here, padded = pl.ds(start, SUB), pl.ds(start + SUB, SUB)
        wait_cols(ITERS, position)
        wait_edges(ITERS, first, last)
        held, pushed, planes = [], [], []
        for p in range(count):
            here, plane = plane_sum(ITERS, p, start)
            plane = spatial[p] * plane
            planes.append(plane)
            held.append(here)
            pushed.append(plane + (temporal[p] * first_edge[p][2]) * here)
        last_sum = last_sum + dot(held, pushed)
        wait_years(ITERS, position)
        pushed = []
        for p in range(count):
            slot, twice, _ = first_edge[p]
            beside = temporal[p] * field[ITERS, slot, p, padded, :]
            resid[ITERS, p, rows_here, :] = planes[p] + beside
            pushed.append(twice * beside)
        return last_sum + dot(held, pushed)

    last_sum = lax.fori_loop(0, chunks, closing, zero)
    notes[1, 0:1, :] = jnp.sum(last_sum, axis=0, keepdims=True)
    for other in range(1, total_devices):
        sum_copy(1, other).start()

    known = jnp.where(lane == level, jnp.broadcast_to(gather(0), (SUB, cols)), 0.0)
    known = jnp.broadcast_to(jnp.sum(known, axis=1, keepdims=True), (SUB, cols))
    mu = [known[at : at + 1, :] for at in range(2 * ITERS - 1)]
    drop = [mu[at] - mu[at + 1] for at in range(2 * ITERS - 2)]

    def form(coefs, table):
        total = None
        for i, left in enumerate(coefs):
            for j in range(i, len(coefs)):
                term = left * coefs[j] * table[i + j]
                term = term if i == j else 2.0 * term
                total = term if total is None else total + term
        return total

    one = jnp.ones_like(mu[0])
    search, direction = [one], [one]
    lengths = [jnp.zeros_like(one)] * ITERS
    inner = mu[0]
    for sweep in range(ITERS - 1):
        alpha = inner / form(direction, drop)
        for j in range(sweep + 1):
            lengths[j] = lengths[j] + alpha * direction[j]
        grown = []
        for j in range(sweep + 2):
            change = None
            if j <= sweep:
                change = direction[j]
            if j > 0:
                change = -direction[j - 1] if change is None else change - direction[j - 1]
            base = search[j] if j <= sweep else None
            grown.append(-alpha * change if base is None else base - alpha * change)
        search = grown
        fresh = form(search, mu)
        ratio = fresh / inner
        inner = fresh
        direction = [
            search[j] + ratio * direction[j] if j <= sweep else search[j]
            for j in range(sweep + 2)
        ]
    curve = form(direction, drop + [mu[-1]])
    bend = direction[-1] * direction[-1]

    def wide(values):
        return [jnp.broadcast_to(value, (SUB, cols)) for value in values]

    def mixes(values, head):
        return wide(
            [head - values[0]]
            + [values[j - 1] - values[j] for j in range(1, ITERS)]
            + [values[-1]]
        )

    paces, steers = wide(lengths[:-1]), wide(direction)
    base_mix, slope_mix = mixes(lengths, 1.0)[:-1], mixes(direction, 0.0)

    def prepare(position, carry):
        start, _, _ = walk(position)
        rows_here, padded = pl.ds(start, SUB), pl.ds(start + SUB, SUB)
        for p in range(count):
            vectors = [field[j + 1, 0, p, padded, :] for j in range(ITERS)]
            total = field[0, 0, p, padded, :]
            for pace, vector in zip(paces, vectors):
                total = total + pace * vector
            anchor[0, p, rows_here, :] = total
            total = steers[0] * vectors[0]
            for steer, vector in zip(steers[1:], vectors[1:]):
                total = total + steer * vector
            slope[0, p, rows_here, :] = total
            vectors = [resid[j, p, rows_here, :] for j in range(ITERS + 1)]
            vectors[-1] = vectors[-1] + temporal[p] * field[ITERS, other_slot[p], p, padded, :]
            total = base_mix[0] * vectors[0]
            for mix, vector in zip(base_mix[1:], vectors[1:]):
                total = total + mix * vector
            anchor[1, p, rows_here, :] = total
            total = slope_mix[0] * vectors[0]
            for mix, vector in zip(slope_mix[1:], vectors[1:]):
                total = total + mix * vector
            slope[1, p, rows_here, :] = total
        return carry

    wait_rest()
    lax.fori_loop(0, chunks, prepare, 0)

    for side in range(4):
        @pl.when(sides[side][0])
        def _(side=side):
            side_sends(side).wait_send()

    for at_last, present in ((False, has_first), (True, has_last)):
        @pl.when(present)
        def _(at_last=at_last):
            row_sends(at_last).wait_send()

    sum_copies(0).wait_send()

    final = jnp.broadcast_to(jnp.sum(gather(1), axis=1, keepdims=True), (1, cols))
    pace[...] = jnp.broadcast_to(inner / (curve - bend * final), (SUB, cols))

    sum_copies(1).wait_send()


def store_kernel(anchor, slope, pace, new_params, residual, total, sem):
    count = total.shape[1]
    step = jnp.broadcast_to(pace[0:1, :], total.shape[1:])
    half = (count + 1) // 2
    copies = []
    for at, out in enumerate((new_params, residual)):
        for piece, (low, high) in enumerate(((0, half), (half, count))):
            where = pl.ds(low, high - low)
            total[at, where] = anchor[at, where] + step[low:high] * slope[at, where]
            copies.append(
                pltpu.make_async_copy(
                    total.at[at, where], out.at[0, where], sem.at[at, piece]
                )
            )
            copies[-1].start()
    for copy in copies:
        copy.wait()


def per_device(sizes, observed, quality, land_mask, params, spatial_weight, temporal_weight):
    n_year, n_row, n_col = sizes
    _, dates, rows, cols = observed.shape
    count = params.shape[1]
    chunks = rows // SUB
    groups = chunks // PAIR
    others = n_year * n_row * n_col - 1
    f32 = jnp.float32
    vmem = pl.BlockSpec(memory_space=pltpu.VMEM)
    hbm = pl.BlockSpec(memory_space=pltpu.HBM)
    dma = pltpu.SemaphoreType.DMA
    both = jax.ShapeDtypeStruct((2, count, rows, cols), f32)
    results = pl.pallas_call(
        functools.partial(kernel, sizes),
        out_shape=(both, both, jax.ShapeDtypeStruct((SUB, cols), f32)),
        in_specs=[hbm] * 6,
        out_specs=(vmem, vmem, vmem),
        scratch_shapes=[
            pltpu.VMEM((dates, rows, cols), f32),
            pltpu.VMEM((dates, rows, cols), jnp.int32),
            pltpu.VMEM((rows, cols), jnp.int32),
            pltpu.SMEM((count,), f32),
            pltpu.SMEM((count,), f32),
            pltpu.VMEM((ROUNDS, 5, count, rows + 2 * SUB, cols), f32),
            pltpu.VMEM((count * (count + 1) // 2, rows, cols), f32),
            pltpu.VMEM((ROUNDS, count, rows, cols), f32),
            pltpu.VMEM((SUB, cols), f32),
            pltpu.VMEM((2, SUB, cols), f32),
            pltpu.VMEM((2, max(others, 1), cols), f32),
            dma((4 + 2 * groups,)),
            dma((4,)),
            dma((2, chunks)),
            dma((2, groups)),
            dma(()),
            dma((2,)),
            dma((2, 2)),
            dma((2,)),
            dma((2,)),
            pltpu.SemaphoreType.REGULAR,
        ],
        compiler_params=pltpu.CompilerParams(
            collective_id=0, has_side_effects=True, vmem_limit_bytes=24 * 2**20
        ),
        name="gauss_newton",
    )(
        *[
            pltpu.with_memory_space_constraint(operand, pltpu.HBM)
            for operand in (
                observed, quality, land_mask, params, spatial_weight, temporal_weight
            )
        ]
    )
    return pl.pallas_call(
        store_kernel,
        out_shape=(
            jax.ShapeDtypeStruct(params.shape, f32),
            jax.ShapeDtypeStruct(params.shape, f32),
        ),
        in_specs=[vmem, vmem, vmem],
        out_specs=(hbm, hbm),
        scratch_shapes=[pltpu.VMEM((2, count, rows, cols), f32), dma((2, 2))],
        compiler_params=pltpu.CompilerParams(vmem_limit_bytes=4 * 2**20),
        name="store",
    )(*results)


def solution(mesh):
    sizes = tuple(mesh.shape[axis] for axis in ("year", "row", "col"))
    grid = P("year", None, "row", "col")
    return jax.shard_map(
        functools.partial(per_device, sizes),
        mesh=mesh,
        in_specs=(grid, grid, P("row", "col"), grid, P(), P()),
        out_specs=(grid, grid),
        check_vma=False,
    )
```

```python
import functools

import jax
import jax.numpy as jnp
from jax import lax
from jax.experimental import pallas as pl
from jax.experimental.pallas import tpu as pltpu
from jax.sharding import PartitionSpec as P

ITERS = 4
ROUNDS = ITERS + 1
SUB = 8
LEAD = 2
PAIR = 2
LEVEL = (1, 2, 3)
DAMPING = 0.1
MESH = pl.DeviceIdType.MESH


def pairs_of(count):
    return [(i, j) for i in range(count) for j in range(i, count)]


def solve(
    sizes,
    observed,
    quality,
    land_mask,
    params,
    spatial_weight,
    temporal_weight,
    anchor,
    slope,
    pace,
    obs,
    qual,
    land,
    spatial,
    temporal,
    field,
    inverse,
    resid,
    moments,
    notes,
    slots,
    load_sem,
    send_sem,
    year_recv,
    col_recv,
    rest_recv,
    row_send,
    row_recv,
    sum_send,
    sum_recv,
    level_sem,
    last_send,
    last_recv,
):
    n_year, n_row, n_col = sizes
    dates, rows, cols = obs.shape
    count = resid.shape[1]
    chunks = rows // SUB
    wide_rows = SUB * PAIR
    pairs = pairs_of(count)
    place = {pair: at for at, pair in enumerate(pairs)}

    year, row, col = lax.axis_index("year"), lax.axis_index("row"), lax.axis_index("col")
    even = lax.rem(row, 2) == 1

    has_prev, has_next = year > 0, year < n_year - 1
    has_left, has_right = col > 0, col < n_col - 1
    has_up, has_down = row > 0, row < n_row - 1
    has_first = jnp.logical_or(jnp.logical_and(even, has_up), jnp.logical_and(~even, has_down))
    has_last = jnp.logical_or(jnp.logical_and(even, has_down), jnp.logical_and(~even, has_up))
    toward_first = row + jnp.where(even, -1, 1)
    toward_last = row + jnp.where(even, 1, -1)

    def chunk_rows(position):
        chunk = jnp.where(even, position, chunks - 1 - position)
        return pl.multiple_of(chunk * SUB, SUB)

    def wide_start(group):
        group = jnp.where(even, group, chunks // PAIR - 1 - group)
        return pl.multiple_of(group * wide_rows, wide_rows)

    total_devices = n_year * n_row * n_col
    near = (n_year - 1) + (n_row - 1) <= ITERS

    def peer(other):
        spot = lax.rem((year * n_row + row) * n_col + col + other, total_devices)
        return (spot // (n_row * n_col), lax.rem(spot // n_col, n_row), lax.rem(spot, n_col))

    barrier = pltpu.get_barrier_semaphore()
    if near:
        for present, target in (
            (has_prev, (year - 1, row, col)),
            (has_next, (year + 1, row, col)),
            (has_up, (year, row - 1, col)),
            (has_down, (year, row + 1, col)),
        ):
            @pl.when(present)
            def _(target=target):
                pl.semaphore_signal(barrier, inc=1, device_id=target, device_id_type=MESH)

        for other in range(1, n_col):
            pl.semaphore_signal(
                barrier,
                inc=1,
                device_id=(year, row, lax.rem(col + other, n_col)),
                device_id_type=MESH,
            )
        expected = n_col - 1
        for present in (has_prev, has_next, has_up, has_down):
            expected = expected + present.astype(jnp.int32)
    else:
        for other in range(1, total_devices):
            pl.semaphore_signal(barrier, inc=1, device_id=peer(other), device_id_type=MESH)
        expected = total_devices - 1

    param_load = pltpu.make_async_copy(
        params.at[0], field.at[0, 0, :, pl.ds(SUB, rows), :], load_sem.at[0]
    )
    small_loads = (
        pltpu.make_async_copy(land_mask, land, load_sem.at[1]),
        pltpu.make_async_copy(spatial_weight, spatial, load_sem.at[2]),
        pltpu.make_async_copy(temporal_weight, temporal, load_sem.at[3]),
    )

    def input_loads(group):
        where = (slice(None), pl.ds(wide_start(group), wide_rows), slice(None))
        return (
            pltpu.make_async_copy(observed.at[0].at[where], obs.at[where], load_sem.at[4 + 2 * group]),
            pltpu.make_async_copy(quality.at[0].at[where], qual.at[where], load_sem.at[5 + 2 * group]),
        )

    param_load.start()
    for copy in small_loads:
        copy.start()
    for group in range(chunks // PAIR):
        for copy in input_loads(group):
            copy.start()

    pl.semaphore_wait(barrier, expected)

    sides = (
        (has_next, (year + 1, row, col), 1, has_prev),
        (has_prev, (year - 1, row, col), 2, has_next),
        (has_right, (year, row, col + 1), 3, has_left),
        (has_left, (year, row, col - 1), 4, has_right),
    )

    split = (count + 1) // 2
    early = (pl.ds(0, split), pl.ds(split, count - split))

    def side_copy(step, position, side):
        _, target, slot, _ = sides[side]
        which = early[side] if side < 2 and step == ITERS else slice(None)
        if side < 2:
            where = pl.ds(chunk_rows(position) + SUB, SUB)
            landing = year_recv.at[step % 2, position]
        else:
            group = position // PAIR
            where = pl.ds(pl.multiple_of(wide_start(group) + SUB, SUB), wide_rows)
            landing = col_recv.at[step % 2, group]
        return pltpu.make_async_remote_copy(
            src_ref=field.at[step, 0, which, where, :],
            dst_ref=field.at[step, slot, which, where, :],
            send_sem=send_sem.at[side],
            recv_sem=landing,
            device_id=target,
            device_id_type=MESH,
        )

    def rest_copy(side):
        _, target, slot, _ = sides[side]
        which, where = early[1 - side], pl.ds(SUB, rows)
        return pltpu.make_async_remote_copy(
            src_ref=field.at[ITERS, 0, which, where, :],
            dst_ref=field.at[ITERS, slot, which, where, :],
            send_sem=send_sem.at[side],
            recv_sem=rest_recv,
            device_id=target,
            device_id_type=MESH,
        )

    def row_spot(last):
        top = jnp.logical_xor(even, last)
        source = pl.multiple_of(jnp.where(top, SUB, rows), SUB)
        target = pl.multiple_of(jnp.where(top, rows + SUB, 0), SUB)
        return source, target, (year, toward_last if last else toward_first, col)

    def row_copy(step, last):
        source, target, device = row_spot(last)
        return pltpu.make_async_remote_copy(
            src_ref=field.at[step, 0, :, pl.ds(source, SUB), :],
            dst_ref=field.at[step, 0, :, pl.ds(target, SUB), :],
            send_sem=row_send.at[int(last)],
            recv_sem=row_recv.at[step % 2, int(last)],
            device_id=device,
            device_id_type=MESH,
        )

    def side_sends(side):
        where = (slice(None), 0, slice(None), pl.ds(SUB, rows), slice(None))
        return pltpu.make_async_remote_copy(
            src_ref=field.at[where],
            dst_ref=field.at[where],
            send_sem=send_sem.at[side],
            recv_sem=send_sem.at[side],
            device_id=sides[side][1],
            device_id_type=MESH,
        )

    def row_sends(last):
        source, _, device = row_spot(last)
        where = (slice(None), 0, slice(None), pl.ds(source, SUB), slice(None))
        return pltpu.make_async_remote_copy(
            src_ref=field.at[where],
            dst_ref=field.at[where],
            send_sem=row_send.at[int(last)],
            recv_sem=row_send.at[int(last)],
            device_id=device,
            device_id_type=MESH,
        )

    def start_sends(step, position):
        for side in range(4):
            present = sides[side][0]
            if side >= 2:
                ready = lax.rem(position, PAIR) == PAIR - 1
                present = jnp.logical_and(present, ready)

            @pl.when(present)
            def _(side=side):
                side_copy(step, position, side).start()

    def wait_pair(first, second, left, right, both):
        @pl.when(jnp.logical_and(first, second))
        def _():
            both.wait_recv()

        @pl.when(jnp.logical_and(first, ~second))
        def _():
            left.wait_recv()

        @pl.when(jnp.logical_and(second, ~first))
        def _():
            right.wait_recv()

    def landing_of(place, semaphore):
        return pltpu.make_async_remote_copy(
            src_ref=place,
            dst_ref=place,
            send_sem=send_sem.at[0],
            recv_sem=semaphore,
            device_id=sides[0][1],
            device_id_type=MESH,
        )

    def wait_years(step, position):
        where = pl.ds(chunk_rows(position) + SUB, SUB)
        slots_here = pl.ds(1, 1 if step == ITERS else 2)
        both = landing_of(
            field.at[step, slots_here, :, where, :], year_recv.at[step % 2, position]
        )
        ends = [side_copy(step, position, side) for side in (0, 1)]
        wait_pair(has_prev, has_next, *ends, both)

    def wait_cols(step, position):
        group = position // PAIR
        where = pl.ds(pl.multiple_of(wide_start(group) + SUB, SUB), wide_rows)
        both = landing_of(
            field.at[step, pl.ds(3, 2), :, where, :], col_recv.at[step % 2, group]
        )
        ends = [side_copy(step, position, side) for side in (2, 3)]

        @pl.when(lax.rem(position, PAIR) == 0)
        def _():
            wait_pair(has_left, has_right, *ends, both)

    def wait_rest():
        both = landing_of(field.at[ITERS, 1, :, pl.ds(SUB, rows), :], rest_recv)
        wait_pair(has_prev, has_next, rest_copy(0), rest_copy(1), both)

    def close_edges(step, first, last):
        for flag, at_last, present in ((first, False, has_first), (last, True, has_last)):
            top = jnp.logical_xor(even, at_last)

            @pl.when(jnp.logical_and(flag, present))
            def _(at_last=at_last):
                row_copy(step, at_last).start()

            def repeat(source, edge, target):
                for p in range(count):
                    block = field[step, 0, p, source : source + SUB, :]
                    field[step, 0, p, target : target + SUB, :] = jnp.broadcast_to(
                        block[edge : edge + 1, :], (SUB, cols)
                    )

            @pl.when(jnp.logical_and(jnp.logical_and(flag, ~present), top))
            def _():
                repeat(SUB, 0, 0)

            @pl.when(jnp.logical_and(jnp.logical_and(flag, ~present), ~top))
            def _():
                repeat(rows, SUB - 1, rows + SUB)

    def wait_edges(step, first, last):
        for flag, at_last, present in ((first, False, has_first), (last, True, has_last)):
            @pl.when(jnp.logical_and(flag, present))
            def _(at_last=at_last):
                row_copy(step, at_last).wait_recv()

    param_load.wait()

    def send_params(position, carry):
        start_sends(0, position)
        return carry

    lax.fori_loop(0, chunks, send_params, 0)
    close_edges(0, True, True)

    prev_slot = jnp.where(has_prev, 1, 0)
    next_slot = jnp.where(has_next, 2, 0)
    left_slot = jnp.where(has_left, 3, 0)
    right_slot = jnp.where(has_right, 4, 0)
    lane = lax.broadcasted_iota(jnp.int32, (SUB, cols), 1)
    level = lax.broadcasted_iota(jnp.int32, (SUB, cols), 0)
    lane_first, lane_last = lane == 0, lane == cols - 1
    level_first, level_last = level == 0, level == SUB - 1
    grid_left = lane == jnp.where(has_left, -1, 0)
    grid_right = lane == jnp.where(has_right, -1, cols - 1)

    def plane_sum(step, p, start):
        own = pl.ds(start + SUB, SUB)
        here = field[step, 0, p, own, :]
        above = field[step, 0, p, pl.ds(start, SUB), :]
        below = field[step, 0, p, pl.ds(start + 2 * SUB, SUB), :]
        up = pltpu.roll(jnp.where(level_last, above, here), 1, 0)
        down = pltpu.roll(jnp.where(level_first, below, here), SUB - 1, 0)
        left = pltpu.roll(jnp.where(lane_last, field[step, left_slot, p, own, :], here), 1, 1)
        right = pltpu.roll(
            jnp.where(lane_first, field[step, right_slot, p, own, :], here), cols - 1, 1
        )
        left = jnp.where(grid_left, here, left)
        right = jnp.where(grid_right, here, right)
        return here, (up + down) + (left + right)

    def around(step, p, start):
        own = pl.ds(start + SUB, SUB)
        here, plane = plane_sum(step, p, start)
        yearly = field[step, prev_slot, p, own, :] + field[step, next_slot, p, own, :]
        return here, spatial[p] * plane + temporal[p] * yearly

    def precondition(start, values):
        rows_here = pl.ds(start, SUB)
        entry = [inverse[at, rows_here, :] for at in range(len(pairs))]
        outs = []
        for p in range(count):
            total = entry[place[(0, p)]] * values[0]
            for q in range(1, count):
                total = total + entry[place[(min(p, q), max(p, q))]] * values[q]
            outs.append(total)
        return outs

    def dot(left, right):
        terms = [a * b for a, b in zip(left, right)]
        while len(terms) > 1:
            terms = [sum(terms[i : i + 2][1:], terms[i]) for i in range(0, len(terms), 2)]
        return terms[0]

    def normal(start):
        here = pl.ds(start, SUB)
        base, peak, slope, rise_mid, rise_log, fall_mid, fall_log = [
            field[0, 0, p, pl.ds(start + SUB, SUB), :] for p in range(count)
        ]
        rise_rate, fall_rate = jnp.exp(rise_log), jnp.exp(fall_log)
        rise_half, fall_half = 0.5 * rise_rate, 0.5 * fall_rate

        def date_step(date, sums):
            time = date.astype(jnp.float32) * (1.0 / dates)
            flag = qual[date, here, :].astype(jnp.float32)
            weight = jnp.maximum(1.0 - 0.5 * flag, 0.0)
            rise_gap = time - rise_mid
            fall_gap = time - fall_mid
            rise = jnp.tanh(rise_half * rise_gap)
            fall = jnp.tanh(fall_half * fall_gap)
            season = rise - fall
            height = peak - slope * time
            rise_bell = height - height * (rise * rise)
            fall_bell = height - height * (fall * fall)
            basis = [
                None,
                season,
                time * season,
                rise_bell,
                rise_gap * rise_bell,
                fall_bell,
                fall_gap * fall_bell,
            ]
            weighted = [weight] + [weight * item for item in basis[1:]]
            out = []
            for i, j in pairs:
                term = weighted[j] if i == 0 else basis[i] * weighted[j]
                out.append(sums[place[(i, j)]] + term)
            seen = obs[date, here, :]
            for i in range(count):
                out.append(sums[len(pairs) + i] + seen * weighted[i])
            return tuple(out)

        zero = jnp.zeros((SUB, cols), jnp.float32)
        sums = lax.fori_loop(
            0, dates, date_step, (zero,) * (len(pairs) + count), unroll=dates
        )
        share = land[here, :].astype(jnp.float32) * (1.0 / dates)
        rise_scale, fall_scale = 0.25 * rise_rate, 0.25 * fall_rate
        scale = [None, 0.5, -0.5, -rise_scale, rise_scale, fall_scale, -fall_scale]
        shared = [share] + [share * item for item in scale[1:]]
        block = {}
        for i, j in pairs:
            factor = shared[j] if i == 0 else shared[j] * scale[i]
            block[(i, j)] = sums[place[(i, j)]] * factor
        for p in range(count):
            total = shared[p] * sums[len(pairs) + p]
            for q, value in ((0, base), (1, peak), (2, slope)):
                total = total - block[(min(p, q), max(p, q))] * value
            resid[0, p, here, :] = total
        for p in range(count):
            block[(p, p)] = block[(p, p)] + (DAMPING + 4.0 * spatial[p] + 2.0 * temporal[p])
        for k in range(count):
            turn = 1.0 / block[(k, k)]
            edge = {i: block[(min(i, k), max(i, k))] for i in range(count) if i != k}
            lean = {i: edge[i] * turn for i in edge}
            for i, j in pairs:
                if i != k and j != k:
                    block[(i, j)] = block[(i, j)] - edge[i] * lean[j]
            for i in edge:
                block[(min(i, k), max(i, k))] = lean[i]
            block[(k, k)] = -turn
        for pair in pairs:
            inverse[place[pair], here, :] = -block[pair]

    zero = jnp.zeros((SUB, cols), jnp.float32)

    def walk(position):
        return chunk_rows(position), position == 0, position == chunks - 1

    def make_stage(stage):
        def body(position, carry):
            odd_sum, even_sum = carry
            start, first, last = walk(position)
            wait_cols(stage, position)
            wait_years(stage, position)
            wait_edges(stage, first, last)
            rows_here = pl.ds(start, SUB)
            held, pushed = [], []
            for p in range(count):
                here, push = around(stage, p, start)
                if stage == 0:
                    push = (resid[0, p, rows_here, :] + push) - (
                        4.0 * spatial[p] + 2.0 * temporal[p]
                    ) * here
                resid[stage, p, rows_here, :] = push
                held.append(here)
                pushed.append(push)
            if stage > 0:
                odd_sum = odd_sum + dot(held, pushed)
            turned = precondition(start, pushed)
            for p in range(count):
                field[stage + 1, 0, p, pl.ds(start + SUB, SUB), :] = turned[p]
            even_sum = even_sum + dot(turned, pushed)
            start_sends(stage + 1, position)
            close_edges(stage + 1, first, last)
            return odd_sum, even_sum

        return body

    def keep_level():
        if n_col % 2 == 0:
            partner = col + 1 - 2 * lax.rem(col, 2)
            pl.semaphore_signal(
                level_sem, inc=1, device_id=(year, row, partner), device_id_type=MESH
            )
            pl.semaphore_wait(level_sem, 1)

    for copy in small_loads:
        copy.wait()

    first_stage = make_stage(0)

    def opening(position, carry):
        @pl.when(position < chunks)
        def _():
            @pl.when(lax.rem(position, PAIR) == 0)
            def _():
                for copy in input_loads(position // PAIR):
                    copy.wait()

            normal(chunk_rows(position))

        return lax.cond(
            position >= LEAD, lambda c: first_stage(position - LEAD, c), lambda c: c, carry
        )

    sums = []
    for stage in range(ITERS):
        if stage == 0:
            odd_sum, even_sum = lax.fori_loop(0, chunks + LEAD, opening, (zero, zero))
        else:
            if stage in LEVEL:
                keep_level()
            odd_sum, even_sum = lax.fori_loop(0, chunks, make_stage(stage), (zero, zero))
            sums.append(odd_sum)
        sums.append(even_sum)

    others = total_devices - 1

    note_sems = ((sum_send, sum_recv), (last_send, last_recv))

    def sum_copy(note, other):
        return pltpu.make_async_remote_copy(
            src_ref=notes.at[note, pl.ds(0, 1)],
            dst_ref=slots.at[note, pl.ds(other - 1, 1)],
            send_sem=note_sems[note][0],
            recv_sem=note_sems[note][1],
            device_id=peer(other),
            device_id_type=MESH,
        )

    for at, value in enumerate(sums):
        moments[at : at + 1, :] = jnp.sum(value, axis=0, keepdims=True)
    moments[len(sums) : SUB, :] = jnp.zeros((SUB - len(sums), cols), jnp.float32)
    folded = jnp.broadcast_to(jnp.sum(moments[...], axis=1, keepdims=True), (SUB, cols))
    notes[0, 0:1, :] = jnp.sum(jnp.where(lane == level, folded, 0.0), axis=0, keepdims=True)
    for other in range(1, total_devices):
        sum_copy(0, other).start()

    for side in range(2):
        @pl.when(sides[side][0])
        def _(side=side):
            rest_copy(side).start()

    def factors(near_side, far_side):
        return jnp.where(near_side, 2.0, 1.0), jnp.where(far_side, 0.0, 1.0)

    first_edge = [(prev_slot, *factors(has_prev, has_next))] * split
    first_edge += [(next_slot, *factors(has_next, has_prev))] * (count - split)
    other_slot = [next_slot] * split + [prev_slot] * (count - split)

    def closing(position, last_sum):
        start, first, last = walk(position)
        rows_here, padded = pl.ds(start, SUB), pl.ds(start + SUB, SUB)
        wait_cols(ITERS, position)
        wait_edges(ITERS, first, last)
        held, pushed, planes = [], [], []
        for p in range(count):
            here, plane = plane_sum(ITERS, p, start)
            plane = spatial[p] * plane
            planes.append(plane)
            held.append(here)
            pushed.append(plane + (temporal[p] * first_edge[p][2]) * here)
        last_sum = last_sum + dot(held, pushed)
        wait_years(ITERS, position)
        pushed = []
        for p in range(count):
            slot, twice, _ = first_edge[p]
            beside = temporal[p] * field[ITERS, slot, p, padded, :]
            resid[ITERS, p, rows_here, :] = planes[p] + beside
            pushed.append(twice * beside)
        return last_sum + dot(held, pushed)

    last_sum = lax.fori_loop(0, chunks, closing, zero)
    notes[1, 0:1, :] = jnp.sum(last_sum, axis=0, keepdims=True)
    for other in range(1, total_devices):
        sum_copy(1, other).start()

    known = gather(slots, notes, 0, *note_sems[0], peer(1))
    known = jnp.where(lane == level, jnp.broadcast_to(known, (SUB, cols)), 0.0)
    known = jnp.broadcast_to(jnp.sum(known, axis=1, keepdims=True), (SUB, cols))
    mu = [known[at : at + 1, :] for at in range(2 * ITERS - 1)]
    drop = [mu[at] - mu[at + 1] for at in range(2 * ITERS - 2)]

    def form(coefs, table):
        total = None
        for i, left in enumerate(coefs):
            for j in range(i, len(coefs)):
                term = left * coefs[j] * table[i + j]
                term = term if i == j else 2.0 * term
                total = term if total is None else total + term
        return total

    one = jnp.ones_like(mu[0])
    search, direction = [one], [one]
    lengths = [jnp.zeros_like(one)] * ITERS
    inner = mu[0]
    for sweep in range(ITERS - 1):
        alpha = inner / form(direction, drop)
        for j in range(sweep + 1):
            lengths[j] = lengths[j] + alpha * direction[j]
        grown = []
        for j in range(sweep + 2):
            change = None
            if j <= sweep:
                change = direction[j]
            if j > 0:
                change = -direction[j - 1] if change is None else change - direction[j - 1]
            base = search[j] if j <= sweep else None
            grown.append(-alpha * change if base is None else base - alpha * change)
        search = grown
        fresh = form(search, mu)
        ratio = fresh / inner
        inner = fresh
        direction = [
            search[j] + ratio * direction[j] if j <= sweep else search[j]
            for j in range(sweep + 2)
        ]
    curve = form(direction, drop + [mu[-1]])
    bend = direction[-1] * direction[-1]

    def wide(values):
        return [jnp.broadcast_to(value, (SUB, cols)) for value in values]

    def mixes(values, head):
        return wide(
            [head - values[0]]
            + [values[j - 1] - values[j] for j in range(1, ITERS)]
            + [values[-1]]
        )

    paces, steers = wide(lengths[:-1]), wide(direction)
    base_mix, slope_mix = mixes(lengths, 1.0)[:-1], mixes(direction, 0.0)

    def prepare(position, carry):
        start, _, _ = walk(position)
        rows_here, padded = pl.ds(start, SUB), pl.ds(start + SUB, SUB)
        for p in range(count):
            vectors = [field[j + 1, 0, p, padded, :] for j in range(ITERS)]
            total = field[0, 0, p, padded, :]
            for pace, vector in zip(paces, vectors):
                total = total + pace * vector
            anchor[0, p, rows_here, :] = total
            total = steers[0] * vectors[0]
            for steer, vector in zip(steers[1:], vectors[1:]):
                total = total + steer * vector
            slope[0, p, rows_here, :] = total
            vectors = [resid[j, p, rows_here, :] for j in range(ITERS + 1)]
            vectors[-1] = vectors[-1] + temporal[p] * field[ITERS, other_slot[p], p, padded, :]
            total = base_mix[0] * vectors[0]
            for mix, vector in zip(base_mix[1:], vectors[1:]):
                total = total + mix * vector
            anchor[1, p, rows_here, :] = total
            total = slope_mix[0] * vectors[0]
            for mix, vector in zip(slope_mix[1:], vectors[1:]):
                total = total + mix * vector
            slope[1, p, rows_here, :] = total
        return carry

    wait_rest()
    lax.fori_loop(0, chunks, prepare, 0)

    for side in range(4):
        @pl.when(sides[side][0])
        def _(side=side):
            side_sends(side).wait_send()

    for at_last, present in ((False, has_first), (True, has_last)):
        @pl.when(present)
        def _(at_last=at_last):
            row_sends(at_last).wait_send()

    note_copies(slots, 0, *note_sems[0], peer(1)).wait_send()

    return inner, curve, bend


def note_copies(slots, note, send, recv, device):
    return pltpu.make_async_remote_copy(
        src_ref=slots.at[note],
        dst_ref=slots.at[note],
        send_sem=send,
        recv_sem=recv,
        device_id=device,
        device_id_type=MESH,
    )


def gather(slots, notes, note, send, recv, device):
    note_copies(slots, note, send, recv, device).wait_recv()
    return jnp.sum(slots[note], axis=0, keepdims=True) + notes[note, 0:1, :]


def kernel(sizes, *refs):
    *refs, last_send, last_recv = refs
    pace, notes, slots = refs[8], refs[-2], refs[-1]
    obs = refs[9]
    chunks = obs.shape[1] // SUB
    groups = chunks // PAIR
    dma = pltpu.SemaphoreType.DMA

    def scope(*sems):
        return solve(sizes, *refs, *sems, last_send, last_recv)

    inner, curve, bend = pl.run_scoped(
        scope,
        dma((4 + 2 * groups,)),
        dma((4,)),
        dma((2, chunks)),
        dma((2, groups)),
        dma(()),
        dma((2,)),
        dma((2, 2)),
        dma(()),
        dma(()),
        pltpu.SemaphoreType.REGULAR,
    )
    years, rows, cols = (lax.axis_index(axis) for axis in ("year", "row", "col"))
    device = (years, rows, lax.rem(cols + 1, sizes[2]))
    final = gather(slots, notes, 1, last_send, last_recv, device)
    final = jnp.broadcast_to(jnp.sum(final, axis=1, keepdims=True), final.shape)
    pace[...] = jnp.broadcast_to(inner / (curve - bend * final), pace.shape)
    note_copies(slots, 1, last_send, last_recv, device).wait_send()


def store_kernel(anchor, slope, pace, new_params, residual, total, sem):
    count = total.shape[1]
    step = jnp.broadcast_to(pace[0:1, :], total.shape[1:])
    half = (count + 1) // 2
    copies = []
    for at, out in enumerate((new_params, residual)):
        for piece, (low, high) in enumerate(((0, half), (half, count))):
            where = pl.ds(low, high - low)
            total[at, where] = anchor[at, where] + step[low:high] * slope[at, where]
            copies.append(
                pltpu.make_async_copy(
                    total.at[at, where], out.at[0, where], sem.at[at, piece]
                )
            )
            copies[-1].start()
    for copy in copies:
        copy.wait()


def per_device(sizes, observed, quality, land_mask, params, spatial_weight, temporal_weight):
    n_year, n_row, n_col = sizes
    _, dates, rows, cols = observed.shape
    count = params.shape[1]
    chunks = rows // SUB
    groups = chunks // PAIR
    others = n_year * n_row * n_col - 1
    f32 = jnp.float32
    vmem = pl.BlockSpec(memory_space=pltpu.VMEM)
    hbm = pl.BlockSpec(memory_space=pltpu.HBM)
    dma = pltpu.SemaphoreType.DMA
    both = jax.ShapeDtypeStruct((2, count, rows, cols), f32)
    results = pl.pallas_call(
        functools.partial(kernel, sizes),
        out_shape=(both, both, jax.ShapeDtypeStruct((SUB, cols), f32)),
        in_specs=[hbm] * 6,
        out_specs=(vmem, vmem, vmem),
        scratch_shapes=[
            pltpu.VMEM((dates, rows, cols), f32),
            pltpu.VMEM((dates, rows, cols), jnp.int32),
            pltpu.VMEM((rows, cols), jnp.int32),
            pltpu.SMEM((count,), f32),
            pltpu.SMEM((count,), f32),
            pltpu.VMEM((ROUNDS, 5, count, rows + 2 * SUB, cols), f32),
            pltpu.VMEM((count * (count + 1) // 2, rows, cols), f32),
            pltpu.VMEM((ROUNDS, count, rows, cols), f32),
            pltpu.VMEM((SUB, cols), f32),
            pltpu.VMEM((2, SUB, cols), f32),
            pltpu.VMEM((2, max(others, 1), cols), f32),
            dma(()),
            dma(()),
        ],
        compiler_params=pltpu.CompilerParams(
            collective_id=0, has_side_effects=True, vmem_limit_bytes=24 * 2**20
        ),
        name="gauss_newton",
    )(
        *[
            pltpu.with_memory_space_constraint(operand, pltpu.HBM)
            for operand in (
                observed, quality, land_mask, params, spatial_weight, temporal_weight
            )
        ]
    )
    return pl.pallas_call(
        store_kernel,
        out_shape=(
            jax.ShapeDtypeStruct(params.shape, f32),
            jax.ShapeDtypeStruct(params.shape, f32),
        ),
        in_specs=[vmem, vmem, vmem],
        out_specs=(hbm, hbm),
        scratch_shapes=[pltpu.VMEM((2, count, rows, cols), f32), dma((2, 2))],
        compiler_params=pltpu.CompilerParams(vmem_limit_bytes=4 * 2**20),
        name="store",
    )(*results)


def solution(mesh):
    sizes = tuple(mesh.shape[axis] for axis in ("year", "row", "col"))
    grid = P("year", None, "row", "col")
    return jax.shard_map(
        functools.partial(per_device, sizes),
        mesh=mesh,
        in_specs=(grid, grid, P("row", "col"), grid, P(), P()),
        out_specs=(grid, grid),
        check_vma=False,
    )
```

```python
import functools

import jax
import jax.numpy as jnp
from jax import lax
from jax.experimental import pallas as pl
from jax.experimental.pallas import tpu as pltpu
from jax.sharding import PartitionSpec as P

ITERS = 4
ROUNDS = ITERS + 1
SUB = 8
LEAD = 2
PAIR = 2
LEVEL = (1, 2, 3)
DAMPING = 0.1
MESH = pl.DeviceIdType.MESH


def pairs_of(count):
    return [(i, j) for i in range(count) for j in range(i, count)]


def solve(
    sizes,
    observed,
    quality,
    land_mask,
    params,
    spatial_weight,
    temporal_weight,
    anchor,
    slope,
    pace,
    obs,
    qual,
    land,
    spatial,
    temporal,
    field,
    inverse,
    resid,
    moments,
    notes,
    slots,
    load_sem,
    send_sem,
    year_recv,
    col_recv,
    rest_recv,
    row_send,
    row_recv,
    sum_send,
    sum_recv,
    level_sem,
    last_send,
    last_recv,
):
    n_year, n_row, n_col = sizes
    dates, rows, cols = obs.shape
    count = resid.shape[1]
    chunks = rows // SUB
    wide_rows = SUB * PAIR
    pairs = pairs_of(count)
    place = {pair: at for at, pair in enumerate(pairs)}

    year, row, col = lax.axis_index("year"), lax.axis_index("row"), lax.axis_index("col")
    even = lax.rem(row, 2) == 1

    has_prev, has_next = year > 0, year < n_year - 1
    has_left, has_right = col > 0, col < n_col - 1
    has_up, has_down = row > 0, row < n_row - 1
    has_first = jnp.logical_or(jnp.logical_and(even, has_up), jnp.logical_and(~even, has_down))
    has_last = jnp.logical_or(jnp.logical_and(even, has_down), jnp.logical_and(~even, has_up))
    toward_first = row + jnp.where(even, -1, 1)
    toward_last = row + jnp.where(even, 1, -1)

    def chunk_rows(position):
        chunk = jnp.where(even, position, chunks - 1 - position)
        return pl.multiple_of(chunk * SUB, SUB)

    def wide_start(group):
        group = jnp.where(even, group, chunks // PAIR - 1 - group)
        return pl.multiple_of(group * wide_rows, wide_rows)

    total_devices = n_year * n_row * n_col
    near = (n_year - 1) + (n_row - 1) <= ITERS

    def peer(other):
        spot = lax.rem((year * n_row + row) * n_col + col + other, total_devices)
        return (spot // (n_row * n_col), lax.rem(spot // n_col, n_row), lax.rem(spot, n_col))

    barrier = pltpu.get_barrier_semaphore()
    if near:
        for present, target in (
            (has_prev, (year - 1, row, col)),
            (has_next, (year + 1, row, col)),
            (has_up, (year, row - 1, col)),
            (has_down, (year, row + 1, col)),
        ):
            @pl.when(present)
            def _(target=target):
                pl.semaphore_signal(barrier, inc=1, device_id=target, device_id_type=MESH)

        for other in range(1, n_col):
            pl.semaphore_signal(
                barrier,
                inc=1,
                device_id=(year, row, lax.rem(col + other, n_col)),
                device_id_type=MESH,
            )
        expected = n_col - 1
        for present in (has_prev, has_next, has_up, has_down):
            expected = expected + present.astype(jnp.int32)
    else:
        for other in range(1, total_devices):
            pl.semaphore_signal(barrier, inc=1, device_id=peer(other), device_id_type=MESH)
        expected = total_devices - 1

    param_load = pltpu.make_async_copy(
        params.at[0], field.at[0, 0, :, pl.ds(SUB, rows), :], load_sem.at[0]
    )
    small_loads = (
        pltpu.make_async_copy(land_mask, land, load_sem.at[1]),
        pltpu.make_async_copy(spatial_weight, spatial, load_sem.at[2]),
        pltpu.make_async_copy(temporal_weight, temporal, load_sem.at[3]),
    )

    def input_loads(group):
        where = (slice(None), pl.ds(wide_start(group), wide_rows), slice(None))
        return (
            pltpu.make_async_copy(observed.at[0].at[where], obs.at[where], load_sem.at[4 + 2 * group]),
            pltpu.make_async_copy(quality.at[0].at[where], qual.at[where], load_sem.at[5 + 2 * group]),
        )

    param_load.start()
    for copy in small_loads:
        copy.start()
    for group in range(chunks // PAIR):
        for copy in input_loads(group):
            copy.start()

    pl.semaphore_wait(barrier, expected)

    sides = (
        (has_next, (year + 1, row, col), 1, has_prev),
        (has_prev, (year - 1, row, col), 2, has_next),
        (has_right, (year, row, col + 1), 3, has_left),
        (has_left, (year, row, col - 1), 4, has_right),
    )

    split = count // 2
    early = (pl.ds(0, split), pl.ds(split, count - split))

    def side_copy(step, position, side):
        _, target, slot, _ = sides[side]
        which = early[side] if side < 2 and step == ITERS else slice(None)
        if side < 2:
            where = pl.ds(chunk_rows(position) + SUB, SUB)
            landing = year_recv.at[step % 2, position]
        else:
            group = position // PAIR
            where = pl.ds(pl.multiple_of(wide_start(group) + SUB, SUB), wide_rows)
            landing = col_recv.at[step % 2, group]
        return pltpu.make_async_remote_copy(
            src_ref=field.at[step, 0, which, where, :],
            dst_ref=field.at[step, slot, which, where, :],
            send_sem=send_sem.at[side],
            recv_sem=landing,
            device_id=target,
            device_id_type=MESH,
        )

    def rest_copy(side, low=0, high=rows):
        _, target, slot, _ = sides[side]
        which, where = early[1 - side], pl.ds(SUB + low, high - low)
        return pltpu.make_async_remote_copy(
            src_ref=field.at[ITERS, 0, which, where, :],
            dst_ref=field.at[ITERS, slot, which, where, :],
            send_sem=send_sem.at[side],
            recv_sem=rest_recv,
            device_id=target,
            device_id_type=MESH,
        )

    def row_spot(last):
        top = jnp.logical_xor(even, last)
        source = pl.multiple_of(jnp.where(top, SUB, rows), SUB)
        target = pl.multiple_of(jnp.where(top, rows + SUB, 0), SUB)
        return source, target, (year, toward_last if last else toward_first, col)

    def row_copy(step, last):
        source, target, device = row_spot(last)
        return pltpu.make_async_remote_copy(
            src_ref=field.at[step, 0, :, pl.ds(source, SUB), :],
            dst_ref=field.at[step, 0, :, pl.ds(target, SUB), :],
            send_sem=row_send.at[int(last)],
            recv_sem=row_recv.at[step % 2, int(last)],
            device_id=device,
            device_id_type=MESH,
        )

    def side_sends(side):
        where = (slice(None), 0, slice(None), pl.ds(SUB, rows), slice(None))
        return pltpu.make_async_remote_copy(
            src_ref=field.at[where],
            dst_ref=field.at[where],
            send_sem=send_sem.at[side],
            recv_sem=send_sem.at[side],
            device_id=sides[side][1],
            device_id_type=MESH,
        )

    def row_sends(last):
        source, _, device = row_spot(last)
        where = (slice(None), 0, slice(None), pl.ds(source, SUB), slice(None))
        return pltpu.make_async_remote_copy(
            src_ref=field.at[where],
            dst_ref=field.at[where],
            send_sem=row_send.at[int(last)],
            recv_sem=row_send.at[int(last)],
            device_id=device,
            device_id_type=MESH,
        )

    def start_sends(step, position):
        for side in range(4):
            present = sides[side][0]
            if side >= 2:
                ready = lax.rem(position, PAIR) == PAIR - 1
                present = jnp.logical_and(present, ready)

            @pl.when(present)
            def _(side=side):
                side_copy(step, position, side).start()

    def wait_pair(first, second, left, right, both):
        @pl.when(jnp.logical_and(first, second))
        def _():
            both.wait_recv()

        @pl.when(jnp.logical_and(first, ~second))
        def _():
            left.wait_recv()

        @pl.when(jnp.logical_and(second, ~first))
        def _():
            right.wait_recv()

    def landing_of(place, semaphore):
        return pltpu.make_async_remote_copy(
            src_ref=place,
            dst_ref=place,
            send_sem=send_sem.at[0],
            recv_sem=semaphore,
            device_id=sides[0][1],
            device_id_type=MESH,
        )

    def wait_years(step, position):
        where = pl.ds(chunk_rows(position) + SUB, SUB)
        slots_here = pl.ds(1, 1 if step == ITERS else 2)
        both = landing_of(
            field.at[step, slots_here, :, where, :], year_recv.at[step % 2, position]
        )
        ends = [side_copy(step, position, side) for side in (0, 1)]
        wait_pair(has_prev, has_next, *ends, both)

    def wait_cols(step, position):
        group = position // PAIR
        where = pl.ds(pl.multiple_of(wide_start(group) + SUB, SUB), wide_rows)
        both = landing_of(
            field.at[step, pl.ds(3, 2), :, where, :], col_recv.at[step % 2, group]
        )
        ends = [side_copy(step, position, side) for side in (2, 3)]

        @pl.when(lax.rem(position, PAIR) == 0)
        def _():
            wait_pair(has_left, has_right, *ends, both)

    def wait_rest():
        both = landing_of(field.at[ITERS, 1, :, pl.ds(SUB, rows), :], rest_recv)
        wait_pair(has_prev, has_next, rest_copy(0), rest_copy(1), both)

    def close_edges(step, first, last):
        for flag, at_last, present in ((first, False, has_first), (last, True, has_last)):
            top = jnp.logical_xor(even, at_last)

            @pl.when(jnp.logical_and(flag, present))
            def _(at_last=at_last):
                row_copy(step, at_last).start()

            def repeat(source, edge, target):
                for p in range(count):
                    block = field[step, 0, p, source : source + SUB, :]
                    field[step, 0, p, target : target + SUB, :] = jnp.broadcast_to(
                        block[edge : edge + 1, :], (SUB, cols)
                    )

            @pl.when(jnp.logical_and(jnp.logical_and(flag, ~present), top))
            def _():
                repeat(SUB, 0, 0)

            @pl.when(jnp.logical_and(jnp.logical_and(flag, ~present), ~top))
            def _():
                repeat(rows, SUB - 1, rows + SUB)

    def wait_edges(step, first, last):
        for flag, at_last, present in ((first, False, has_first), (last, True, has_last)):
            @pl.when(jnp.logical_and(flag, present))
            def _(at_last=at_last):
                row_copy(step, at_last).wait_recv()

    param_load.wait()

    def send_params(position, carry):
        start_sends(0, position)
        return carry

    lax.fori_loop(0, chunks, send_params, 0)
    close_edges(0, True, True)

    prev_slot = jnp.where(has_prev, 1, 0)
    next_slot = jnp.where(has_next, 2, 0)
    left_slot = jnp.where(has_left, 3, 0)
    right_slot = jnp.where(has_right, 4, 0)
    lane = lax.broadcasted_iota(jnp.int32, (SUB, cols), 1)
    level = lax.broadcasted_iota(jnp.int32, (SUB, cols), 0)
    lane_first, lane_last = lane == 0, lane == cols - 1
    level_first, level_last = level == 0, level == SUB - 1
    grid_left = lane == jnp.where(has_left, -1, 0)
    grid_right = lane == jnp.where(has_right, -1, cols - 1)

    def plane_sum(step, p, start):
        own = pl.ds(start + SUB, SUB)
        here = field[step, 0, p, own, :]
        above = field[step, 0, p, pl.ds(start, SUB), :]
        below = field[step, 0, p, pl.ds(start + 2 * SUB, SUB), :]
        up = pltpu.roll(jnp.where(level_last, above, here), 1, 0)
        down = pltpu.roll(jnp.where(level_first, below, here), SUB - 1, 0)
        left = pltpu.roll(jnp.where(lane_last, field[step, left_slot, p, own, :], here), 1, 1)
        right = pltpu.roll(
            jnp.where(lane_first, field[step, right_slot, p, own, :], here), cols - 1, 1
        )
        left = jnp.where(grid_left, here, left)
        right = jnp.where(grid_right, here, right)
        return here, (up + down) + (left + right)

    def around(step, p, start):
        own = pl.ds(start + SUB, SUB)
        here, plane = plane_sum(step, p, start)
        yearly = field[step, prev_slot, p, own, :] + field[step, next_slot, p, own, :]
        return here, spatial[p] * plane + temporal[p] * yearly

    def precondition(start, values):
        rows_here = pl.ds(start, SUB)
        entry = [inverse[at, rows_here, :] for at in range(len(pairs))]
        outs = []
        for p in range(count):
            total = entry[place[(0, p)]] * values[0]
            for q in range(1, count):
                total = total + entry[place[(min(p, q), max(p, q))]] * values[q]
            outs.append(total)
        return outs

    def dot(left, right):
        terms = [a * b for a, b in zip(left, right)]
        while len(terms) > 1:
            terms = [sum(terms[i : i + 2][1:], terms[i]) for i in range(0, len(terms), 2)]
        return terms[0]

    def normal(start):
        here = pl.ds(start, SUB)
        base, peak, slope, rise_mid, rise_log, fall_mid, fall_log = [
            field[0, 0, p, pl.ds(start + SUB, SUB), :] for p in range(count)
        ]
        rise_rate, fall_rate = jnp.exp(rise_log), jnp.exp(fall_log)
        rise_half, fall_half = 0.5 * rise_rate, 0.5 * fall_rate

        def date_step(date, sums):
            time = date.astype(jnp.float32) * (1.0 / dates)
            flag = qual[date, here, :].astype(jnp.float32)
            weight = jnp.maximum(1.0 - 0.5 * flag, 0.0)
            rise_gap = time - rise_mid
            fall_gap = time - fall_mid
            rise = jnp.tanh(rise_half * rise_gap)
            fall = jnp.tanh(fall_half * fall_gap)
            season = rise - fall
            height = peak - slope * time
            rise_bell = height - height * (rise * rise)
            fall_bell = height - height * (fall * fall)
            basis = [
                None,
                season,
                time * season,
                rise_bell,
                rise_gap * rise_bell,
                fall_bell,
                fall_gap * fall_bell,
            ]
            weighted = [weight] + [weight * item for item in basis[1:]]
            out = []
            for i, j in pairs:
                term = weighted[j] if i == 0 else basis[i] * weighted[j]
                out.append(sums[place[(i, j)]] + term)
            seen = obs[date, here, :]
            for i in range(count):
                out.append(sums[len(pairs) + i] + seen * weighted[i])
            return tuple(out)

        zero = jnp.zeros((SUB, cols), jnp.float32)
        sums = lax.fori_loop(
            0, dates, date_step, (zero,) * (len(pairs) + count), unroll=dates
        )
        share = land[here, :].astype(jnp.float32) * (1.0 / dates)
        rise_scale, fall_scale = 0.25 * rise_rate, 0.25 * fall_rate
        scale = [None, 0.5, -0.5, -rise_scale, rise_scale, fall_scale, -fall_scale]
        shared = [share] + [share * item for item in scale[1:]]
        block = {}
        for i, j in pairs:
            factor = shared[j] if i == 0 else shared[j] * scale[i]
            block[(i, j)] = sums[place[(i, j)]] * factor
        for p in range(count):
            total = shared[p] * sums[len(pairs) + p]
            for q, value in ((0, base), (1, peak), (2, slope)):
                total = total - block[(min(p, q), max(p, q))] * value
            resid[0, p, here, :] = total
        for p in range(count):
            block[(p, p)] = block[(p, p)] + (DAMPING + 4.0 * spatial[p] + 2.0 * temporal[p])
        for k in range(count):
            turn = 1.0 / block[(k, k)]
            edge = {i: block[(min(i, k), max(i, k))] for i in range(count) if i != k}
            lean = {i: edge[i] * turn for i in edge}
            for i, j in pairs:
                if i != k and j != k:
                    block[(i, j)] = block[(i, j)] - edge[i] * lean[j]
            for i in edge:
                block[(min(i, k), max(i, k))] = lean[i]
            block[(k, k)] = -turn
        for pair in pairs:
            inverse[place[pair], here, :] = -block[pair]

    zero = jnp.zeros((SUB, cols), jnp.float32)

    def walk(position):
        return chunk_rows(position), position == 0, position == chunks - 1

    def make_stage(stage):
        def body(position, carry):
            odd_sum, even_sum = carry
            start, first, last = walk(position)
            wait_cols(stage, position)
            wait_years(stage, position)
            wait_edges(stage, first, last)
            rows_here = pl.ds(start, SUB)
            held, pushed = [], []
            for p in range(count):
                here, push = around(stage, p, start)
                if stage == 0:
                    push = (resid[0, p, rows_here, :] + push) - (
                        4.0 * spatial[p] + 2.0 * temporal[p]
                    ) * here
                resid[stage, p, rows_here, :] = push
                held.append(here)
                pushed.append(push)
            if stage > 0:
                odd_sum = odd_sum + dot(held, pushed)
            turned = precondition(start, pushed)
            for p in range(count):
                field[stage + 1, 0, p, pl.ds(start + SUB, SUB), :] = turned[p]
            even_sum = even_sum + dot(turned, pushed)
            start_sends(stage + 1, position)
            close_edges(stage + 1, first, last)
            return odd_sum, even_sum

        return body

    def keep_level():
        if n_col % 2 == 0:
            partner = col + 1 - 2 * lax.rem(col, 2)
            pl.semaphore_signal(
                level_sem, inc=1, device_id=(year, row, partner), device_id_type=MESH
            )
            pl.semaphore_wait(level_sem, 1)

    for copy in small_loads:
        copy.wait()

    first_stage = make_stage(0)

    def opening(position, carry):
        @pl.when(position < chunks)
        def _():
            @pl.when(lax.rem(position, PAIR) == 0)
            def _():
                for copy in input_loads(position // PAIR):
                    copy.wait()

            normal(chunk_rows(position))

        return lax.cond(
            position >= LEAD, lambda c: first_stage(position - LEAD, c), lambda c: c, carry
        )

    sums = []
    for stage in range(ITERS):
        if stage == 0:
            odd_sum, even_sum = lax.fori_loop(0, chunks + LEAD, opening, (zero, zero))
        else:
            if stage in LEVEL:
                keep_level()
            odd_sum, even_sum = lax.fori_loop(0, chunks, make_stage(stage), (zero, zero))
            sums.append(odd_sum)
        sums.append(even_sum)

    others = total_devices - 1

    note_sems = ((sum_send, sum_recv), (last_send, last_recv))

    def sum_copy(note, other):
        return pltpu.make_async_remote_copy(
            src_ref=notes.at[note, pl.ds(0, 1)],
            dst_ref=slots.at[note, pl.ds(other - 1, 1)],
            send_sem=note_sems[note][0],
            recv_sem=note_sems[note][1],
            device_id=peer(other),
            device_id_type=MESH,
        )

    def start_rest(low, high):
        for side in range(2):
            @pl.when(sides[side][0])
            def _(side=side):
                rest_copy(side, low, high).start()

    cut, tail = rows // 2 // SUB * SUB, rows // 4 // SUB * SUB
    start_rest(0, cut)

    for at, value in enumerate(sums):
        moments[at : at + 1, :] = jnp.sum(value, axis=0, keepdims=True)
    moments[len(sums) : SUB, :] = jnp.zeros((SUB - len(sums), cols), jnp.float32)
    folded = jnp.broadcast_to(jnp.sum(moments[...], axis=1, keepdims=True), (SUB, cols))
    notes[0, 0:1, :] = jnp.sum(jnp.where(lane == level, folded, 0.0), axis=0, keepdims=True)
    for other in range(1, total_devices):
        sum_copy(0, other).start()

    start_rest(cut, rows - tail)

    def factors(near_side, far_side):
        return jnp.where(near_side, 2.0, 1.0), jnp.where(far_side, 0.0, 1.0)

    first_edge = [(prev_slot, *factors(has_prev, has_next))] * split
    first_edge += [(next_slot, *factors(has_next, has_prev))] * (count - split)
    other_slot = [next_slot] * split + [prev_slot] * (count - split)

    def closing(position, last_sum):
        start, first, last = walk(position)
        rows_here, padded = pl.ds(start, SUB), pl.ds(start + SUB, SUB)
        wait_cols(ITERS, position)
        wait_edges(ITERS, first, last)
        held, pushed, planes = [], [], []
        for p in range(count):
            here, plane = plane_sum(ITERS, p, start)
            plane = spatial[p] * plane
            planes.append(plane)
            held.append(here)
            pushed.append(plane + (temporal[p] * first_edge[p][2]) * here)
        last_sum = last_sum + dot(held, pushed)
        wait_years(ITERS, position)
        pushed = []
        for p in range(count):
            slot, twice, _ = first_edge[p]
            beside = temporal[p] * field[ITERS, slot, p, padded, :]
            resid[ITERS, p, rows_here, :] = planes[p] + beside
            pushed.append(twice * beside)
        return last_sum + dot(held, pushed)

    last_sum = lax.fori_loop(0, chunks, closing, zero)
    notes[1, 0:1, :] = jnp.sum(last_sum, axis=0, keepdims=True)
    for other in range(1, total_devices):
        sum_copy(1, other).start()
    start_rest(rows - tail, rows)

    known = gather(slots, notes, 0, *note_sems[0], peer(1))
    known = jnp.where(lane == level, jnp.broadcast_to(known, (SUB, cols)), 0.0)
    known = jnp.broadcast_to(jnp.sum(known, axis=1, keepdims=True), (SUB, cols))
    mu = [known[at : at + 1, :] for at in range(2 * ITERS - 1)]
    drop = [mu[at] - mu[at + 1] for at in range(2 * ITERS - 2)]

    def form(coefs, table):
        total = None
        for i, left in enumerate(coefs):
            for j in range(i, len(coefs)):
                term = left * coefs[j] * table[i + j]
                term = term if i == j else 2.0 * term
                total = term if total is None else total + term
        return total

    one = jnp.ones_like(mu[0])
    search, direction = [one], [one]
    lengths = [jnp.zeros_like(one)] * ITERS
    inner = mu[0]
    for sweep in range(ITERS - 1):
        alpha = inner / form(direction, drop)
        for j in range(sweep + 1):
            lengths[j] = lengths[j] + alpha * direction[j]
        grown = []
        for j in range(sweep + 2):
            change = None
            if j <= sweep:
                change = direction[j]
            if j > 0:
                change = -direction[j - 1] if change is None else change - direction[j - 1]
            base = search[j] if j <= sweep else None
            grown.append(-alpha * change if base is None else base - alpha * change)
        search = grown
        fresh = form(search, mu)
        ratio = fresh / inner
        inner = fresh
        direction = [
            search[j] + ratio * direction[j] if j <= sweep else search[j]
            for j in range(sweep + 2)
        ]
    curve = form(direction, drop + [mu[-1]])
    bend = direction[-1] * direction[-1]

    def wide(values):
        return [jnp.broadcast_to(value, (SUB, cols)) for value in values]

    def mixes(values, head):
        return wide(
            [head - values[0]]
            + [values[j - 1] - values[j] for j in range(1, ITERS)]
            + [values[-1]]
        )

    paces, steers = wide(lengths[:-1]), wide(direction)
    base_mix, slope_mix = mixes(lengths, 1.0)[:-1], mixes(direction, 0.0)

    def prepare(position, carry):
        start, _, _ = walk(position)
        rows_here, padded = pl.ds(start, SUB), pl.ds(start + SUB, SUB)
        for p in range(count):
            vectors = [field[j + 1, 0, p, padded, :] for j in range(ITERS)]
            total = field[0, 0, p, padded, :]
            for pace, vector in zip(paces, vectors):
                total = total + pace * vector
            anchor[0, p, rows_here, :] = total
            total = steers[0] * vectors[0]
            for steer, vector in zip(steers[1:], vectors[1:]):
                total = total + steer * vector
            slope[0, p, rows_here, :] = total
            vectors = [resid[j, p, rows_here, :] for j in range(ITERS + 1)]
            vectors[-1] = vectors[-1] + temporal[p] * field[ITERS, other_slot[p], p, padded, :]
            total = base_mix[0] * vectors[0]
            for mix, vector in zip(base_mix[1:], vectors[1:]):
                total = total + mix * vector
            anchor[1, p, rows_here, :] = total
            total = slope_mix[0] * vectors[0]
            for mix, vector in zip(slope_mix[1:], vectors[1:]):
                total = total + mix * vector
            slope[1, p, rows_here, :] = total
        return carry

    wait_rest()
    lax.fori_loop(0, chunks, prepare, 0)

    for side in range(4):
        @pl.when(sides[side][0])
        def _(side=side):
            side_sends(side).wait_send()

    for at_last, present in ((False, has_first), (True, has_last)):
        @pl.when(present)
        def _(at_last=at_last):
            row_sends(at_last).wait_send()

    note_copies(slots, 0, *note_sems[0], peer(1)).wait_send()

    return inner, curve, bend


def note_copies(slots, note, send, recv, device):
    return pltpu.make_async_remote_copy(
        src_ref=slots.at[note],
        dst_ref=slots.at[note],
        send_sem=send,
        recv_sem=recv,
        device_id=device,
        device_id_type=MESH,
    )


def gather(slots, notes, note, send, recv, device):
    note_copies(slots, note, send, recv, device).wait_recv()
    return jnp.sum(slots[note], axis=0, keepdims=True) + notes[note, 0:1, :]


def kernel(sizes, *refs):
    *refs, last_send, last_recv = refs
    pace, notes, slots = refs[8], refs[-2], refs[-1]
    obs = refs[9]
    chunks = obs.shape[1] // SUB
    groups = chunks // PAIR
    dma = pltpu.SemaphoreType.DMA

    def scope(*sems):
        return solve(sizes, *refs, *sems, last_send, last_recv)

    inner, curve, bend = pl.run_scoped(
        scope,
        dma((4 + 2 * groups,)),
        dma((4,)),
        dma((2, chunks)),
        dma((2, groups)),
        dma(()),
        dma((2,)),
        dma((2, 2)),
        dma(()),
        dma(()),
        pltpu.SemaphoreType.REGULAR,
    )
    years, rows, cols = (lax.axis_index(axis) for axis in ("year", "row", "col"))
    device = (years, rows, lax.rem(cols + 1, sizes[2]))
    final = gather(slots, notes, 1, last_send, last_recv, device)
    final = jnp.broadcast_to(jnp.sum(final, axis=1, keepdims=True), final.shape)
    pace[...] = jnp.broadcast_to(inner / (curve - bend * final), pace.shape)
    note_copies(slots, 1, last_send, last_recv, device).wait_send()


def store_kernel(anchor, slope, pace, new_params, residual, total, sem):
    count = total.shape[1]
    step = jnp.broadcast_to(pace[0:1, :], total.shape[1:])
    half = (count + 1) // 2
    copies = []
    for at, out in enumerate((new_params, residual)):
        for piece, (low, high) in enumerate(((0, half), (half, count))):
            where = pl.ds(low, high - low)
            total[at, where] = anchor[at, where] + step[low:high] * slope[at, where]
            copies.append(
                pltpu.make_async_copy(
                    total.at[at, where], out.at[0, where], sem.at[at, piece]
                )
            )
            copies[-1].start()
    for copy in copies:
        copy.wait()


def per_device(sizes, observed, quality, land_mask, params, spatial_weight, temporal_weight):
    n_year, n_row, n_col = sizes
    _, dates, rows, cols = observed.shape
    count = params.shape[1]
    chunks = rows // SUB
    groups = chunks // PAIR
    others = n_year * n_row * n_col - 1
    f32 = jnp.float32
    vmem = pl.BlockSpec(memory_space=pltpu.VMEM)
    hbm = pl.BlockSpec(memory_space=pltpu.HBM)
    dma = pltpu.SemaphoreType.DMA
    both = jax.ShapeDtypeStruct((2, count, rows, cols), f32)
    results = pl.pallas_call(
        functools.partial(kernel, sizes),
        out_shape=(both, both, jax.ShapeDtypeStruct((SUB, cols), f32)),
        in_specs=[hbm] * 6,
        out_specs=(vmem, vmem, vmem),
        scratch_shapes=[
            pltpu.VMEM((dates, rows, cols), f32),
            pltpu.VMEM((dates, rows, cols), jnp.int32),
            pltpu.VMEM((rows, cols), jnp.int32),
            pltpu.SMEM((count,), f32),
            pltpu.SMEM((count,), f32),
            pltpu.VMEM((ROUNDS, 5, count, rows + 2 * SUB, cols), f32),
            pltpu.VMEM((count * (count + 1) // 2, rows, cols), f32),
            pltpu.VMEM((ROUNDS, count, rows, cols), f32),
            pltpu.VMEM((SUB, cols), f32),
            pltpu.VMEM((2, SUB, cols), f32),
            pltpu.VMEM((2, max(others, 1), cols), f32),
            dma(()),
            dma(()),
        ],
        compiler_params=pltpu.CompilerParams(
            collective_id=0, has_side_effects=True, vmem_limit_bytes=24 * 2**20
        ),
        name="gauss_newton",
    )(
        *[
            pltpu.with_memory_space_constraint(operand, pltpu.HBM)
            for operand in (
                observed, quality, land_mask, params, spatial_weight, temporal_weight
            )
        ]
    )
    return pl.pallas_call(
        store_kernel,
        out_shape=(
            jax.ShapeDtypeStruct(params.shape, f32),
            jax.ShapeDtypeStruct(params.shape, f32),
        ),
        in_specs=[vmem, vmem, vmem],
        out_specs=(hbm, hbm),
        scratch_shapes=[pltpu.VMEM((2, count, rows, cols), f32), dma((2, 2))],
        compiler_params=pltpu.CompilerParams(vmem_limit_bytes=4 * 2**20),
        name="store",
    )(*results)


def solution(mesh):
    sizes = tuple(mesh.shape[axis] for axis in ("year", "row", "col"))
    grid = P("year", None, "row", "col")
    return jax.shard_map(
        functools.partial(per_device, sizes),
        mesh=mesh,
        in_specs=(grid, grid, P("row", "col"), grid, P(), P()),
        out_specs=(grid, grid),
        check_vma=False,
    )
```

```python
import functools

import jax
import jax.numpy as jnp
from jax import lax
from jax.experimental import pallas as pl
from jax.experimental.pallas import tpu as pltpu
from jax.sharding import PartitionSpec as P

ITERS = 4
ROUNDS = ITERS + 1
SUB = 8
LEAD = 2
PAIR = 2
LEVEL = (1, 3)
DAMPING = 0.1
MESH = pl.DeviceIdType.MESH


def pairs_of(count):
    return [(i, j) for i in range(count) for j in range(i, count)]


def solve(
    sizes,
    observed,
    quality,
    land_mask,
    params,
    spatial_weight,
    temporal_weight,
    anchor,
    slope,
    pace,
    obs,
    qual,
    land,
    spatial,
    temporal,
    field,
    inverse,
    resid,
    moments,
    notes,
    slots,
    load_sem,
    send_sem,
    year_recv,
    col_recv,
    rest_recv,
    row_send,
    row_recv,
    sum_send,
    sum_recv,
    level_sem,
    last_send,
    last_recv,
):
    n_year, n_row, n_col = sizes
    dates, rows, cols = obs.shape
    count = resid.shape[1]
    chunks = rows // SUB
    wide_rows = SUB * PAIR
    pairs = pairs_of(count)
    place = {pair: at for at, pair in enumerate(pairs)}

    year, row, col = lax.axis_index("year"), lax.axis_index("row"), lax.axis_index("col")
    even = lax.rem(row, 2) == 1

    has_prev, has_next = year > 0, year < n_year - 1
    has_left, has_right = col > 0, col < n_col - 1
    has_up, has_down = row > 0, row < n_row - 1
    has_first = jnp.logical_or(jnp.logical_and(even, has_up), jnp.logical_and(~even, has_down))
    has_last = jnp.logical_or(jnp.logical_and(even, has_down), jnp.logical_and(~even, has_up))
    toward_first = row + jnp.where(even, -1, 1)
    toward_last = row + jnp.where(even, 1, -1)

    def chunk_rows(position):
        chunk = jnp.where(even, position, chunks - 1 - position)
        return pl.multiple_of(chunk * SUB, SUB)

    def wide_start(group):
        group = jnp.where(even, group, chunks // PAIR - 1 - group)
        return pl.multiple_of(group * wide_rows, wide_rows)

    total_devices = n_year * n_row * n_col
    near = (n_year - 1) + (n_row - 1) <= ITERS

    def peer(other):
        spot = lax.rem((year * n_row + row) * n_col + col + other, total_devices)
        return (spot // (n_row * n_col), lax.rem(spot // n_col, n_row), lax.rem(spot, n_col))

    barrier = pltpu.get_barrier_semaphore()
    if near:
        for present, target in (
            (has_prev, (year - 1, row, col)),
            (has_next, (year + 1, row, col)),
            (has_up, (year, row - 1, col)),
            (has_down, (year, row + 1, col)),
        ):
            @pl.when(present)
            def _(target=target):
                pl.semaphore_signal(barrier, inc=1, device_id=target, device_id_type=MESH)

        for other in range(1, n_col):
            pl.semaphore_signal(
                barrier,
                inc=1,
                device_id=(year, row, lax.rem(col + other, n_col)),
                device_id_type=MESH,
            )
        expected = n_col - 1
        for present in (has_prev, has_next, has_up, has_down):
            expected = expected + present.astype(jnp.int32)
    else:
        for other in range(1, total_devices):
            pl.semaphore_signal(barrier, inc=1, device_id=peer(other), device_id_type=MESH)
        expected = total_devices - 1

    param_load = pltpu.make_async_copy(
        params.at[0], field.at[0, 0, :, pl.ds(SUB, rows), :], load_sem.at[0]
    )
    small_loads = (
        pltpu.make_async_copy(land_mask, land, load_sem.at[1]),
        pltpu.make_async_copy(spatial_weight, spatial, load_sem.at[2]),
        pltpu.make_async_copy(temporal_weight, temporal, load_sem.at[3]),
    )

    def input_loads(group):
        where = (slice(None), pl.ds(wide_start(group), wide_rows), slice(None))
        return (
            pltpu.make_async_copy(observed.at[0].at[where], obs.at[where], load_sem.at[4 + 2 * group]),
            pltpu.make_async_copy(quality.at[0].at[where], qual.at[where], load_sem.at[5 + 2 * group]),
        )

    param_load.start()
    for copy in small_loads:
        copy.start()
    for group in range(chunks // PAIR):
        for copy in input_loads(group):
            copy.start()

    pl.semaphore_wait(barrier, expected)

    sides = (
        (has_next, (year + 1, row, col), 1, has_prev),
        (has_prev, (year - 1, row, col), 2, has_next),
        (has_right, (year, row, col + 1), 3, has_left),
        (has_left, (year, row, col - 1), 4, has_right),
    )

    split = count // 2
    early = (pl.ds(0, split), pl.ds(split, count - split))

    def side_copy(step, position, side):
        _, target, slot, _ = sides[side]
        which = early[side] if side < 2 and step == ITERS else slice(None)
        if side < 2:
            where = pl.ds(chunk_rows(position) + SUB, SUB)
            landing = year_recv.at[step % 2, position]
        else:
            group = position // PAIR
            where = pl.ds(pl.multiple_of(wide_start(group) + SUB, SUB), wide_rows)
            landing = col_recv.at[step % 2, group]
        return pltpu.make_async_remote_copy(
            src_ref=field.at[step, 0, which, where, :],
            dst_ref=field.at[step, slot, which, where, :],
            send_sem=send_sem.at[side],
            recv_sem=landing,
            device_id=target,
            device_id_type=MESH,
        )

    def rest_copy(side, low=0, high=rows):
        _, target, slot, _ = sides[side]
        which, where = early[1 - side], pl.ds(SUB + low, high - low)
        return pltpu.make_async_remote_copy(
            src_ref=field.at[ITERS, 0, which, where, :],
            dst_ref=field.at[ITERS, slot, which, where, :],
            send_sem=send_sem.at[side],
            recv_sem=rest_recv,
            device_id=target,
            device_id_type=MESH,
        )

    def row_spot(last):
        top = jnp.logical_xor(even, last)
        source = pl.multiple_of(jnp.where(top, SUB, rows), SUB)
        target = pl.multiple_of(jnp.where(top, rows + SUB, 0), SUB)
        return source, target, (year, toward_last if last else toward_first, col)

    def row_copy(step, last):
        source, target, device = row_spot(last)
        return pltpu.make_async_remote_copy(
            src_ref=field.at[step, 0, :, pl.ds(source, SUB), :],
            dst_ref=field.at[step, 0, :, pl.ds(target, SUB), :],
            send_sem=row_send.at[int(last)],
            recv_sem=row_recv.at[step % 2, int(last)],
            device_id=device,
            device_id_type=MESH,
        )

    def side_sends(side):
        where = (slice(None), 0, slice(None), pl.ds(SUB, rows), slice(None))
        return pltpu.make_async_remote_copy(
            src_ref=field.at[where],
            dst_ref=field.at[where],
            send_sem=send_sem.at[side],
            recv_sem=send_sem.at[side],
            device_id=sides[side][1],
            device_id_type=MESH,
        )

    def row_sends(last):
        source, _, device = row_spot(last)
        where = (slice(None), 0, slice(None), pl.ds(source, SUB), slice(None))
        return pltpu.make_async_remote_copy(
            src_ref=field.at[where],
            dst_ref=field.at[where],
            send_sem=row_send.at[int(last)],
            recv_sem=row_send.at[int(last)],
            device_id=device,
            device_id_type=MESH,
        )

    def start_sends(step, position):
        for side in range(4):
            present = sides[side][0]
            if side >= 2:
                ready = lax.rem(position, PAIR) == PAIR - 1
                present = jnp.logical_and(present, ready)

            @pl.when(present)
            def _(side=side):
                side_copy(step, position, side).start()

    def wait_pair(first, second, left, right, both):
        @pl.when(jnp.logical_and(first, second))
        def _():
            both.wait_recv()

        @pl.when(jnp.logical_and(first, ~second))
        def _():
            left.wait_recv()

        @pl.when(jnp.logical_and(second, ~first))
        def _():
            right.wait_recv()

    def landing_of(place, semaphore):
        return pltpu.make_async_remote_copy(
            src_ref=place,
            dst_ref=place,
            send_sem=send_sem.at[0],
            recv_sem=semaphore,
            device_id=sides[0][1],
            device_id_type=MESH,
        )

    def wait_years(step, position):
        where = pl.ds(chunk_rows(position) + SUB, SUB)
        slots_here = pl.ds(1, 1 if step == ITERS else 2)
        both = landing_of(
            field.at[step, slots_here, :, where, :], year_recv.at[step % 2, position]
        )
        ends = [side_copy(step, position, side) for side in (0, 1)]
        wait_pair(has_prev, has_next, *ends, both)

    def wait_cols(step, position):
        group = position // PAIR
        where = pl.ds(pl.multiple_of(wide_start(group) + SUB, SUB), wide_rows)
        both = landing_of(
            field.at[step, pl.ds(3, 2), :, where, :], col_recv.at[step % 2, group]
        )
        ends = [side_copy(step, position, side) for side in (2, 3)]

        @pl.when(lax.rem(position, PAIR) == 0)
        def _():
            wait_pair(has_left, has_right, *ends, both)

    def wait_rest():
        both = landing_of(field.at[ITERS, 1, :, pl.ds(SUB, rows), :], rest_recv)
        wait_pair(has_prev, has_next, rest_copy(0), rest_copy(1), both)

    def close_edges(step, first, last):
        for flag, at_last, present in ((first, False, has_first), (last, True, has_last)):
            top = jnp.logical_xor(even, at_last)

            @pl.when(jnp.logical_and(flag, present))
            def _(at_last=at_last):
                row_copy(step, at_last).start()

            def repeat(source, edge, target):
                for p in range(count):
                    block = field[step, 0, p, source : source + SUB, :]
                    field[step, 0, p, target : target + SUB, :] = jnp.broadcast_to(
                        block[edge : edge + 1, :], (SUB, cols)
                    )

            @pl.when(jnp.logical_and(jnp.logical_and(flag, ~present), top))
            def _():
                repeat(SUB, 0, 0)

            @pl.when(jnp.logical_and(jnp.logical_and(flag, ~present), ~top))
            def _():
                repeat(rows, SUB - 1, rows + SUB)

    def wait_edges(step, first, last):
        for flag, at_last, present in ((first, False, has_first), (last, True, has_last)):
            @pl.when(jnp.logical_and(flag, present))
            def _(at_last=at_last):
                row_copy(step, at_last).wait_recv()

    param_load.wait()

    def send_params(position, carry):
        start_sends(0, position)
        return carry

    lax.fori_loop(0, chunks, send_params, 0)
    close_edges(0, True, True)

    prev_slot = jnp.where(has_prev, 1, 0)
    next_slot = jnp.where(has_next, 2, 0)
    left_slot = jnp.where(has_left, 3, 0)
    right_slot = jnp.where(has_right, 4, 0)
    lane = lax.broadcasted_iota(jnp.int32, (SUB, cols), 1)
    level = lax.broadcasted_iota(jnp.int32, (SUB, cols), 0)
    lane_first, lane_last = lane == 0, lane == cols - 1
    level_first, level_last = level == 0, level == SUB - 1
    grid_left = lane == jnp.where(has_left, -1, 0)
    grid_right = lane == jnp.where(has_right, -1, cols - 1)

    def plane_sum(step, p, start):
        own = pl.ds(start + SUB, SUB)
        here = field[step, 0, p, own, :]
        above = field[step, 0, p, pl.ds(start, SUB), :]
        below = field[step, 0, p, pl.ds(start + 2 * SUB, SUB), :]
        up = pltpu.roll(jnp.where(level_last, above, here), 1, 0)
        down = pltpu.roll(jnp.where(level_first, below, here), SUB - 1, 0)
        left = pltpu.roll(jnp.where(lane_last, field[step, left_slot, p, own, :], here), 1, 1)
        right = pltpu.roll(
            jnp.where(lane_first, field[step, right_slot, p, own, :], here), cols - 1, 1
        )
        left = jnp.where(grid_left, here, left)
        right = jnp.where(grid_right, here, right)
        return here, (up + down) + (left + right)

    def around(step, p, start):
        own = pl.ds(start + SUB, SUB)
        here, plane = plane_sum(step, p, start)
        yearly = field[step, prev_slot, p, own, :] + field[step, next_slot, p, own, :]
        return here, spatial[p] * plane + temporal[p] * yearly

    def precondition(start, values):
        rows_here = pl.ds(start, SUB)
        entry = [inverse[at, rows_here, :] for at in range(len(pairs))]
        outs = []
        for p in range(count):
            total = entry[place[(0, p)]] * values[0]
            for q in range(1, count):
                total = total + entry[place[(min(p, q), max(p, q))]] * values[q]
            outs.append(total)
        return outs

    def dot(left, right):
        terms = [a * b for a, b in zip(left, right)]
        while len(terms) > 1:
            terms = [sum(terms[i : i + 2][1:], terms[i]) for i in range(0, len(terms), 2)]
        return terms[0]

    def normal(start):
        here = pl.ds(start, SUB)
        base, peak, slope, rise_mid, rise_log, fall_mid, fall_log = [
            field[0, 0, p, pl.ds(start + SUB, SUB), :] for p in range(count)
        ]
        rise_rate, fall_rate = jnp.exp(rise_log), jnp.exp(fall_log)
        rise_half, fall_half = 0.5 * rise_rate, 0.5 * fall_rate

        def date_step(date, sums):
            time = date.astype(jnp.float32) * (1.0 / dates)
            flag = qual[date, here, :].astype(jnp.float32)
            weight = jnp.maximum(1.0 - 0.5 * flag, 0.0)
            rise_gap = time - rise_mid
            fall_gap = time - fall_mid
            rise = jnp.tanh(rise_half * rise_gap)
            fall = jnp.tanh(fall_half * fall_gap)
            season = rise - fall
            height = peak - slope * time
            rise_bell = height - height * (rise * rise)
            fall_bell = height - height * (fall * fall)
            basis = [
                None,
                season,
                time * season,
                rise_bell,
                rise_gap * rise_bell,
                fall_bell,
                fall_gap * fall_bell,
            ]
            weighted = [weight] + [weight * item for item in basis[1:]]
            out = []
            for i, j in pairs:
                term = weighted[j] if i == 0 else basis[i] * weighted[j]
                out.append(sums[place[(i, j)]] + term)
            seen = obs[date, here, :]
            for i in range(count):
                out.append(sums[len(pairs) + i] + seen * weighted[i])
            return tuple(out)

        zero = jnp.zeros((SUB, cols), jnp.float32)
        sums = lax.fori_loop(
            0, dates, date_step, (zero,) * (len(pairs) + count), unroll=dates
        )
        share = land[here, :].astype(jnp.float32) * (1.0 / dates)
        rise_scale, fall_scale = 0.25 * rise_rate, 0.25 * fall_rate
        scale = [None, 0.5, -0.5, -rise_scale, rise_scale, fall_scale, -fall_scale]
        shared = [share] + [share * item for item in scale[1:]]
        block = {}
        for i, j in pairs:
            factor = shared[j] if i == 0 else shared[j] * scale[i]
            block[(i, j)] = sums[place[(i, j)]] * factor
        for p in range(count):
            total = shared[p] * sums[len(pairs) + p]
            for q, value in ((0, base), (1, peak), (2, slope)):
                total = total - block[(min(p, q), max(p, q))] * value
            resid[0, p, here, :] = total
        for p in range(count):
            block[(p, p)] = block[(p, p)] + (DAMPING + 4.0 * spatial[p] + 2.0 * temporal[p])
        for k in range(count):
            turn = 1.0 / block[(k, k)]
            edge = {i: block[(min(i, k), max(i, k))] for i in range(count) if i != k}
            lean = {i: edge[i] * turn for i in edge}
            for i, j in pairs:
                if i != k and j != k:
                    block[(i, j)] = block[(i, j)] - edge[i] * lean[j]
            for i in edge:
                block[(min(i, k), max(i, k))] = lean[i]
            block[(k, k)] = -turn
        for pair in pairs:
            inverse[place[pair], here, :] = -block[pair]

    zero = jnp.zeros((SUB, cols), jnp.float32)

    def walk(position):
        return chunk_rows(position), position == 0, position == chunks - 1

    def make_stage(stage):
        def body(position, carry):
            odd_sum, even_sum = carry
            start, first, last = walk(position)
            wait_cols(stage, position)
            wait_years(stage, position)
            wait_edges(stage, first, last)
            rows_here = pl.ds(start, SUB)
            held, pushed = [], []
            for p in range(count):
                here, push = around(stage, p, start)
                if stage == 0:
                    push = (resid[0, p, rows_here, :] + push) - (
                        4.0 * spatial[p] + 2.0 * temporal[p]
                    ) * here
                resid[stage, p, rows_here, :] = push
                held.append(here)
                pushed.append(push)
            if stage > 0:
                odd_sum = odd_sum + dot(held, pushed)
            turned = precondition(start, pushed)
            for p in range(count):
                field[stage + 1, 0, p, pl.ds(start + SUB, SUB), :] = turned[p]
            even_sum = even_sum + dot(turned, pushed)
            start_sends(stage + 1, position)
            close_edges(stage + 1, first, last)
            return odd_sum, even_sum

        return body

    def keep_level():
        if n_col % 2 == 0:
            partner = col + 1 - 2 * lax.rem(col, 2)
            pl.semaphore_signal(
                level_sem, inc=1, device_id=(year, row, partner), device_id_type=MESH
            )
            pl.semaphore_wait(level_sem, 1)

    for copy in small_loads:
        copy.wait()

    first_stage = make_stage(0)

    def opening(position, carry):
        @pl.when(position < chunks)
        def _():
            @pl.when(lax.rem(position, PAIR) == 0)
            def _():
                for copy in input_loads(position // PAIR):
                    copy.wait()

            normal(chunk_rows(position))

        return lax.cond(
            position >= LEAD, lambda c: first_stage(position - LEAD, c), lambda c: c, carry
        )

    sums = []
    for stage in range(ITERS):
        if stage == 0:
            odd_sum, even_sum = lax.fori_loop(0, chunks + LEAD, opening, (zero, zero))
        else:
            if stage in LEVEL:
                keep_level()
            odd_sum, even_sum = lax.fori_loop(0, chunks, make_stage(stage), (zero, zero))
            sums.append(odd_sum)
        sums.append(even_sum)

    others = total_devices - 1

    note_sems = ((sum_send, sum_recv), (last_send, last_recv))

    def sum_copy(note, other):
        return pltpu.make_async_remote_copy(
            src_ref=notes.at[note, pl.ds(0, 1)],
            dst_ref=slots.at[note, pl.ds(other - 1, 1)],
            send_sem=note_sems[note][0],
            recv_sem=note_sems[note][1],
            device_id=peer(other),
            device_id_type=MESH,
        )

    def start_rest(low, high):
        for side in range(2):
            @pl.when(sides[side][0])
            def _(side=side):
                rest_copy(side, low, high).start()

    cut, tail = rows // 2 // SUB * SUB, 3 * rows // 8 // SUB * SUB
    start_rest(0, cut)

    for at, value in enumerate(sums):
        moments[at : at + 1, :] = jnp.sum(value, axis=0, keepdims=True)
    moments[len(sums) : SUB, :] = jnp.zeros((SUB - len(sums), cols), jnp.float32)
    folded = jnp.broadcast_to(jnp.sum(moments[...], axis=1, keepdims=True), (SUB, cols))
    notes[0, 0:1, :] = jnp.sum(jnp.where(lane == level, folded, 0.0), axis=0, keepdims=True)
    for other in range(1, total_devices):
        sum_copy(0, other).start()

    start_rest(cut, rows - tail)

    def factors(near_side, far_side):
        return jnp.where(near_side, 2.0, 1.0), jnp.where(far_side, 0.0, 1.0)

    first_edge = [(prev_slot, *factors(has_prev, has_next))] * split
    first_edge += [(next_slot, *factors(has_next, has_prev))] * (count - split)
    other_slot = [next_slot] * split + [prev_slot] * (count - split)

    def closing(position, last_sum):
        start, first, last = walk(position)
        rows_here, padded = pl.ds(start, SUB), pl.ds(start + SUB, SUB)
        wait_cols(ITERS, position)
        wait_edges(ITERS, first, last)
        held, pushed, planes = [], [], []
        for p in range(count):
            here, plane = plane_sum(ITERS, p, start)
            plane = spatial[p] * plane
            planes.append(plane)
            held.append(here)
            pushed.append(plane + (temporal[p] * first_edge[p][2]) * here)
        last_sum = last_sum + dot(held, pushed)
        wait_years(ITERS, position)
        pushed = []
        for p in range(count):
            slot, twice, _ = first_edge[p]
            beside = temporal[p] * field[ITERS, slot, p, padded, :]
            resid[ITERS, p, rows_here, :] = planes[p] + beside
            pushed.append(twice * beside)
        return last_sum + dot(held, pushed)

    last_sum = lax.fori_loop(0, chunks, closing, zero)
    notes[1, 0:1, :] = jnp.sum(last_sum, axis=0, keepdims=True)
    for other in range(1, total_devices):
        sum_copy(1, other).start()
    start_rest(rows - tail, rows)

    known = gather(slots, notes, 0, *note_sems[0], peer(1))
    known = jnp.where(lane == level, jnp.broadcast_to(known, (SUB, cols)), 0.0)
    known = jnp.broadcast_to(jnp.sum(known, axis=1, keepdims=True), (SUB, cols))
    mu = [known[at : at + 1, :] for at in range(2 * ITERS - 1)]
    drop = [mu[at] - mu[at + 1] for at in range(2 * ITERS - 2)]

    def form(coefs, table):
        total = None
        for i, left in enumerate(coefs):
            for j in range(i, len(coefs)):
                term = left * coefs[j] * table[i + j]
                term = term if i == j else 2.0 * term
                total = term if total is None else total + term
        return total

    one = jnp.ones_like(mu[0])
    search, direction = [one], [one]
    lengths = [jnp.zeros_like(one)] * ITERS
    inner = mu[0]
    for sweep in range(ITERS - 1):
        alpha = inner / form(direction, drop)
        for j in range(sweep + 1):
            lengths[j] = lengths[j] + alpha * direction[j]
        grown = []
        for j in range(sweep + 2):
            change = None
            if j <= sweep:
                change = direction[j]
            if j > 0:
                change = -direction[j - 1] if change is None else change - direction[j - 1]
            base = search[j] if j <= sweep else None
            grown.append(-alpha * change if base is None else base - alpha * change)
        search = grown
        fresh = form(search, mu)
        ratio = fresh / inner
        inner = fresh
        direction = [
            search[j] + ratio * direction[j] if j <= sweep else search[j]
            for j in range(sweep + 2)
        ]
    curve = form(direction, drop + [mu[-1]])
    bend = direction[-1] * direction[-1]

    def wide(values):
        return [jnp.broadcast_to(value, (SUB, cols)) for value in values]

    def mixes(values, head):
        return wide(
            [head - values[0]]
            + [values[j - 1] - values[j] for j in range(1, ITERS)]
            + [values[-1]]
        )

    paces, steers = wide(lengths[:-1]), wide(direction)
    base_mix, slope_mix = mixes(lengths, 1.0)[:-1], mixes(direction, 0.0)

    def prepare(position, carry):
        start, _, _ = walk(position)
        rows_here, padded = pl.ds(start, SUB), pl.ds(start + SUB, SUB)
        for p in range(count):
            vectors = [field[j + 1, 0, p, padded, :] for j in range(ITERS)]
            total = field[0, 0, p, padded, :]
            for pace, vector in zip(paces, vectors):
                total = total + pace * vector
            anchor[0, p, rows_here, :] = total
            total = steers[0] * vectors[0]
            for steer, vector in zip(steers[1:], vectors[1:]):
                total = total + steer * vector
            slope[0, p, rows_here, :] = total
            vectors = [resid[j, p, rows_here, :] for j in range(ITERS + 1)]
            vectors[-1] = vectors[-1] + temporal[p] * field[ITERS, other_slot[p], p, padded, :]
            total = base_mix[0] * vectors[0]
            for mix, vector in zip(base_mix[1:], vectors[1:]):
                total = total + mix * vector
            anchor[1, p, rows_here, :] = total
            total = slope_mix[0] * vectors[0]
            for mix, vector in zip(slope_mix[1:], vectors[1:]):
                total = total + mix * vector
            slope[1, p, rows_here, :] = total
        return carry

    wait_rest()
    lax.fori_loop(0, chunks, prepare, 0)

    for side in range(4):
        @pl.when(sides[side][0])
        def _(side=side):
            side_sends(side).wait_send()

    for at_last, present in ((False, has_first), (True, has_last)):
        @pl.when(present)
        def _(at_last=at_last):
            row_sends(at_last).wait_send()

    note_copies(slots, 0, *note_sems[0], peer(1)).wait_send()

    return inner, curve, bend


def note_copies(slots, note, send, recv, device):
    return pltpu.make_async_remote_copy(
        src_ref=slots.at[note],
        dst_ref=slots.at[note],
        send_sem=send,
        recv_sem=recv,
        device_id=device,
        device_id_type=MESH,
    )


def gather(slots, notes, note, send, recv, device):
    note_copies(slots, note, send, recv, device).wait_recv()
    return jnp.sum(slots[note], axis=0, keepdims=True) + notes[note, 0:1, :]


def kernel(sizes, *refs):
    *refs, last_send, last_recv = refs
    pace, notes, slots = refs[8], refs[-2], refs[-1]
    obs = refs[9]
    chunks = obs.shape[1] // SUB
    groups = chunks // PAIR
    dma = pltpu.SemaphoreType.DMA

    def scope(*sems):
        return solve(sizes, *refs, *sems, last_send, last_recv)

    inner, curve, bend = pl.run_scoped(
        scope,
        dma((4 + 2 * groups,)),
        dma((4,)),
        dma((2, chunks)),
        dma((2, groups)),
        dma(()),
        dma((2,)),
        dma((2, 2)),
        dma(()),
        dma(()),
        pltpu.SemaphoreType.REGULAR,
    )
    years, rows, cols = (lax.axis_index(axis) for axis in ("year", "row", "col"))
    device = (years, rows, lax.rem(cols + 1, sizes[2]))
    final = gather(slots, notes, 1, last_send, last_recv, device)
    final = jnp.broadcast_to(jnp.sum(final, axis=1, keepdims=True), final.shape)
    pace[...] = jnp.broadcast_to(inner / (curve - bend * final), pace.shape)
    note_copies(slots, 1, last_send, last_recv, device).wait_send()


def store_kernel(anchor, slope, pace, new_params, residual, total, sem):
    count = total.shape[1]
    step = jnp.broadcast_to(pace[0:1, :], total.shape[1:])
    half = (count + 1) // 2
    copies = []
    for at, out in enumerate((new_params, residual)):
        for piece, (low, high) in enumerate(((0, half), (half, count))):
            where = pl.ds(low, high - low)
            total[at, where] = anchor[at, where] + step[low:high] * slope[at, where]
            copies.append(
                pltpu.make_async_copy(
                    total.at[at, where], out.at[0, where], sem.at[at, piece]
                )
            )
            copies[-1].start()
    for copy in copies:
        copy.wait()


def per_device(sizes, observed, quality, land_mask, params, spatial_weight, temporal_weight):
    n_year, n_row, n_col = sizes
    _, dates, rows, cols = observed.shape
    count = params.shape[1]
    chunks = rows // SUB
    groups = chunks // PAIR
    others = n_year * n_row * n_col - 1
    f32 = jnp.float32
    vmem = pl.BlockSpec(memory_space=pltpu.VMEM)
    hbm = pl.BlockSpec(memory_space=pltpu.HBM)
    dma = pltpu.SemaphoreType.DMA
    both = jax.ShapeDtypeStruct((2, count, rows, cols), f32)
    results = pl.pallas_call(
        functools.partial(kernel, sizes),
        out_shape=(both, both, jax.ShapeDtypeStruct((SUB, cols), f32)),
        in_specs=[hbm] * 6,
        out_specs=(vmem, vmem, vmem),
        scratch_shapes=[
            pltpu.VMEM((dates, rows, cols), f32),
            pltpu.VMEM((dates, rows, cols), jnp.int32),
            pltpu.VMEM((rows, cols), jnp.int32),
            pltpu.SMEM((count,), f32),
            pltpu.SMEM((count,), f32),
            pltpu.VMEM((ROUNDS, 5, count, rows + 2 * SUB, cols), f32),
            pltpu.VMEM((count * (count + 1) // 2, rows, cols), f32),
            pltpu.VMEM((ROUNDS, count, rows, cols), f32),
            pltpu.VMEM((SUB, cols), f32),
            pltpu.VMEM((2, SUB, cols), f32),
            pltpu.VMEM((2, max(others, 1), cols), f32),
            dma(()),
            dma(()),
        ],
        compiler_params=pltpu.CompilerParams(
            collective_id=0, has_side_effects=True, vmem_limit_bytes=24 * 2**20
        ),
        name="gauss_newton",
    )(
        *[
            pltpu.with_memory_space_constraint(operand, pltpu.HBM)
            for operand in (
                observed, quality, land_mask, params, spatial_weight, temporal_weight
            )
        ]
    )
    return pl.pallas_call(
        store_kernel,
        out_shape=(
            jax.ShapeDtypeStruct(params.shape, f32),
            jax.ShapeDtypeStruct(params.shape, f32),
        ),
        in_specs=[vmem, vmem, vmem],
        out_specs=(hbm, hbm),
        scratch_shapes=[pltpu.VMEM((2, count, rows, cols), f32), dma((2, 2))],
        compiler_params=pltpu.CompilerParams(vmem_limit_bytes=4 * 2**20),
        name="store",
    )(*results)


def solution(mesh):
    sizes = tuple(mesh.shape[axis] for axis in ("year", "row", "col"))
    grid = P("year", None, "row", "col")
    return jax.shard_map(
        functools.partial(per_device, sizes),
        mesh=mesh,
        in_specs=(grid, grid, P("row", "col"), grid, P(), P()),
        out_specs=(grid, grid),
        check_vma=False,
    )
```

```python
import functools

import jax
import jax.numpy as jnp
from jax import lax
from jax.experimental import pallas as pl
from jax.experimental.pallas import tpu as pltpu
from jax.sharding import PartitionSpec as P

ITERS = 4
ROUNDS = ITERS + 1
SUB = 8
LEAD = 2
PAIR = 2
LEVEL = (1, 3)
DAMPING = 0.1
MESH = pl.DeviceIdType.MESH


def pairs_of(count):
    return [(i, j) for i in range(count) for j in range(i, count)]


def solve(
    sizes,
    observed,
    quality,
    land_mask,
    params,
    spatial_weight,
    temporal_weight,
    anchor,
    slope,
    pace,
    obs,
    qual,
    land,
    spatial,
    temporal,
    field,
    inverse,
    resid,
    moments,
    notes,
    slots,
    load_sem,
    send_sem,
    year_recv,
    col_recv,
    rest_recv,
    row_send,
    row_recv,
    sum_send,
    sum_recv,
    level_sem,
    last_send,
    last_recv,
):
    n_year, n_row, n_col = sizes
    dates, rows, cols = obs.shape
    count = resid.shape[1]
    chunks = rows // SUB
    wide_rows = SUB * PAIR
    pairs = pairs_of(count)
    place = {pair: at for at, pair in enumerate(pairs)}

    year, row, col = lax.axis_index("year"), lax.axis_index("row"), lax.axis_index("col")
    even = lax.rem(row, 2) == 1

    has_prev, has_next = year > 0, year < n_year - 1
    has_left, has_right = col > 0, col < n_col - 1
    has_up, has_down = row > 0, row < n_row - 1
    has_first = jnp.logical_or(jnp.logical_and(even, has_up), jnp.logical_and(~even, has_down))
    has_last = jnp.logical_or(jnp.logical_and(even, has_down), jnp.logical_and(~even, has_up))
    toward_first = row + jnp.where(even, -1, 1)
    toward_last = row + jnp.where(even, 1, -1)

    def chunk_rows(position):
        chunk = jnp.where(even, position, chunks - 1 - position)
        return pl.multiple_of(chunk * SUB, SUB)

    def wide_start(group):
        group = jnp.where(even, group, chunks // PAIR - 1 - group)
        return pl.multiple_of(group * wide_rows, wide_rows)

    total_devices = n_year * n_row * n_col
    near = (n_year - 1) + (n_row - 1) <= ITERS

    def peer(other):
        spot = lax.rem((year * n_row + row) * n_col + col + other, total_devices)
        return (spot // (n_row * n_col), lax.rem(spot // n_col, n_row), lax.rem(spot, n_col))

    barrier = pltpu.get_barrier_semaphore()
    if near:
        for present, target in (
            (has_prev, (year - 1, row, col)),
            (has_next, (year + 1, row, col)),
            (has_up, (year, row - 1, col)),
            (has_down, (year, row + 1, col)),
        ):
            @pl.when(present)
            def _(target=target):
                pl.semaphore_signal(barrier, inc=1, device_id=target, device_id_type=MESH)

        for other in range(1, n_col):
            pl.semaphore_signal(
                barrier,
                inc=1,
                device_id=(year, row, lax.rem(col + other, n_col)),
                device_id_type=MESH,
            )
        expected = n_col - 1
        for present in (has_prev, has_next, has_up, has_down):
            expected = expected + present.astype(jnp.int32)
    else:
        for other in range(1, total_devices):
            pl.semaphore_signal(barrier, inc=1, device_id=peer(other), device_id_type=MESH)
        expected = total_devices - 1

    param_load = pltpu.make_async_copy(
        params.at[0], field.at[0, 0, :, pl.ds(SUB, rows), :], load_sem.at[0]
    )
    small_loads = (
        pltpu.make_async_copy(land_mask, land, load_sem.at[1]),
        pltpu.make_async_copy(spatial_weight, spatial, load_sem.at[2]),
        pltpu.make_async_copy(temporal_weight, temporal, load_sem.at[3]),
    )

    def input_loads(group):
        where = (slice(None), pl.ds(wide_start(group), wide_rows), slice(None))
        return (
            pltpu.make_async_copy(observed.at[0].at[where], obs.at[where], load_sem.at[4 + 2 * group]),
            pltpu.make_async_copy(quality.at[0].at[where], qual.at[where], load_sem.at[5 + 2 * group]),
        )

    param_load.start()
    for copy in small_loads:
        copy.start()
    for group in range(chunks // PAIR):
        for copy in input_loads(group):
            copy.start()

    pl.semaphore_wait(barrier, expected)

    sides = (
        (has_next, (year + 1, row, col), 1, has_prev),
        (has_prev, (year - 1, row, col), 2, has_next),
        (has_right, (year, row, col + 1), 3, has_left),
        (has_left, (year, row, col - 1), 4, has_right),
    )

    split = count // 2
    early = (pl.ds(0, split), pl.ds(split, count - split))

    def side_copy(step, position, side):
        _, target, slot, _ = sides[side]
        which = early[side] if side < 2 and step == ITERS else slice(None)
        if side < 2:
            where = pl.ds(chunk_rows(position) + SUB, SUB)
            landing = year_recv.at[step % 2, position]
        else:
            group = position // PAIR
            where = pl.ds(pl.multiple_of(wide_start(group) + SUB, SUB), wide_rows)
            landing = col_recv.at[step % 2, group]
        return pltpu.make_async_remote_copy(
            src_ref=field.at[step, 0, which, where, :],
            dst_ref=field.at[step, slot, which, where, :],
            send_sem=send_sem.at[side],
            recv_sem=landing,
            device_id=target,
            device_id_type=MESH,
        )

    def rest_copy(side, low=0, high=rows):
        _, target, slot, _ = sides[side]
        which, where = early[1 - side], pl.ds(SUB + low, high - low)
        return pltpu.make_async_remote_copy(
            src_ref=field.at[ITERS, 0, which, where, :],
            dst_ref=field.at[ITERS, slot, which, where, :],
            send_sem=send_sem.at[side],
            recv_sem=rest_recv,
            device_id=target,
            device_id_type=MESH,
        )

    def row_spot(last):
        top = jnp.logical_xor(even, last)
        source = pl.multiple_of(jnp.where(top, SUB, rows), SUB)
        target = pl.multiple_of(jnp.where(top, rows + SUB, 0), SUB)
        return source, target, (year, toward_last if last else toward_first, col)

    def row_copy(step, last):
        source, target, device = row_spot(last)
        return pltpu.make_async_remote_copy(
            src_ref=field.at[step, 0, :, pl.ds(source, SUB), :],
            dst_ref=field.at[step, 0, :, pl.ds(target, SUB), :],
            send_sem=row_send.at[int(last)],
            recv_sem=row_recv.at[step % 2, int(last)],
            device_id=device,
            device_id_type=MESH,
        )

    def side_sends(side):
        where = (slice(None), 0, slice(None), pl.ds(SUB, rows), slice(None))
        return pltpu.make_async_remote_copy(
            src_ref=field.at[where],
            dst_ref=field.at[where],
            send_sem=send_sem.at[side],
            recv_sem=send_sem.at[side],
            device_id=sides[side][1],
            device_id_type=MESH,
        )

    def row_sends(last):
        source, _, device = row_spot(last)
        where = (slice(None), 0, slice(None), pl.ds(source, SUB), slice(None))
        return pltpu.make_async_remote_copy(
            src_ref=field.at[where],
            dst_ref=field.at[where],
            send_sem=row_send.at[int(last)],
            recv_sem=row_send.at[int(last)],
            device_id=device,
            device_id_type=MESH,
        )

    def start_sends(step, position):
        for side in range(4):
            present = sides[side][0]
            if side >= 2:
                ready = lax.rem(position, PAIR) == PAIR - 1
                present = jnp.logical_and(present, ready)

            @pl.when(present)
            def _(side=side):
                side_copy(step, position, side).start()

    def wait_pair(first, second, left, right, both):
        @pl.when(jnp.logical_and(first, second))
        def _():
            both.wait_recv()

        @pl.when(jnp.logical_and(first, ~second))
        def _():
            left.wait_recv()

        @pl.when(jnp.logical_and(second, ~first))
        def _():
            right.wait_recv()

    def landing_of(place, semaphore):
        return pltpu.make_async_remote_copy(
            src_ref=place,
            dst_ref=place,
            send_sem=send_sem.at[0],
            recv_sem=semaphore,
            device_id=sides[0][1],
            device_id_type=MESH,
        )

    def wait_years(step, position):
        where = pl.ds(chunk_rows(position) + SUB, SUB)
        slots_here = pl.ds(1, 1 if step == ITERS else 2)
        both = landing_of(
            field.at[step, slots_here, :, where, :], year_recv.at[step % 2, position]
        )
        ends = [side_copy(step, position, side) for side in (0, 1)]
        wait_pair(has_prev, has_next, *ends, both)

    def wait_cols(step, position):
        group = position // PAIR
        where = pl.ds(pl.multiple_of(wide_start(group) + SUB, SUB), wide_rows)
        both = landing_of(
            field.at[step, pl.ds(3, 2), :, where, :], col_recv.at[step % 2, group]
        )
        ends = [side_copy(step, position, side) for side in (2, 3)]

        @pl.when(lax.rem(position, PAIR) == 0)
        def _():
            wait_pair(has_left, has_right, *ends, both)

    def wait_rest():
        both = landing_of(field.at[ITERS, 1, :, pl.ds(SUB, rows), :], rest_recv)
        wait_pair(has_prev, has_next, rest_copy(0), rest_copy(1), both)

    def close_edges(step, first, last):
        for flag, at_last, present in ((first, False, has_first), (last, True, has_last)):
            top = jnp.logical_xor(even, at_last)

            @pl.when(jnp.logical_and(flag, present))
            def _(at_last=at_last):
                row_copy(step, at_last).start()

            def repeat(source, edge, target):
                for p in range(count):
                    block = field[step, 0, p, source : source + SUB, :]
                    field[step, 0, p, target : target + SUB, :] = jnp.broadcast_to(
                        block[edge : edge + 1, :], (SUB, cols)
                    )

            @pl.when(jnp.logical_and(jnp.logical_and(flag, ~present), top))
            def _():
                repeat(SUB, 0, 0)

            @pl.when(jnp.logical_and(jnp.logical_and(flag, ~present), ~top))
            def _():
                repeat(rows, SUB - 1, rows + SUB)

    def wait_edges(step, first, last):
        for flag, at_last, present in ((first, False, has_first), (last, True, has_last)):
            @pl.when(jnp.logical_and(flag, present))
            def _(at_last=at_last):
                row_copy(step, at_last).wait_recv()

    param_load.wait()

    def send_params(position, carry):
        start_sends(0, position)
        return carry

    lax.fori_loop(0, chunks, send_params, 0)
    close_edges(0, True, True)

    prev_slot = jnp.where(has_prev, 1, 0)
    next_slot = jnp.where(has_next, 2, 0)
    left_slot = jnp.where(has_left, 3, 0)
    right_slot = jnp.where(has_right, 4, 0)
    lane = lax.broadcasted_iota(jnp.int32, (SUB, cols), 1)
    level = lax.broadcasted_iota(jnp.int32, (SUB, cols), 0)
    lane_first, lane_last = lane == 0, lane == cols - 1
    level_first, level_last = level == 0, level == SUB - 1
    grid_left = lane == jnp.where(has_left, -1, 0)
    grid_right = lane == jnp.where(has_right, -1, cols - 1)

    def plane_sum(step, p, start):
        own = pl.ds(start + SUB, SUB)
        here = field[step, 0, p, own, :]
        above = field[step, 0, p, pl.ds(start, SUB), :]
        below = field[step, 0, p, pl.ds(start + 2 * SUB, SUB), :]
        up = pltpu.roll(jnp.where(level_last, above, here), 1, 0)
        down = pltpu.roll(jnp.where(level_first, below, here), SUB - 1, 0)
        left = pltpu.roll(jnp.where(lane_last, field[step, left_slot, p, own, :], here), 1, 1)
        right = pltpu.roll(
            jnp.where(lane_first, field[step, right_slot, p, own, :], here), cols - 1, 1
        )
        left = jnp.where(grid_left, here, left)
        right = jnp.where(grid_right, here, right)
        return here, (up + down) + (left + right)

    def around(step, p, start):
        own = pl.ds(start + SUB, SUB)
        here, plane = plane_sum(step, p, start)
        yearly = field[step, prev_slot, p, own, :] + field[step, next_slot, p, own, :]
        return here, spatial[p] * plane + temporal[p] * yearly

    def precondition(start, values):
        rows_here = pl.ds(start, SUB)
        entry = [inverse[at, rows_here, :] for at in range(len(pairs))]
        outs = []
        for p in range(count):
            total = entry[place[(0, p)]] * values[0]
            for q in range(1, count):
                total = total + entry[place[(min(p, q), max(p, q))]] * values[q]
            outs.append(total)
        return outs

    def dot(left, right):
        terms = [a * b for a, b in zip(left, right)]
        while len(terms) > 1:
            terms = [sum(terms[i : i + 2][1:], terms[i]) for i in range(0, len(terms), 2)]
        return terms[0]

    def normal(start):
        here = pl.ds(start, SUB)
        base, peak, slope, rise_mid, rise_log, fall_mid, fall_log = [
            field[0, 0, p, pl.ds(start + SUB, SUB), :] for p in range(count)
        ]
        rise_rate, fall_rate = jnp.exp(rise_log), jnp.exp(fall_log)
        rise_half, fall_half = 0.5 * rise_rate, 0.5 * fall_rate

        def date_step(date, sums):
            time = date.astype(jnp.float32) * (1.0 / dates)
            flag = qual[date, here, :].astype(jnp.float32)
            weight = jnp.maximum(1.0 - 0.5 * flag, 0.0)
            rise_gap = time - rise_mid
            fall_gap = time - fall_mid
            rise = jnp.tanh(rise_half * rise_gap)
            fall = jnp.tanh(fall_half * fall_gap)
            season = rise - fall
            height = peak - slope * time
            rise_bell = height - height * (rise * rise)
            fall_bell = height - height * (fall * fall)
            basis = [
                None,
                season,
                time * season,
                rise_bell,
                rise_gap * rise_bell,
                fall_bell,
                fall_gap * fall_bell,
            ]
            weighted = [weight] + [weight * item for item in basis[1:]]
            out = []
            for i, j in pairs:
                term = weighted[j] if i == 0 else basis[i] * weighted[j]
                out.append(sums[place[(i, j)]] + term)
            seen = obs[date, here, :]
            for i in range(count):
                out.append(sums[len(pairs) + i] + seen * weighted[i])
            return tuple(out)

        zero = jnp.zeros((SUB, cols), jnp.float32)
        sums = lax.fori_loop(
            0, dates, date_step, (zero,) * (len(pairs) + count), unroll=dates
        )
        share = land[here, :].astype(jnp.float32) * (1.0 / dates)
        rise_scale, fall_scale = 0.25 * rise_rate, 0.25 * fall_rate
        scale = [None, 0.5, -0.5, -rise_scale, rise_scale, fall_scale, -fall_scale]
        shared = [share] + [share * item for item in scale[1:]]
        block = {}
        for i, j in pairs:
            factor = shared[j] if i == 0 else shared[j] * scale[i]
            block[(i, j)] = sums[place[(i, j)]] * factor
        for p in range(count):
            total = shared[p] * sums[len(pairs) + p]
            for q, value in ((0, base), (1, peak), (2, slope)):
                total = total - block[(min(p, q), max(p, q))] * value
            resid[0, p, here, :] = total
        for p in range(count):
            block[(p, p)] = block[(p, p)] + (DAMPING + 4.0 * spatial[p] + 2.0 * temporal[p])
        for k in range(count):
            turn = 1.0 / block[(k, k)]
            edge = {i: block[(min(i, k), max(i, k))] for i in range(count) if i != k}
            lean = {i: edge[i] * turn for i in edge}
            for i, j in pairs:
                if i != k and j != k:
                    block[(i, j)] = block[(i, j)] - edge[i] * lean[j]
            for i in edge:
                block[(min(i, k), max(i, k))] = lean[i]
            block[(k, k)] = -turn
        for pair in pairs:
            inverse[place[pair], here, :] = -block[pair]

    zero = jnp.zeros((SUB, cols), jnp.float32)

    def walk(position):
        return chunk_rows(position), position == 0, position == chunks - 1

    def make_stage(stage):
        def body(position, carry):
            odd_sum, even_sum = carry
            start, first, last = walk(position)
            wait_cols(stage, position)
            wait_years(stage, position)
            wait_edges(stage, first, last)
            rows_here = pl.ds(start, SUB)
            held, pushed = [], []
            for p in range(count):
                here, push = around(stage, p, start)
                if stage == 0:
                    push = (resid[0, p, rows_here, :] + push) - (
                        4.0 * spatial[p] + 2.0 * temporal[p]
                    ) * here
                resid[stage, p, rows_here, :] = push
                held.append(here)
                pushed.append(push)
            if stage > 0:
                odd_sum = odd_sum + dot(held, pushed)
            turned = precondition(start, pushed)
            for p in range(count):
                field[stage + 1, 0, p, pl.ds(start + SUB, SUB), :] = turned[p]
            even_sum = even_sum + dot(turned, pushed)
            start_sends(stage + 1, position)
            close_edges(stage + 1, first, last)
            return odd_sum, even_sum

        return body

    def keep_level():
        if n_col % 2 == 0:
            partner = col + 1 - 2 * lax.rem(col, 2)
            pl.semaphore_signal(
                level_sem, inc=1, device_id=(year, row, partner), device_id_type=MESH
            )
            pl.semaphore_wait(level_sem, 1)

    for copy in small_loads:
        copy.wait()

    first_stage = make_stage(0)

    def opening(position, carry):
        @pl.when(position < chunks)
        def _():
            @pl.when(lax.rem(position, PAIR) == 0)
            def _():
                for copy in input_loads(position // PAIR):
                    copy.wait()

            normal(chunk_rows(position))

        return lax.cond(
            position >= LEAD, lambda c: first_stage(position - LEAD, c), lambda c: c, carry
        )

    sums = []
    for stage in range(ITERS):
        if stage == 0:
            odd_sum, even_sum = lax.fori_loop(0, chunks + LEAD, opening, (zero, zero))
        else:
            if stage in LEVEL:
                keep_level()
            odd_sum, even_sum = lax.fori_loop(0, chunks, make_stage(stage), (zero, zero))
            sums.append(odd_sum)
        sums.append(even_sum)

    others = total_devices - 1

    note_sems = ((sum_send, sum_recv), (last_send, last_recv))

    me = (year * n_row + row) * n_col + col

    def sum_copy(note, turn):
        below = (turn < me).astype(jnp.int32)
        target = turn + 1 - below
        landing = me - below
        return pltpu.make_async_remote_copy(
            src_ref=notes.at[note, pl.ds(0, 1)],
            dst_ref=slots.at[note, pl.ds(landing, 1)],
            send_sem=note_sems[note][0],
            recv_sem=note_sems[note][1],
            device_id=peer(target - me + total_devices),
            device_id_type=MESH,
        )

    def start_rest(low, high):
        for side in range(2):
            @pl.when(sides[side][0])
            def _(side=side):
                rest_copy(side, low, high).start()

    cut, tail = rows // 2 // SUB * SUB, 3 * rows // 8 // SUB * SUB
    start_rest(0, cut)

    for at, value in enumerate(sums):
        moments[at : at + 1, :] = jnp.sum(value, axis=0, keepdims=True)
    moments[len(sums) : SUB, :] = jnp.zeros((SUB - len(sums), cols), jnp.float32)
    folded = jnp.broadcast_to(jnp.sum(moments[...], axis=1, keepdims=True), (SUB, cols))
    notes[0, 0:1, :] = jnp.sum(jnp.where(lane == level, folded, 0.0), axis=0, keepdims=True)
    for turn in range(total_devices - 1):
        sum_copy(0, turn).start()

    start_rest(cut, rows - tail)

    def factors(near_side, far_side):
        return jnp.where(near_side, 2.0, 1.0), jnp.where(far_side, 0.0, 1.0)

    first_edge = [(prev_slot, *factors(has_prev, has_next))] * split
    first_edge += [(next_slot, *factors(has_next, has_prev))] * (count - split)
    other_slot = [next_slot] * split + [prev_slot] * (count - split)

    def closing(position, last_sum):
        start, first, last = walk(position)
        rows_here, padded = pl.ds(start, SUB), pl.ds(start + SUB, SUB)
        wait_cols(ITERS, position)
        wait_edges(ITERS, first, last)
        held, pushed, planes = [], [], []
        for p in range(count):
            here, plane = plane_sum(ITERS, p, start)
            plane = spatial[p] * plane
            planes.append(plane)
            held.append(here)
            pushed.append(plane + (temporal[p] * first_edge[p][2]) * here)
        last_sum = last_sum + dot(held, pushed)
        wait_years(ITERS, position)
        pushed = []
        for p in range(count):
            slot, twice, _ = first_edge[p]
            beside = temporal[p] * field[ITERS, slot, p, padded, :]
            resid[ITERS, p, rows_here, :] = planes[p] + beside
            pushed.append(twice * beside)
        return last_sum + dot(held, pushed)

    last_sum = lax.fori_loop(0, chunks, closing, zero)
    notes[1, 0:1, :] = jnp.sum(last_sum, axis=0, keepdims=True)
    for turn in range(total_devices - 1):
        sum_copy(1, turn).start()
    start_rest(rows - tail, rows)

    known = gather(slots, notes, 0, *note_sems[0], peer(1))
    known = jnp.where(lane == level, jnp.broadcast_to(known, (SUB, cols)), 0.0)
    known = jnp.broadcast_to(jnp.sum(known, axis=1, keepdims=True), (SUB, cols))
    mu = [known[at : at + 1, :] for at in range(2 * ITERS - 1)]
    drop = [mu[at] - mu[at + 1] for at in range(2 * ITERS - 2)]

    def form(coefs, table):
        total = None
        for i, left in enumerate(coefs):
            for j in range(i, len(coefs)):
                term = left * coefs[j] * table[i + j]
                term = term if i == j else 2.0 * term
                total = term if total is None else total + term
        return total

    one = jnp.ones_like(mu[0])
    search, direction = [one], [one]
    lengths = [jnp.zeros_like(one)] * ITERS
    inner = mu[0]
    for sweep in range(ITERS - 1):
        alpha = inner / form(direction, drop)
        for j in range(sweep + 1):
            lengths[j] = lengths[j] + alpha * direction[j]
        grown = []
        for j in range(sweep + 2):
            change = None
            if j <= sweep:
                change = direction[j]
            if j > 0:
                change = -direction[j - 1] if change is None else change - direction[j - 1]
            base = search[j] if j <= sweep else None
            grown.append(-alpha * change if base is None else base - alpha * change)
        search = grown
        fresh = form(search, mu)
        ratio = fresh / inner
        inner = fresh
        direction = [
            search[j] + ratio * direction[j] if j <= sweep else search[j]
            for j in range(sweep + 2)
        ]
    curve = form(direction, drop + [mu[-1]])
    bend = direction[-1] * direction[-1]

    def wide(values):
        return [jnp.broadcast_to(value, (SUB, cols)) for value in values]

    def mixes(values, head):
        return wide(
            [head - values[0]]
            + [values[j - 1] - values[j] for j in range(1, ITERS)]
            + [values[-1]]
        )

    paces, steers = wide(lengths[:-1]), wide(direction)
    base_mix, slope_mix = mixes(lengths, 1.0)[:-1], mixes(direction, 0.0)

    def prepare(position, carry):
        start, _, _ = walk(position)
        rows_here, padded = pl.ds(start, SUB), pl.ds(start + SUB, SUB)
        for p in range(count):
            vectors = [field[j + 1, 0, p, padded, :] for j in range(ITERS)]
            total = field[0, 0, p, padded, :]
            for pace, vector in zip(paces, vectors):
                total = total + pace * vector
            anchor[0, p, rows_here, :] = total
            total = steers[0] * vectors[0]
            for steer, vector in zip(steers[1:], vectors[1:]):
                total = total + steer * vector
            slope[0, p, rows_here, :] = total
            vectors = [resid[j, p, rows_here, :] for j in range(ITERS + 1)]
            vectors[-1] = vectors[-1] + temporal[p] * field[ITERS, other_slot[p], p, padded, :]
            total = base_mix[0] * vectors[0]
            for mix, vector in zip(base_mix[1:], vectors[1:]):
                total = total + mix * vector
            anchor[1, p, rows_here, :] = total
            total = slope_mix[0] * vectors[0]
            for mix, vector in zip(slope_mix[1:], vectors[1:]):
                total = total + mix * vector
            slope[1, p, rows_here, :] = total
        return carry

    wait_rest()
    lax.fori_loop(0, chunks, prepare, 0)

    for side in range(4):
        @pl.when(sides[side][0])
        def _(side=side):
            side_sends(side).wait_send()

    for at_last, present in ((False, has_first), (True, has_last)):
        @pl.when(present)
        def _(at_last=at_last):
            row_sends(at_last).wait_send()

    note_copies(slots, 0, *note_sems[0], peer(1)).wait_send()

    return inner, curve, bend


def note_copies(slots, note, send, recv, device):
    return pltpu.make_async_remote_copy(
        src_ref=slots.at[note],
        dst_ref=slots.at[note],
        send_sem=send,
        recv_sem=recv,
        device_id=device,
        device_id_type=MESH,
    )


def gather(slots, notes, note, send, recv, device):
    note_copies(slots, note, send, recv, device).wait_recv()
    return jnp.sum(slots[note], axis=0, keepdims=True) + notes[note, 0:1, :]


def kernel(sizes, *refs):
    *refs, last_send, last_recv = refs
    pace, notes, slots = refs[8], refs[-2], refs[-1]
    obs = refs[9]
    chunks = obs.shape[1] // SUB
    groups = chunks // PAIR
    dma = pltpu.SemaphoreType.DMA

    def scope(*sems):
        return solve(sizes, *refs, *sems, last_send, last_recv)

    inner, curve, bend = pl.run_scoped(
        scope,
        dma((4 + 2 * groups,)),
        dma((4,)),
        dma((2, chunks)),
        dma((2, groups)),
        dma(()),
        dma((2,)),
        dma((2, 2)),
        dma(()),
        dma(()),
        pltpu.SemaphoreType.REGULAR,
    )
    years, rows, cols = (lax.axis_index(axis) for axis in ("year", "row", "col"))
    device = (years, rows, lax.rem(cols + 1, sizes[2]))
    final = gather(slots, notes, 1, last_send, last_recv, device)
    final = jnp.broadcast_to(jnp.sum(final, axis=1, keepdims=True), final.shape)
    pace[...] = jnp.broadcast_to(inner / (curve - bend * final), pace.shape)
    note_copies(slots, 1, last_send, last_recv, device).wait_send()


def store_kernel(anchor, slope, pace, new_params, residual, total, sem):
    count = total.shape[1]
    step = jnp.broadcast_to(pace[0:1, :], total.shape[1:])
    half = (count + 1) // 2
    copies = []
    for at, out in enumerate((new_params, residual)):
        for piece, (low, high) in enumerate(((0, half), (half, count))):
            where = pl.ds(low, high - low)
            total[at, where] = anchor[at, where] + step[low:high] * slope[at, where]
            copies.append(
                pltpu.make_async_copy(
                    total.at[at, where], out.at[0, where], sem.at[at, piece]
                )
            )
            copies[-1].start()
    for copy in copies:
        copy.wait()


def per_device(sizes, observed, quality, land_mask, params, spatial_weight, temporal_weight):
    n_year, n_row, n_col = sizes
    _, dates, rows, cols = observed.shape
    count = params.shape[1]
    chunks = rows // SUB
    groups = chunks // PAIR
    others = n_year * n_row * n_col - 1
    f32 = jnp.float32
    vmem = pl.BlockSpec(memory_space=pltpu.VMEM)
    hbm = pl.BlockSpec(memory_space=pltpu.HBM)
    dma = pltpu.SemaphoreType.DMA
    both = jax.ShapeDtypeStruct((2, count, rows, cols), f32)
    results = pl.pallas_call(
        functools.partial(kernel, sizes),
        out_shape=(both, both, jax.ShapeDtypeStruct((SUB, cols), f32)),
        in_specs=[hbm] * 6,
        out_specs=(vmem, vmem, vmem),
        scratch_shapes=[
            pltpu.VMEM((dates, rows, cols), f32),
            pltpu.VMEM((dates, rows, cols), jnp.int32),
            pltpu.VMEM((rows, cols), jnp.int32),
            pltpu.SMEM((count,), f32),
            pltpu.SMEM((count,), f32),
            pltpu.VMEM((ROUNDS, 5, count, rows + 2 * SUB, cols), f32),
            pltpu.VMEM((count * (count + 1) // 2, rows, cols), f32),
            pltpu.VMEM((ROUNDS, count, rows, cols), f32),
            pltpu.VMEM((SUB, cols), f32),
            pltpu.VMEM((2, SUB, cols), f32),
            pltpu.VMEM((2, max(others, 1), cols), f32),
            dma(()),
            dma(()),
        ],
        compiler_params=pltpu.CompilerParams(
            collective_id=0, has_side_effects=True, vmem_limit_bytes=24 * 2**20
        ),
        name="gauss_newton",
    )(
        *[
            pltpu.with_memory_space_constraint(operand, pltpu.HBM)
            for operand in (
                observed, quality, land_mask, params, spatial_weight, temporal_weight
            )
        ]
    )
    return pl.pallas_call(
        store_kernel,
        out_shape=(
            jax.ShapeDtypeStruct(params.shape, f32),
            jax.ShapeDtypeStruct(params.shape, f32),
        ),
        in_specs=[vmem, vmem, vmem],
        out_specs=(hbm, hbm),
        scratch_shapes=[pltpu.VMEM((2, count, rows, cols), f32), dma((2, 2))],
        compiler_params=pltpu.CompilerParams(vmem_limit_bytes=4 * 2**20),
        name="store",
    )(*results)


def solution(mesh):
    sizes = tuple(mesh.shape[axis] for axis in ("year", "row", "col"))
    grid = P("year", None, "row", "col")
    return jax.shard_map(
        functools.partial(per_device, sizes),
        mesh=mesh,
        in_specs=(grid, grid, P("row", "col"), grid, P(), P()),
        out_specs=(grid, grid),
        check_vma=False,
    )
```
